256 devices in a mesh: dp: 8 (over y, core), tensor: 32 (over x, z).
Axes of the slice: x: 4, y: 4, z: 8, core: 2. Of those that a mesh axis runs over, the one named last changes fastest.
Arguments:
- hidden_sel: bfloat16 [8, 512, 2048], P('dp', 'tensor'), may hold values from -8 to 8
- picked: int32 [8, 512], P('dp'), may hold values from 0 to 12287, as said below
- order: int32 [8, 12], P('dp'), may hold values from 0 to 11, each once within a row
- lengths: int32 [8, 3], P('dp'), may hold values from 1 to 6, 12 in all within a row
- offsets: int32 [8, 3], P('dp'), may hold values from 0 to 4095
- cache_keys: bfloat16 [8, 12288, 2048], P('dp', 'tensor'), may hold values from -64 to 64
- cache_values: bfloat16 [8, 12288, 2048], P('dp', 'tensor'), may hold values from -6 to 6
- w_qkv: bfloat16 [3, 2048, 2048], P(None, 'dp', 'tensor'), may hold values from -0.088388348 to 0.088388348
- w_out: bfloat16 [2048, 2048], P('tensor', 'dp'), may hold values from -0.125 to 0.125
- w_gate_up: bfloat16 [2, 2048, 8192], P(None, 'dp', 'tensor'), may hold values from -0.125 to 0.125
- w_down: bfloat16 [8192, 2048], P('tensor', 'dp'), may hold values from -0.0625 to 0.0625
- gains: float32 [4, 2048], replicated, may hold values from 0.5 to 1.5
Outputs:
- layer_out: bfloat16 [8, 512, 2048], P('dp', 'tensor')
- fresh_keys: bfloat16 [8, 512, 2048], P('dp', 'tensor')
The draws below stay inside these ranges and needn't reach their ends.
Inputs may be any that keep to these rules, and one draw needn't show every extreme that they name: `picked`: distinct context rows in increasing order; the first and last rows of the context are always among them. `lengths`: they sum to 12.
All inputs are finite; a program needn't handle non-finite values.
Results may differ from the reference program's by a relative error of at most 0.04.
Values may be sent and summed in bfloat16 or wider, within the bound.
A program may use at most 64 MiB of HBM per device.

```python
import math
import jax
import jax.numpy as jnp
import numpy as np
from jax import lax

D = 2048
HEADS = 16
HEAD_DIM = 128
FF = 8192
CH = 1024
NCH = 12
REQS = 3
SEL = 512
CTX = 12288
GROUPS = 8
N_TENSOR = 32


def draw_picked(key, part):

    def one_group(group_key):
        inner = jax.random.permutation(group_key, CTX - 2)[:SEL - 2].astype(jnp.int32) + 1
        return jnp.concatenate([jnp.zeros((1,), jnp.int32), jnp.sort(inner).astype(jnp.int32), jnp.full((1,), CTX - 1, jnp.int32)])
    group_keys = jax.random.split(jax.random.fold_in(key, 7), GROUPS)
    return jax.vmap(one_group)(group_keys)


def projection_block(key):
    return jax.random.truncated_normal(jax.random.fold_in(key, 101), -4.0, 4.0, (3, D, D), jnp.float32) * D ** (-0.5)


def aligned_features(key):
    quarter = max(2, HEAD_DIM // 16)
    chosen_head = jax.random.randint(jax.random.fold_in(key, 103), (), 0, HEADS).astype(jnp.int32)
    within = jnp.concatenate([jnp.arange(HEAD_DIM // 2 - quarter, HEAD_DIM // 2, dtype=jnp.int32), jnp.arange(HEAD_DIM - quarter, HEAD_DIM, dtype=jnp.int32)])
    features = chosen_head * HEAD_DIM + within
    sign_pattern = jnp.where(jax.random.bernoulli(jax.random.fold_in(key, 104), 0.5, (2 * quarter,)), 1.0, -1.0).astype(jnp.float32)
    return (features, sign_pattern)


def draw_w_qkv(key, part):
    return projection_block(key).astype(jnp.bfloat16)


def draw_hidden_sel(key, part):
    noise_rows = jax.random.truncated_normal(jax.random.fold_in(key, 105), -6.0, 6.0, (GROUPS, SEL, D), jnp.float32)
    weights_query = projection_block(key)[0]
    features, sign_pattern = aligned_features(key)
    picked_columns = jnp.take(weights_query, features, axis=1)
    direction = picked_columns[:, 0] * sign_pattern[0]
    for column in range(1, sign_pattern.shape[0]):
        direction = direction + picked_columns[:, column] * sign_pattern[column]
    aligned_rows = jax.random.bernoulli(jax.random.fold_in(key, 116), 0.1, (GROUPS, SEL))
    strength = jax.random.uniform(jax.random.fold_in(key, 117), (GROUPS, SEL), jnp.float32, 10.0, 18.0)
    lift_rows = jnp.where(aligned_rows, strength, 0.0)
    noise_rows = jnp.clip(noise_rows + lift_rows[:, :, None] * direction[None, None, :], -8.0, 8.0)
    return noise_rows.astype(jnp.bfloat16)


def draw_cache_keys(key, part):
    base_keys = jax.random.truncated_normal(jax.random.fold_in(key, 108), -6.0, 6.0, (GROUPS, CTX, D), jnp.float32)
    features, sign_pattern = aligned_features(key)
    band_rows = jax.random.bernoulli(jax.random.fold_in(key, 119), 0.05, (GROUPS, CTX))
    strength = jax.random.uniform(jax.random.fold_in(key, 120), (GROUPS, CTX), jnp.float32, 30.0, 55.0)
    current = base_keys[:, :, features]
    lifted = jnp.where(band_rows[:, :, None], strength[:, :, None] * sign_pattern[None, None, :], current)
    base_keys = base_keys.at[:, :, features].set(lifted)
    return base_keys.astype(jnp.bfloat16)


def with_ends(values, rng, smallest, largest):
    longest = values.shape.index(max(values.shape))
    spots = []
    for shift in (0, 1):
        where = [jax.random.randint(jax.random.fold_in(rng, axis), (), 0, length) for axis, length in enumerate(values.shape)]
        where[longest] = (where[longest] + shift) % values.shape[longest]
        spots.append(tuple(where))
    return values.at[spots[0]].set(smallest).at[spots[1]].set(largest)


def shard_levels(rng, extent, shards, least, high):
    level = 1.0
    for axis_at, shards_of in shards:
        heights = jax.random.uniform(jax.random.fold_in(jax.random.fold_in(rng, 6), axis_at), (shards_of,), jnp.float32, least / len(shards), high / len(shards))
        level = level * jnp.repeat(jnp.exp(heights), extent[axis_at] // shards_of).reshape((-1,) + (1,) * (len(extent) - 1 - axis_at))
    return level


def split_up(number_of, total, reach, slope):
    loads = [(1 << 20) // math.isqrt(rank ** slope) + 1 for rank in range(2, number_of + 1)]
    surplus, counts = total - reach - (number_of - 1), [1] * (number_of - 1)
    while surplus > 0:
        movable = [i for i in range(number_of - 1) if counts[i] < reach]
        whole, remaining = sum([loads[i] for i in movable]), surplus
        for i in movable:
            extra = min(reach - counts[i], max(1, remaining * loads[i] // whole), surplus)
            counts[i] = counts[i] + extra
            surplus = surplus - extra
    return np.array([reach] + counts)


def uneven(stream_key, number_of, total, reach, skew):
    if number_of == 2:
        one = jax.random.randint(stream_key, (), max(1, total - reach), min(reach, total - 1) + 1)
        return jnp.stack([one, total - one])
    sizes = jnp.asarray(split_up(number_of, total, reach, skew), jnp.int32)
    couples = (number_of - 1) // 2
    donor, receiver = sizes[1:1 + 2 * couples:2], sizes[2:2 + 2 * couples:2]
    slack = jnp.minimum(donor - 1, reach - receiver)
    passed = jax.random.randint(jax.random.fold_in(stream_key, 1), (couples,), 0, 1 << 20) % (slack + 1)
    sizes = sizes.at[1:1 + 2 * couples:2].set(donor - passed).at[2:2 + 2 * couples:2].set(receiver + passed)
    return sizes[jax.random.permutation(jax.random.fold_in(stream_key, 2), number_of)]


def normal_values(rng, dims, deviation, most, cuts=(), kind=jnp.bfloat16):
    entries = deviation * jax.random.normal(rng, dims, jnp.float32)
    if cuts:
        entries = entries * shard_levels(rng, dims, cuts, -0.22, 0.18)
    return jnp.clip(entries, -most, most).astype(kind)


def setup_inputs(seed: int = 0) -> dict:
    streams_of = jax.random.split(jax.random.key(seed), 13)
    return {
        "hidden_sel": draw_hidden_sel(jax.random.fold_in(streams_of[12], 71), 0),
        "picked": draw_picked(jax.random.fold_in(streams_of[12], 71), 0),
        "order": jax.vmap(lambda own: jax.random.permutation(own, NCH))(jax.random.split(streams_of[2], GROUPS)).reshape((GROUPS, NCH)).astype(jnp.int32),
        "lengths": jax.vmap(lambda own: uneven(own, REQS, NCH, NCH // 2, 2))(jax.random.split(streams_of[3], GROUPS)).reshape((GROUPS, REQS)).astype(jnp.int32),
        "offsets": with_ends(jax.random.randint(streams_of[4], (GROUPS, REQS), 0, 4096), jax.random.fold_in(streams_of[4], 1), 0, 4095).astype(jnp.int32),
        "cache_keys": draw_cache_keys(jax.random.fold_in(streams_of[12], 71), 0),
        "cache_values": normal_values(streams_of[6], (GROUPS, CTX, D), 1.0, 6.0, ((0, 8), (1, 32))),
        "w_qkv": draw_w_qkv(jax.random.fold_in(streams_of[12], 71), 0),
        "w_out": normal_values(streams_of[8], (D, D), D ** -0.5, 0.125, ((0, 32), (1, 8))),
        "w_gate_up": normal_values(streams_of[9], (2, D, FF), D ** -0.5, 0.125, ((1, 8), (2, 32))),
        "w_down": normal_values(streams_of[10], (FF, D), FF ** -0.5, 0.0625, ((0, 32), (1, 8))),
        "gains": jnp.clip(1.0 + 0.1 * jax.random.normal(streams_of[11], (4, D), jnp.float32), 0.5, 1.5),
    }


THETA = 500000.0
EPSILON = 1e-06
NEGATIVE = -1e+30

def token_meta(rows, order_row, length_row, offset_row):
    slot_index = rows // CH
    in_span = rows % CH
    ordinal = lax.optimization_barrier(jnp.sum(jnp.where(slot_index[:, None] == jnp.arange(NCH, dtype=jnp.int32)[None, :], order_row[None, :], 0), axis=1))
    request_end = jnp.cumsum(length_row).astype(jnp.int32)
    request = lax.optimization_barrier(jnp.sum((ordinal[:, None] >= request_end[None, :]).astype(jnp.int32), axis=1))
    request_pick = request[:, None] == jnp.arange(REQS, dtype=jnp.int32)[None, :]
    request_start = lax.optimization_barrier(jnp.sum(jnp.where(request_pick, (request_end - length_row)[None, :], 0), axis=1))
    request_shift = lax.optimization_barrier(jnp.sum(jnp.where(request_pick, offset_row[None, :], 0), axis=1))
    position = request_shift + (ordinal - request_start) * CH + in_span
    return (request, position, in_span)

def frequencies(index_float):
    return jnp.exp(index_float * (-2.0 * math.log(THETA) / HEAD_DIM))

def rope_full(values_in, position):
    row_count = values_in.shape[0]
    half_dim = HEAD_DIM // 2
    split = values_in.reshape(row_count, -1, HEAD_DIM)
    angles = position.astype(jnp.float32)[:, None] * frequencies(jnp.arange(half_dim, dtype=jnp.int32).astype(jnp.float32))[None, :]
    cosine = jnp.cos(angles)[:, None, :]
    sine = jnp.sin(angles)[:, None, :]
    first = split[..., :half_dim]
    second = split[..., half_dim:]
    turned = jnp.concatenate([first * cosine - second * sine, second * cosine + first * sine], axis=-1)
    return turned.reshape(row_count, -1)

def rms_scale(values_in, gain):
    return values_in * lax.rsqrt(lax.optimization_barrier(jnp.mean(values_in * values_in, axis=-1, keepdims=True)) + EPSILON) * gain

def blocked_product(left, right, blocks):
    row_count, inner = left.shape
    left_blocks = left.reshape(row_count, blocks, inner // blocks).transpose(1, 0, 2)
    right_blocks = right.reshape(blocks, inner // blocks, right.shape[1])

    def step(totals, pair):
        part = jnp.dot(pair[0], pair[1], preferred_element_type=jnp.float32)
        part = lax.optimization_barrier(part.astype(jnp.bfloat16)).astype(jnp.float32)
        return (totals + part, None)
    start = jnp.zeros((row_count, right.shape[1]), jnp.float32)
    totals, _ = lax.scan(step, start, (left_blocks, right_blocks))
    return totals

def one_group(hidden, picked_row, order_row, length_row, offset_row, keys_cached, values_cached, w_qkv, w_out, w_gate_up, w_down, gains):
    context_rows = jnp.arange(CTX, dtype=jnp.int32)
    key_request, key_position, key_local = token_meta(context_rows, order_row, length_row, offset_row)
    query_request, query_position, _ = token_meta(picked_row, order_row, length_row, offset_row)
    chosen = jnp.zeros((CTX,), jnp.int32).at[picked_row].set(1)
    projected = jnp.einsum('nd,kdc->knc', hidden.astype(jnp.float32), w_qkv.astype(jnp.float32))
    query = rope_full(rms_scale(projected[0], gains[0]), query_position).astype(jnp.bfloat16)
    fresh_keys = rope_full(rms_scale(projected[1], gains[1]), query_position).astype(jnp.bfloat16)
    fresh_values = projected[2].astype(jnp.bfloat16)
    turned = rope_full(keys_cached.astype(jnp.float32), key_position - key_local).astype(jnp.bfloat16)
    usable_cached = (query_request[:, None] == key_request[None, :]) & (key_position[None, :] <= query_position[:, None]) & (chosen[None, :] == 0)
    usable_fresh = (query_request[:, None] == query_request[None, :]) & (query_position[None, :] <= query_position[:, None])
    usable_c = usable_cached.reshape(SEL, N_TENSOR, -1)
    usable_f = usable_fresh.reshape(SEL, N_TENSOR, -1)

    def per_head(operands):
        query_h, key_c, value_c, key_f, value_f = operands
        scores_c = jnp.dot(query_h, key_c.T, preferred_element_type=jnp.float32) * HEAD_DIM ** (-0.5)
        scores_f = jnp.dot(query_h, key_f.T, preferred_element_type=jnp.float32) * HEAD_DIM ** (-0.5)
        masked_c = jnp.where(usable_cached, scores_c, NEGATIVE).reshape(SEL, N_TENSOR, -1)
        masked_f = jnp.where(usable_fresh, scores_f, NEGATIVE).reshape(SEL, N_TENSOR, -1)
        block_max = jnp.maximum(lax.optimization_barrier(jnp.max(masked_c, axis=2)), lax.optimization_barrier(jnp.max(masked_f, axis=2)))
        expo_c = jnp.where(usable_c, jnp.exp(masked_c - block_max[:, :, None]), 0.0)
        expo_f = jnp.where(usable_f, jnp.exp(masked_f - block_max[:, :, None]), 0.0)
        totals = lax.optimization_barrier(jnp.sum(expo_c, axis=2)) + lax.optimization_barrier(jnp.sum(expo_f, axis=2))
        weight_c = lax.optimization_barrier(expo_c.astype(jnp.bfloat16)).astype(jnp.float32)
        weight_f = lax.optimization_barrier(expo_f.astype(jnp.bfloat16)).astype(jnp.float32)
        mixed = jnp.einsum('qtk,tkd->qtd', weight_c, value_c.reshape(N_TENSOR, -1, HEAD_DIM).astype(jnp.float32))
        mixed = mixed + jnp.einsum('qtk,tkd->qtd', weight_f, value_f.reshape(N_TENSOR, -1, HEAD_DIM).astype(jnp.float32))
        overall = lax.optimization_barrier(jnp.max(block_max, axis=1))
        factor = jnp.exp(block_max - overall[:, None])
        parts = lax.optimization_barrier((mixed * factor[:, :, None]).astype(jnp.bfloat16)).astype(jnp.float32)
        return lax.optimization_barrier(jnp.sum(parts, axis=1)) / lax.optimization_barrier(jnp.sum(totals * factor, axis=1))[:, None]

    def by_head(array_in):
        return array_in.reshape(array_in.shape[0], HEADS, HEAD_DIM).transpose(1, 0, 2)
    heads_out = lax.map(per_head, (by_head(query), by_head(turned), by_head(values_cached), by_head(fresh_keys), by_head(fresh_values)))
    attn = heads_out.transpose(1, 0, 2).reshape(SEL, D).astype(jnp.bfloat16)
    y_out = blocked_product(attn, w_out, N_TENSOR)
    hidden_next = (hidden.astype(jnp.float32) + rms_scale(y_out, gains[2])).astype(jnp.bfloat16)
    gate_part = jnp.dot(hidden_next, w_gate_up[0], preferred_element_type=jnp.float32)
    up_part = jnp.dot(hidden_next, w_gate_up[1], preferred_element_type=jnp.float32)
    activated = (jax.nn.silu(gate_part) * up_part).astype(jnp.bfloat16)
    z_out = blocked_product(activated, w_down, N_TENSOR)
    layer_out = (hidden_next.astype(jnp.float32) + rms_scale(z_out, gains[3])).astype(jnp.bfloat16)
    return (layer_out, fresh_keys)

def reference(hidden_sel, picked, order, lengths, offsets, cache_keys, cache_values, w_qkv, w_out, w_gate_up, w_down, gains):
    outputs = []
    keys_out = []
    for group in range(GROUPS):
        layer_out, fresh_keys = one_group(hidden_sel[group], picked[group], order[group], lengths[group], offsets[group], cache_keys[group], cache_values[group], w_qkv, w_out, w_gate_up, w_down, gains)
        outputs.append(layer_out)
        keys_out.append(fresh_keys)
    return (jnp.stack(outputs), jnp.stack(keys_out))
```

```python
import math

import jax
import jax.numpy as jnp
from jax import lax
from jax.sharding import PartitionSpec as P

HEAD_DIM = 128
CH = 1024
NCH = 12
REQS = 3
NX = 4
NZ = 8

THETA = 500000.0
EPSILON = 1e-06
NEGATIVE = -1e30

ZG = [[x * NZ + z for z in range(NZ)] for x in range(NX)]
XG = [[x * NZ + z for x in range(NX)] for z in range(NZ)]


def token_meta(rows, order_row, length_row, offset_row):
    slot_index = rows // CH
    in_span = rows % CH
    ordinal = jnp.sum(
        jnp.where(
            slot_index[:, None] == jnp.arange(NCH, dtype=jnp.int32)[None, :], order_row[None, :], 0
        ),
        axis=1,
    )
    request_end = jnp.cumsum(length_row)
    request = jnp.sum((ordinal[:, None] >= request_end[None, :]).astype(jnp.int32), axis=1)
    request_pick = request[:, None] == jnp.arange(REQS, dtype=jnp.int32)[None, :]
    request_start = jnp.sum(jnp.where(request_pick, (request_end - length_row)[None, :], 0), axis=1)
    request_shift = jnp.sum(jnp.where(request_pick, offset_row[None, :], 0), axis=1)
    position = request_shift + (ordinal - request_start) * CH + in_span
    return (request, position, in_span)


def frequencies(index_float):
    return jnp.exp(index_float * (-2.0 * math.log(THETA) / HEAD_DIM))


def rope_full(values_in, position):
    row_count = values_in.shape[0]
    half_dim = HEAD_DIM // 2
    split = values_in.reshape(row_count, -1, HEAD_DIM)
    angles = (
        position.astype(jnp.float32)[:, None]
        * frequencies(jnp.arange(half_dim, dtype=jnp.int32).astype(jnp.float32))[None, :]
    )
    cosine = jnp.cos(angles)[:, None, :]
    sine = jnp.sin(angles)[:, None, :]
    first = split[..., :half_dim]
    second = split[..., half_dim:]
    turned = jnp.concatenate(
        [first * cosine - second * sine, second * cosine + first * sine], axis=-1
    )
    return turned.reshape(row_count, -1)


def rms_scale(values_in, gain):
    return (
        values_in
        * lax.rsqrt(jnp.mean(values_in * values_in, axis=-1, keepdims=True) + EPSILON)
        * gain
    )


def swap(blocks, groups):
    return lax.all_to_all(
        blocks, "tensor", split_axis=0, concat_axis=0, axis_index_groups=groups, tiled=True
    )


def share(block, groups):
    count = len(groups[0])
    return swap(jnp.broadcast_to(block[None], (count,) + block.shape), groups)


def shards(
    hidden_sel,
    picked,
    order,
    lengths,
    offsets,
    cache_keys,
    cache_values,
    w_qkv,
    w_out,
    w_gate_up,
    w_down,
    gains,
):
    f32, bf16 = jnp.float32, jnp.bfloat16
    hidden = hidden_sel[0]
    meta = (order[0], lengths[0], offsets[0])
    picked_row = picked[0]
    lane = lax.axis_index("tensor")
    at_x, at_z = lane // NZ, lane % NZ
    own, width = hidden.shape
    sel = own * NX * NZ
    ctx = cache_keys.shape[1]
    part = width // NX
    heads = part // HEAD_DIM
    qkv_full = lax.all_gather(w_qkv, "dp", axis=1, tiled=True)
    out_full = lax.all_gather(w_out, "dp", axis=1, tiled=True)
    gate_full = lax.all_gather(w_gate_up, "dp", axis=1, tiled=True)
    down_full = lax.all_gather(w_down, "dp", axis=1, tiled=True)
    out_rows = share(out_full, ZG).reshape(part, width)
    cache = jnp.concatenate([cache_keys[0], cache_values[0]], axis=0)
    cache = swap(cache.reshape(2 * ctx, NX, part).transpose(1, 0, 2), XG)
    raw_keys = cache[:, :ctx].reshape(NX * ctx, part)
    values_c = cache[:, ctx:].reshape(NX * ctx, part)
    rows = (
        (jnp.arange(NX, dtype=jnp.int32)[:, None] * NZ + at_z) * ctx
        + jnp.arange(ctx, dtype=jnp.int32)[None, :]
    ).reshape(-1)
    c_req, c_pos, c_local = token_meta(rows, *meta)
    chosen = jnp.any(picked_row[:, None] == rows[None, :], axis=0)
    keys_c = rope_full(raw_keys.astype(f32), c_pos - c_local).astype(bf16)
    x_rows = share(hidden, ZG).reshape(NZ * own, width)
    all_rows = share(x_rows, XG).reshape(sel, width)
    proj = jnp.einsum("nd,kdc->knc", all_rows, qkv_full, preferred_element_type=f32).astype(bf16)
    cols = proj.shape[2]
    q_req, q_pos, _ = token_meta(picked_row, *meta)

    def by_z(rows_in):
        return rows_in.reshape(NX, NZ, own, -1).transpose(1, 0, 2, 3).reshape(NZ, NX * own, -1)

    def of_z(vector):
        return lax.dynamic_index_in_dim(
            vector.reshape(NX, NZ, own).transpose(1, 0, 2).reshape(NZ, NX * own),
            at_z, 0, keepdims=False,
        )

    f_req, f_pos = of_z(q_req), of_z(q_pos)
    payload = jnp.concatenate(
        [jnp.broadcast_to(proj[0][None], (NZ, sel, cols)), by_z(proj[1]), by_z(proj[2])], axis=1
    )
    got = swap(payload, ZG).transpose(1, 0, 2).reshape(-1, part).astype(f32)
    squares = jnp.sum(got[: sel + NX * own] ** 2, axis=1)
    squares = jnp.sum(share(squares, XG), axis=0)
    scale = lax.rsqrt(squares / width + EPSILON)[:, None]
    gain_x = lax.dynamic_slice_in_dim(gains, at_x * part, part, axis=1)
    query = rope_full(got[:sel] * scale[:sel] * gain_x[0], q_pos).astype(bf16)
    key_f = rope_full(got[sel : sel + NX * own] * scale[sel:] * gain_x[1], f_pos).astype(bf16)
    value_f = got[sel + NX * own :].astype(bf16)
    fresh_out = swap(key_f.reshape(NX, own, part), XG).transpose(1, 0, 2).reshape(own, width)
    all_keys = jnp.concatenate([keys_c, key_f], axis=0).reshape(-1, heads, HEAD_DIM)
    all_values = jnp.concatenate([values_c, value_f], axis=0).reshape(-1, heads, HEAD_DIM)
    k_req = jnp.concatenate([c_req, f_req])
    k_pos = jnp.concatenate([c_pos, f_pos])
    live = jnp.concatenate([jnp.logical_not(chosen), jnp.ones((NX * own,), bool)])
    scores = jnp.einsum(
        "qhd,khd->hqk", query.reshape(sel, heads, HEAD_DIM), all_keys, preferred_element_type=f32
    ) * HEAD_DIM ** (-0.5)
    usable = (
        (q_req[:, None] == k_req[None, :]) & (k_pos[None, :] <= q_pos[:, None]) & live[None, :]
    )
    masked = jnp.where(usable[None], scores, NEGATIVE)
    top = jnp.max(masked, axis=2)
    weights = jnp.where(usable[None], jnp.exp(masked - top[:, :, None]), 0.0)
    total = jnp.sum(weights, axis=2)
    mixed = jnp.einsum(
        "hqk,khd->qhd", weights.astype(bf16), all_values, preferred_element_type=f32
    ).reshape(sel, part)
    mixed = swap(by_z(mixed.astype(bf16)), ZG).astype(f32).reshape(NZ, NX * own, heads, HEAD_DIM)
    stats = swap(by_z(jnp.concatenate([top, total], axis=0).T), ZG)
    top, total = stats[..., :heads], stats[..., heads:]
    factor = jnp.exp(top - jnp.max(top, axis=0))
    attn = jnp.sum(mixed * factor[..., None], axis=0) / jnp.sum(total * factor, axis=0)[..., None]
    attn = attn.reshape(NX * own, part).astype(bf16)
    y_part = jnp.dot(attn, out_rows, preferred_element_type=f32).astype(bf16)
    y = jnp.sum(swap(y_part.reshape(NX, own, width), XG).astype(f32), axis=0)
    hidden_next = (hidden.astype(f32) + rms_scale(y, gains[2])).astype(bf16)
    x_rows = share(hidden_next, ZG).reshape(NZ * own, width)
    all_next = share(x_rows, XG).reshape(sel, width)
    gate_part = jnp.dot(all_next, gate_full[0], preferred_element_type=f32)
    up_part = jnp.dot(all_next, gate_full[1], preferred_element_type=f32)
    activated = (jax.nn.silu(gate_part) * up_part).astype(bf16)
    down = jnp.dot(activated, down_full, preferred_element_type=f32).astype(bf16)
    down = jnp.sum(swap(down.reshape(NX, NZ * own, width), XG).astype(f32), axis=0).astype(bf16)
    down = jnp.sum(swap(down.reshape(NZ, own, width), ZG).astype(f32), axis=0)
    result = (hidden_next.astype(f32) + rms_scale(down, gains[3])).astype(bf16)
    return (result[None], fresh_out[None])


def solution(mesh):
    placed = (
        P("dp", "tensor", None),
        P("dp", None),
        P("dp", None),
        P("dp", None),
        P("dp", None),
        P("dp", "tensor", None),
        P("dp", "tensor", None),
        P(None, "dp", "tensor"),
        P("tensor", "dp"),
        P(None, "dp", "tensor"),
        P("tensor", "dp"),
        P(),
    )
    return jax.shard_map(
        shards,
        mesh=mesh,
        in_specs=placed,
        out_specs=(P("dp", "tensor", None), P("dp", "tensor", None)),
        check_vma=False,
    )
```

```python
import math

import jax
import jax.numpy as jnp
from jax import lax
from jax.experimental import pallas as pl
from jax.experimental.pallas import tpu as pltpu
from jax.sharding import PartitionSpec as P

HEAD_DIM = 128
CH = 1024
NCH = 12
REQS = 3
NX = 4
NZ = 8
NDP = 8
NY = 4
D = 2048
PART = D // NX
HEADS = PART // HEAD_DIM
OWN = 16
GRP = NX * OWN
SEL = NZ * GRP
CTX = 384
CACHED = NX * CTX
KEYS = CACHED + 128
SPAN = 1 << 14
DEAD = 1 << 30

THETA = 500000.0
EPSILON = 1e-06
NEGATIVE = -1e30
FLOOR = -1e20
SCORE = HEAD_DIM ** (-0.5) * math.log2(math.e)
MESH = pl.DeviceIdType.MESH
F32, BF16 = jnp.float32, jnp.bfloat16
HIGH = lax.Precision.HIGHEST


def lanes(rows):
    return lax.broadcasted_iota(jnp.int32, (rows, HEAD_DIM), 1)


def kernel(
    hidden,
    keys,
    values,
    w4,
    wo,
    wm,
    gains,
    qmeta,
    fcode,
    qcos,
    qsin,
    scos,
    ssin,
    sbase,
    out,
    fresh,
    hid,
    w4buf,
    wobuf,
    wbuf,
    kraw,
    kall,
    vall,
    kcode,
    qpk,
    kvs,
    qrecv,
    kvrecv,
    sq,
    stat,
    qh,
    kf,
    frecv,
    obuf,
    obst,
    orecv,
    strecv,
    ysend,
    yrecv,
    hn,
    hbuf,
    act,
    dsend,
    drecv,
    hz_s,
    hz_r,
    hx_s,
    hx_r,
    w4_s,
    w4_r,
    oz_s,
    oz_r,
    oy_s,
    oy_r,
    os_s,
    os_r,
    wx_s,
    wx_r,
    wy_s,
    wy_r,
    ws_s,
    ws_r,
    k_s,
    k_r,
    v_s,
    v_r,
    q_s,
    q_r,
    c_s,
    c_r,
    st_s,
    st_r,
    f_s,
    f_r,
    o_s,
    o_r,
    t_s,
    t_r,
    y_s,
    y_r,
    n_s,
    n_r,
    d_s,
    d_r,
    loc,
):
    tens = lax.axis_index("tensor")
    dp = lax.axis_index("dp")
    x = lax.div(tens, NZ)
    z = lax.rem(tens, NZ)
    core = lax.rem(dp, 2)
    sib = dp + 1 - 2 * core

    def xa(k):
        return lax.rem(x + k, NX)

    def za(k):
        return lax.rem(z + k, NZ)

    def ya(k):
        return lax.rem(dp + 2 * k, NDP)

    def da(k):
        return lax.rem(dp + k, NDP)

    def zdev(k):
        return {"tensor": x * NZ + za(k)}

    def xdev(k):
        return {"tensor": xa(k) * NZ + z}

    def send(src, dst, ssem, rsem, dev):
        return pltpu.make_async_remote_copy(
            src_ref=src, dst_ref=dst, send_sem=ssem, recv_sem=rsem, device_id=dev,
            device_id_type=MESH,
        )

    def each(first, last, body):
        def step(k, carry):
            body(k)
            return carry

        lax.fori_loop(first, last, step, 0)

    def hz(k):
        return send(hidden, hid.at[z * NX + x], hz_s.at[k], hz_r.at[k], zdev(k))

    def hz_in(k):
        at = hid.at[za(NZ - k) * NX + x]
        return send(at, at, hz_s.at[k], hz_r.at[k], zdev(k))

    def hx(k, j):
        at = hid.at[za(NZ - k) * NX + x]
        return send(at, at, hx_s.at[k, j], hx_r.at[k, j], xdev(j))

    def hx_in(k, j):
        at = hid.at[za(NZ - k) * NX + xa(NX - j)]
        return send(at, at, hx_s.at[k, j], hx_r.at[k, j], xdev(j))

    def w4c(k):
        return send(w4, w4buf.at[dp], w4_s.at[k], w4_r.at[k], {"dp": da(k)})

    def w4_in(k):
        at = w4buf.at[da(NDP - k)]
        return send(at, at, w4_s.at[k], w4_r.at[k], {"dp": da(k)})

    def oz(k):
        return send(wo, wobuf.at[dp, z], oz_s.at[k], oz_r.at[k], zdev(k))

    def oz_in(k):
        at = wobuf.at[dp, za(NZ - k)]
        return send(at, at, oz_s.at[k], oz_r.at[k], zdev(k))

    def oy(k):
        at = wobuf.at[dp]
        return send(at, at, oy_s.at[k], oy_r.at[k], {"dp": ya(k)})

    def oy_in(k):
        at = wobuf.at[ya(NY - k)]
        return send(at, at, oy_s.at[k], oy_r.at[k], {"dp": ya(k)})

    def osib(k):
        at = wobuf.at[ya(NY - k)]
        return send(at, at, os_s.at[k], os_r.at[k], {"dp": sib})

    def osib_in(k):
        at = wobuf.at[lax.rem(sib + 2 * (NY - k), NDP)]
        return send(at, at, os_s.at[k], os_r.at[k], {"dp": sib})

    def wx(k):
        return send(wm, wbuf.at[dp, x], wx_s.at[k], wx_r.at[k], xdev(k))

    def wx_in(k):
        at = wbuf.at[dp, xa(NX - k)]
        return send(at, at, wx_s.at[k], wx_r.at[k], xdev(k))

    def wy(k, j):
        at = wbuf.at[dp, xa(NX - k)]
        return send(at, at, wy_s.at[k, j], wy_r.at[k, j], {"dp": ya(j)})

    def wy_in(k, j):
        at = wbuf.at[ya(NY - j), xa(NX - k)]
        return send(at, at, wy_s.at[k, j], wy_r.at[k, j], {"dp": ya(j)})

    def ws(k, j):
        at = wbuf.at[ya(NY - j), xa(NX - k)]
        return send(at, at, ws_s.at[k, j], ws_r.at[k, j], {"dp": sib})

    def ws_in(k, j):
        at = wbuf.at[lax.rem(sib + 2 * (NY - j), NDP), xa(NX - k)]
        return send(at, at, ws_s.at[k, j], ws_r.at[k, j], {"dp": sib})

    def columns(at):
        return pl.ds(pl.multiple_of(at * PART, PART), PART)

    def key_rows(at):
        return pl.ds(pl.multiple_of(at * CTX, 128), CTX)

    def kx(k):
        return send(keys.at[:, columns(xa(k))], kraw.at[x], k_s.at[k], k_r.at[k], xdev(k))

    def kx_in(k):
        at = kraw.at[xa(NX - k)]
        return send(at, at, k_s.at[k], k_r.at[k], xdev(k))

    def vx(k):
        return send(
            values.at[:, columns(xa(k))], vall.at[key_rows(x)], v_s.at[k], v_r.at[k], xdev(k)
        )

    def vx_in(k):
        at = vall.at[key_rows(xa(NX - k))]
        return send(at, at, v_s.at[k], v_r.at[k], xdev(k))

    def qz(k):
        return send(qpk, qrecv.at[z], q_s.at[k], q_r.at[k], zdev(k))

    def qz_in(k):
        at = qrecv.at[za(NZ - k)]
        return send(at, at, q_s.at[k], q_r.at[k], zdev(k))

    def cz(k):
        return send(kvs.at[za(k)], kvrecv.at[z], c_s.at[k], c_r.at[k], zdev(k))

    def cz_in(k):
        at = kvrecv.at[za(NZ - k)]
        return send(at, at, c_s.at[k], c_r.at[k], zdev(k))

    def stx(k):
        return send(stat.at[x], stat.at[x], st_s.at[k], st_r.at[k], xdev(k))

    def stx_in(k):
        at = stat.at[xa(NX - k)]
        return send(at, at, st_s.at[k], st_r.at[k], xdev(k))

    def fx(k):
        return send(kf.at[xa(k)], frecv.at[x], f_s.at[k], f_r.at[k], xdev(k))

    def fx_in(k):
        at = frecv.at[xa(NX - k)]
        return send(at, at, f_s.at[k], f_r.at[k], xdev(k))

    def oex(k):
        return send(obuf.at[za(k)], orecv.at[z], o_s.at[k], o_r.at[k], zdev(k))

    def oex_in(k):
        at = orecv.at[za(NZ - k)]
        return send(at, at, o_s.at[k], o_r.at[k], zdev(k))

    def tex(k):
        return send(obst.at[za(k)], strecv.at[z], t_s.at[k], t_r.at[k], zdev(k))

    def tex_in(k):
        at = strecv.at[za(NZ - k)]
        return send(at, at, t_s.at[k], t_r.at[k], zdev(k))

    def yx(k):
        return send(ysend.at[xa(k)], yrecv.at[x], y_s.at[k], y_r.at[k], xdev(k))

    def yx_in(k):
        at = yrecv.at[xa(NX - k)]
        return send(at, at, y_s.at[k], y_r.at[k], xdev(k))

    def nz(k):
        return send(hn, hbuf.at[z], n_s.at[k], n_r.at[k], zdev(k))

    def nz_in(k):
        at = hbuf.at[za(NZ - k)]
        return send(at, at, n_s.at[k], n_r.at[k], zdev(k))

    def dz(k):
        return send(dsend.at[za(k)], drecv.at[z], d_s.at[k], d_r.at[k], zdev(k))

    def dz_in(k):
        at = drecv.at[za(NZ - k)]
        return send(at, at, d_s.at[k], d_r.at[k], zdev(k))

    own_copies = [
        pltpu.make_async_copy(hidden, hid.at[z * NX + x], loc.at[0]),
        pltpu.make_async_copy(w4, w4buf.at[dp], loc.at[1]),
        pltpu.make_async_copy(wo, wobuf.at[dp, z], loc.at[2]),
        pltpu.make_async_copy(wm, wbuf.at[dp, x], loc.at[3]),
        pltpu.make_async_copy(keys.at[:, columns(x)], kraw.at[x], loc.at[4]),
        pltpu.make_async_copy(values.at[:, columns(x)], vall.at[key_rows(x)], loc.at[5]),
    ]
    for copy in own_copies:
        copy.start()

    barrier = pltpu.get_barrier_semaphore()

    def greet(dev):
        pl.semaphore_signal(barrier, inc=1, device_id=dev, device_id_type=MESH)

    each(1, NZ, lambda k: greet(zdev(k)))
    each(1, NX, lambda k: greet(xdev(k)))
    each(1, NDP, lambda k: greet({"dp": da(k)}))
    pl.semaphore_wait(barrier, NZ + NX + NDP - 3)

    own_copies[0].wait()
    each(1, NZ, lambda k: hz(k).start())
    each(1, NX, lambda j: hx(0, j).start())
    each(1, NDP, lambda k: w4c(k).start())
    each(1, NX, lambda k: wx(k).start())
    each(1, NZ, lambda k: oz(k).start())

    def forward(k):
        hz_in(k).wait_recv()
        each(1, NX, lambda j: hx(k, j).start())

    each(1, NZ, forward)
    own_copies[3].wait()
    each(1, NY, lambda j: wy(0, j).start())
    ws(0, 0).start()
    each(1, NX, lambda k: kx(k).start())
    each(1, NX, lambda k: vx(k).start())

    for block in range(NX):
        first = (block * NZ + z) * CTX
        slot = lax.div(first, CH)
        later = lax.min(slot + 1, NCH - 1)
        row = first + lax.broadcasted_iota(jnp.int32, (1, CTX), 1)
        code = jnp.where(
            row < (slot + 1) * CH, sbase[slot] - slot * CH, sbase[later] - (slot + 1) * CH
        ) + row
        hit = jnp.max(
            jnp.where(qmeta[:, 2:3] == row, 1, 0), axis=0, keepdims=True
        )
        kcode[:, block * CTX : (block + 1) * CTX] = jnp.where(hit > 0, DEAD, code)
    kcode[:, CACHED:KEYS] = fcode[pl.ds(z, 1), :]
    kall[CACHED:KEYS, :] = jnp.zeros((KEYS - CACHED, PART), BF16)
    vall[CACHED:KEYS, :] = jnp.zeros((KEYS - CACHED, PART), BF16)

    def arrived(k):
        each(1, NX, lambda j: hx_in(k, j).wait_recv())

    each(0, NZ, arrived)
    own_copies[1].wait()
    each(1, NDP, lambda k: w4_in(k).wait_recv())
    low = lanes(SEL // 2) < HEAD_DIM // 2

    def project(part):
        rows = hid[pl.ds(part * 8, 8)].reshape(128, D)
        got = jnp.dot(rows, w4buf[...].reshape(D, 256), preferred_element_type=F32)
        got = got.astype(BF16)
        kvs[pl.ds(part * 2, 2)] = got[:, :HEAD_DIM].reshape(2, GRP, HEAD_DIM)
        return got[:, HEAD_DIM:]

    for half in range(2):
        first = project(half)
        second = project(half + 2)
        qpk[half * 128 : (half + 1) * 128, :] = jnp.where(
            low[:128], first.astype(F32), second.astype(F32)
        ).astype(BF16)
    each(1, NZ, lambda k: qz(k).start())
    each(1, NZ, lambda k: cz(k).start())
    qrecv[pl.ds(z, 1)] = qpk[...][None]
    kvrecv[pl.ds(z, 1)] = kvs[pl.ds(z, 1)]

    own_copies[2].wait()
    each(1, NZ, lambda k: oz_in(k).wait_recv())
    each(1, NY, lambda k: oy(k).start())
    osib(0).start()

    def weights_on(k):
        wx_in(k).wait_recv()
        each(1, NY, lambda j: wy(k, j).start())
        ws(k, 0).start()

    each(1, NX, weights_on)

    def weights_side(k):
        def one(j):
            wy_in(k, j).wait_recv()
            ws(k, j).start()

        each(1, NY, one)

    each(1, NZ, lambda k: qz_in(k).wait_recv())
    each(1, NZ, lambda k: cz_in(k).wait_recv())
    low_f = lanes(GRP) < HEAD_DIM // 2

    def q_head(h):
        a = qrecv[2 * h].astype(F32)
        b = qrecv[2 * h + 1].astype(F32)
        top = jnp.where(low, a, pltpu.roll(b, 64, 1))
        bottom = jnp.where(low, pltpu.roll(a, 64, 1), b)
        return top, bottom

    def f_head(h):
        a = kvrecv[2 * h].astype(F32)
        b = kvrecv[2 * h + 1].astype(F32)
        return jnp.where(low_f, a, pltpu.roll(b, 64, 1)), jnp.where(low_f, pltpu.roll(a, 64, 1), b)

    sq[...] = jnp.zeros_like(sq)
    for h in range(HEADS):
        top, bottom = q_head(h)
        sq[: SEL // 2] += top * top
        sq[SEL // 2 : SEL] += bottom * bottom
        key, value = f_head(h)
        sq[SEL : SEL + GRP] += key * key
        vall[CACHED : CACHED + GRP, h * HEAD_DIM : (h + 1) * HEAD_DIM] = value.astype(BF16)
    stat[pl.ds(x, 1)] = lax.dot_general(
        jnp.ones((8, HEAD_DIM), F32), sq[...], (((1,), (1,)), ((), ())),
        precision=HIGH, preferred_element_type=F32,
    )[None]
    each(1, NX, lambda k: stx(k).start())
    each(1, NX, lambda k: stx_in(k).wait_recv())
    total = stat[0] + stat[1] + stat[2] + stat[3]
    factor = lax.rsqrt(total * (1.0 / D) + EPSILON)
    sq[...] = lax.dot_general(
        factor, jnp.full((8, HEAD_DIM), 0.125, F32), (((0,), (0,)), ((), ())),
        precision=HIGH, preferred_element_type=F32,
    )
    grp_rows = pl.ds(pl.multiple_of(z * GRP, GRP), GRP)
    for h in range(HEADS):
        cols = pl.ds(pl.multiple_of(x * PART + h * HEAD_DIM, HEAD_DIM), HEAD_DIM)
        top, bottom = q_head(h)
        gain = gains[0:1, cols]
        for part, rows in ((top, slice(0, SEL // 2)), (bottom, slice(SEL // 2, SEL))):
            v = part * sq[rows] * gain
            qh[h, rows] = (v * qcos[rows] + pltpu.roll(v, 64, 1) * qsin[rows]).astype(BF16)
        key, _ = f_head(h)
        v = key * sq[SEL : SEL + GRP] * gains[1:2, cols]
        v = (v * qcos[grp_rows] + pltpu.roll(v, 64, 1) * qsin[grp_rows]).astype(BF16)
        kall[CACHED : CACHED + GRP, h * HEAD_DIM : (h + 1) * HEAD_DIM] = v
        kf[:, :, h * HEAD_DIM : (h + 1) * HEAD_DIM] = v.reshape(NX, OWN, HEAD_DIM)
    each(1, NX, lambda k: fx(k).start())
    frecv[pl.ds(x, 1)] = kf[pl.ds(x, 1)]
    weights_side(0)

    own_copies[4].wait()
    each(1, NX, lambda k: kx_in(k).wait_recv())

    def turn(block):
        first = (block * NZ + z) * CTX
        slot = lax.div(first, CH)
        later = lax.min(slot + 1, NCH - 1)
        row = first + lax.broadcasted_iota(jnp.int32, (CTX, HEAD_DIM), 0)
        here = row < (slot + 1) * CH
        cosine = jnp.where(here, scos[pl.ds(slot, 1), :], scos[pl.ds(later, 1), :])
        sine = jnp.where(here, ssin[pl.ds(slot, 1), :], ssin[pl.ds(later, 1), :])
        for h in range(HEADS):
            cols = slice(h * HEAD_DIM, (h + 1) * HEAD_DIM)
            v = kraw[block, :, cols].astype(F32)
            kall[key_rows(block), cols] = (v * cosine + pltpu.roll(v, 64, 1) * sine).astype(BF16)

    each(0, NX, turn)
    own_copies[5].wait()
    each(1, NX, lambda k: vx_in(k).wait_recv())

    obst[...] = jnp.zeros_like(obst)
    lane = lanes(128)

    def attend(step):
        h = lax.div(step, SEL // 128)
        part = lax.rem(step, SEL // 128)
        rows = pl.ds(pl.multiple_of(part * 128, 128), 128)
        cols = pl.ds(pl.multiple_of(h * HEAD_DIM, HEAD_DIM), HEAD_DIM)
        scores = lax.dot_general(
            qh[h, rows], kall[:, cols], (((1,), (1,)), ((), ())), preferred_element_type=F32
        )
        code = kcode[...]
        usable = (code <= qmeta[rows, 0:1]) & (code >= qmeta[rows, 1:2])
        scores = jnp.where(usable, scores * SCORE, NEGATIVE)
        most = jnp.maximum(jnp.max(scores, axis=1, keepdims=True), FLOOR)
        weight = jnp.exp2(scores - most)
        mass = jnp.sum(weight, axis=1, keepdims=True)
        mixed = jnp.dot(weight.astype(BF16), vall[:, cols], preferred_element_type=F32)
        two = pl.ds(part * 2, 2)
        obuf[two, :, cols] = mixed.astype(BF16).reshape(2, GRP, HEAD_DIM)
        old = obst[two].reshape(128, HEAD_DIM)
        new = jnp.where(lane == h, most, jnp.where(lane == h + HEADS, mass, old))
        obst[two] = new.reshape(2, GRP, HEAD_DIM)

    each(0, HEADS * (SEL // 128), attend)
    each(1, NZ, lambda k: tex(k).start())
    each(1, NZ, lambda k: oex(k).start())
    orecv[pl.ds(z, 1)] = obuf[pl.ds(z, 1)]
    strecv[pl.ds(z, 1)] = obst[pl.ds(z, 1)]
    each(1, NY, lambda k: oy_in(k).wait_recv())
    each(1, NY, lambda k: osib(k).start())
    weights_side(1)
    each(1, NZ, lambda k: tex_in(k).wait_recv())
    each(1, NZ, lambda k: oex_in(k).wait_recv())
    peak = strecv[0]
    for p in range(1, NZ):
        peak = jnp.maximum(peak, strecv[p])
    mass = jnp.zeros((GRP, HEAD_DIM), F32)
    for p in range(NZ):
        mass += jnp.exp2(strecv[p] - peak) * pltpu.roll(strecv[p], HEAD_DIM - HEADS, 1)
    valid = lanes(GRP) < HEADS
    inverse = 1.0 / jnp.where(valid, mass, 1.0)
    heads = [jnp.zeros((GRP, HEAD_DIM), F32) for _ in range(HEADS)]
    for p in range(NZ):
        share = jnp.exp2(strecv[p] - peak) * inverse
        for h in range(HEADS):
            part = orecv[p, :, h * HEAD_DIM : (h + 1) * HEAD_DIM].astype(F32)
            heads[h] += part * share[:, h : h + 1]
    attn = jnp.concatenate(heads, axis=1).astype(BF16)
    each(0, NY, lambda k: osib_in(k).wait_recv())

    def out_block(c):
        got = jnp.dot(attn, wobuf[c].reshape(PART, 256), preferred_element_type=F32)
        cols = pl.ds(pl.multiple_of(c * 256, 256), 256)
        ysend[:, :, cols] = got.astype(BF16).reshape(NX, OWN, 256)

    each(0, NDP, out_block)
    each(1, NX, lambda k: yx(k).start())
    yrecv[pl.ds(x, 1)] = ysend[pl.ds(x, 1)]
    weights_side(2)
    each(1, NX, lambda k: yx_in(k).wait_recv())
    y = yrecv[0].astype(F32)
    for p in range(1, NX):
        y += yrecv[p].astype(F32)
    y = y * lax.rsqrt(jnp.mean(y * y, axis=1, keepdims=True) + EPSILON) * gains[2:3, :]
    following = (hid[z * NX + x].astype(F32) + y).astype(BF16)
    hn[...] = following
    each(1, NZ, lambda k: nz(k).start())
    hbuf[pl.ds(z, 1)] = following[None]
    weights_side(3)

    each(1, NZ, lambda k: nz_in(k).wait_recv())

    def sides(k):
        each(0, NY, lambda j: ws_in(k, j).wait_recv())

    each(0, NX, sides)

    def gate(c):
        rows = hbuf[...].reshape(NZ * OWN, D)
        g = jnp.dot(rows, wbuf[:, c, 0].reshape(D, 256), preferred_element_type=F32)
        u = jnp.dot(rows, wbuf[:, c, 1].reshape(D, 256), preferred_element_type=F32)
        cols = pl.ds(pl.multiple_of(c * 256, 256), 256)
        act[:, cols] = (jax.nn.silu(g) * u).astype(BF16)

    each(0, NX, gate)

    def down(c):
        got = jnp.dot(act[...], wbuf[c, :, 2].reshape(NX * 256, 256), preferred_element_type=F32)
        cols = pl.ds(pl.multiple_of(c * 256, 256), 256)
        dsend[:, :, cols] = got.astype(BF16).reshape(NZ, OWN, 256)

    each(0, NDP, down)
    each(1, NZ, lambda k: dz(k).start())
    drecv[pl.ds(z, 1)] = dsend[pl.ds(z, 1)]

    each(1, NX, lambda k: fx_in(k).wait_recv())
    for p in range(NX):
        fresh[:, p * PART : (p + 1) * PART] = frecv[p]

    each(1, NZ, lambda k: dz_in(k).wait_recv())
    t = drecv[0].astype(F32)
    for p in range(1, NZ):
        t += drecv[p].astype(F32)
    t = t * lax.rsqrt(jnp.mean(t * t, axis=1, keepdims=True) + EPSILON) * gains[3:4, :]
    out[...] = (hn[...].astype(F32) + t).astype(BF16)

    for copy in (hz, oz, qz, cz, oex, tex, nz, dz):
        each(1, NZ, lambda k, copy=copy: copy(k).wait_send())
    for copy in (wx, kx, vx, stx, fx, yx):
        each(1, NX, lambda k, copy=copy: copy(k).wait_send())
    each(1, NDP, lambda k: w4c(k).wait_send())
    each(1, NY, lambda k: oy(k).wait_send())
    each(0, NY, lambda k: osib(k).wait_send())
    each(0, NZ, lambda k: each(1, NX, lambda j: hx(k, j).wait_send()))
    each(0, NX, lambda k: each(1, NY, lambda j: wy(k, j).wait_send()))
    each(0, NX, lambda k: each(0, NY, lambda j: ws(k, j).wait_send()))


def frequencies(index_float):
    return jnp.exp(index_float * (-2.0 * math.log(THETA) / HEAD_DIM))


def tables(position):
    half = jnp.arange(HEAD_DIM // 2, dtype=jnp.int32).astype(F32)
    angles = position.astype(F32)[:, None] * frequencies(half)[None, :]
    cosine, sine = jnp.cos(angles), jnp.sin(angles)
    return jnp.concatenate([cosine, cosine], axis=1), jnp.concatenate([-sine, sine], axis=1)


def layer(
    hidden_sel, picked, order, lengths, offsets, cache_keys, cache_values, w_qkv, w_out,
    w_gate_up, w_down, gains,
):
    order_row, length_row, offset_row = order[0], lengths[0], offsets[0]
    ends = jnp.cumsum(length_row)
    request = jnp.sum((order_row[:, None] >= ends[None, :]).astype(jnp.int32), axis=1)
    mine = request[:, None] == jnp.arange(REQS, dtype=jnp.int32)[None, :]
    start = jnp.sum(jnp.where(mine, (ends - length_row)[None, :], 0), axis=1)
    shift = jnp.sum(jnp.where(mine, offset_row[None, :], 0), axis=1)
    base = shift + (order_row - start) * CH
    code = request * SPAN + base
    scos, ssin = tables(jnp.pad(base, (0, 16 - NCH)))
    rows = picked[0].reshape(NX, NZ, OWN).transpose(1, 0, 2).reshape(SEL)
    chosen = (rows // CH)[:, None] == jnp.arange(NCH, dtype=jnp.int32)[None, :]
    in_span = rows % CH
    q_code = jnp.sum(jnp.where(chosen, code[None, :], 0), axis=1) + in_span
    q_low = (q_code // SPAN) * SPAN
    qcos, qsin = tables(q_code - q_low)
    qmeta = jnp.stack([q_code, q_low, rows, rows], axis=1)
    fcode = jnp.pad(q_code.reshape(NZ, GRP), ((0, 0), (0, HEAD_DIM - GRP)), constant_values=DEAD)
    w4 = jnp.concatenate([w_qkv[1], w_qkv[2], w_qkv[0], w_qkv[0]], axis=1)
    wm = jnp.concatenate([w_gate_up, w_down[None]], axis=0)

    vmem = pl.BlockSpec(memory_space=pltpu.VMEM)
    far = pl.BlockSpec(memory_space=pl.ANY)
    smem = pl.BlockSpec(memory_space=pltpu.SMEM)
    dma = pltpu.SemaphoreType.DMA
    out, fresh = pl.pallas_call(
        kernel,
        out_shape=(
            jax.ShapeDtypeStruct((OWN, D), BF16),
            jax.ShapeDtypeStruct((OWN, D), BF16),
        ),
        in_specs=[vmem, far, far, far, far, far, vmem, vmem, vmem, vmem, vmem, vmem, vmem, smem],
        out_specs=(vmem, vmem),
        scratch_shapes=[
            pltpu.VMEM((NZ * NX, OWN, D), BF16),
            pltpu.VMEM((NDP, 256, 256), BF16),
            pltpu.VMEM((NDP, NZ, 64, 256), BF16),
            pltpu.VMEM((NDP, NX, 3, 256, 256), BF16),
            pltpu.VMEM((NX, CTX, PART), BF16),
            pltpu.VMEM((KEYS, PART), BF16),
            pltpu.VMEM((KEYS, PART), BF16),
            pltpu.VMEM((1, KEYS), jnp.int32),
            pltpu.VMEM((SEL // 2, HEAD_DIM), BF16),
            pltpu.VMEM((NZ, GRP, HEAD_DIM), BF16),
            pltpu.VMEM((NZ, SEL // 2, HEAD_DIM), BF16),
            pltpu.VMEM((NZ, GRP, HEAD_DIM), BF16),
            pltpu.VMEM((SEL + 128, HEAD_DIM), F32),
            pltpu.VMEM((NX, 8, SEL + 128), F32),
            pltpu.VMEM((HEADS, SEL, HEAD_DIM), BF16),
            pltpu.VMEM((NX, OWN, PART), BF16),
            pltpu.VMEM((NX, OWN, PART), BF16),
            pltpu.VMEM((NZ, GRP, PART), BF16),
            pltpu.VMEM((NZ, GRP, HEAD_DIM), F32),
            pltpu.VMEM((NZ, GRP, PART), BF16),
            pltpu.VMEM((NZ, GRP, HEAD_DIM), F32),
            pltpu.VMEM((NX, OWN, D), BF16),
            pltpu.VMEM((NX, OWN, D), BF16),
            pltpu.VMEM((OWN, D), BF16),
            pltpu.VMEM((NZ, OWN, D), BF16),
            pltpu.VMEM((NZ * OWN, NX * 256), BF16),
            pltpu.VMEM((NZ, OWN, D), BF16),
            pltpu.VMEM((NZ, OWN, D), BF16),
            dma((NZ,)), dma((NZ,)),
            dma((NZ, NX)), dma((NZ, NX)),
            dma((NDP,)), dma((NDP,)),
            dma((NZ,)), dma((NZ,)),
            dma((NY,)), dma((NY,)),
            dma((NY,)), dma((NY,)),
            dma((NX,)), dma((NX,)),
            dma((NX, NY)), dma((NX, NY)),
            dma((NX, NY)), dma((NX, NY)),
            dma((NX,)), dma((NX,)),
            dma((NX,)), dma((NX,)),
            dma((NZ,)), dma((NZ,)),
            dma((NZ,)), dma((NZ,)),
            dma((NX,)), dma((NX,)),
            dma((NX,)), dma((NX,)),
            dma((NZ,)), dma((NZ,)),
            dma((NZ,)), dma((NZ,)),
            dma((NX,)), dma((NX,)),
            dma((NZ,)), dma((NZ,)),
            dma((NZ,)), dma((NZ,)),
            dma((6,)),
        ],
        compiler_params=pltpu.CompilerParams(
            collective_id=0, has_side_effects=True, vmem_limit_bytes=56 << 20
        ),
    )(
        hidden_sel[0], cache_keys[0], cache_values[0], w4, w_out, wm, gains, qmeta, fcode,
        qcos, qsin, scos, ssin, code,
    )
    return (out[None], fresh[None])


def solution(mesh):
    placed = (
        P("dp", "tensor", None),
        P("dp", None),
        P("dp", None),
        P("dp", None),
        P("dp", None),
        P("dp", "tensor", None),
        P("dp", "tensor", None),
        P(None, "dp", "tensor"),
        P("tensor", "dp"),
        P(None, "dp", "tensor"),
        P("tensor", "dp"),
        P(),
    )
    return jax.shard_map(
        layer,
        mesh=mesh,
        in_specs=placed,
        out_specs=(P("dp", "tensor", None), P("dp", "tensor", None)),
        check_vma=False,
    )
```

```python
import math

import jax
import jax.numpy as jnp
from jax import lax
from jax.experimental import pallas as pl
from jax.experimental.pallas import tpu as pltpu
from jax.sharding import PartitionSpec as P

HEAD_DIM = 128
CH = 1024
NCH = 12
REQS = 3
NX = 4
NZ = 8
NDP = 8
NY = 4
D = 2048
PART = D // NX
HEADS = PART // HEAD_DIM
OWN = 16
GRP = NX * OWN
SEL = NZ * GRP
CTX = 384
CACHED = NX * CTX
KEYS = CACHED + 128
SPAN = 1 << 14
DEAD = 1 << 30

THETA = 500000.0
EPSILON = 1e-06
NEGATIVE = -1e30
FLOOR = -1e20
SCORE = HEAD_DIM ** (-0.5) * math.log2(math.e)
MESH = pl.DeviceIdType.MESH
F32, BF16 = jnp.float32, jnp.bfloat16
HIGH = lax.Precision.HIGHEST


def lanes(rows):
    return lax.broadcasted_iota(jnp.int32, (rows, HEAD_DIM), 1)


def kernel(
    hidden,
    keys,
    values,
    w4,
    wo,
    wm,
    gains,
    qmeta,
    fcode,
    qcos,
    qsin,
    scos,
    ssin,
    sbase,
    out,
    fresh,
    hid,
    w4buf,
    wobuf,
    wbuf,
    kraw,
    kall,
    vall,
    kcode,
    psend,
    precv,
    qpk,
    kvs,
    qrecv,
    kvrecv,
    sq,
    stat,
    qh,
    kf,
    frecv,
    obuf,
    orecv,
    ysend,
    yrecv,
    hn,
    hbuf,
    act,
    dsend,
    drecv,
    hz_s,
    hz_r,
    w4_sems,
    wo_sems,
    wm_sems,
    k_s,
    k_r,
    v_s,
    v_r,
    p_s,
    p_r,
    q_s,
    q_r,
    c_s,
    c_r,
    st_s,
    st_r,
    f_s,
    f_r,
    o_s,
    o_r,
    y_s,
    y_r,
    n_s,
    n_r,
    d_s,
    d_r,
    loc,
):
    tens = lax.axis_index("tensor")
    dp = lax.axis_index("dp")
    x = lax.div(tens, NZ)
    z = lax.rem(tens, NZ)
    core = lax.rem(dp, 2)
    sib = dp + 1 - 2 * core

    def xa(k):
        return lax.rem(x + k, NX)

    def za(k):
        return lax.rem(z + k, NZ)

    def da(k):
        return lax.rem(dp + k, NDP)

    def zdev(k):
        return {"tensor": x * NZ + za(k)}

    def xdev(k):
        return {"tensor": xa(k) * NZ + z}

    def send(src, dst, ssem, rsem, dev):
        return pltpu.make_async_remote_copy(
            src_ref=src, dst_ref=dst, send_sem=ssem, recv_sem=rsem, device_id=dev,
            device_id_type=MESH,
        )

    def each(first, last, body):
        def step(k, carry):
            body(k)
            return carry

        lax.fori_loop(first, last, step, 0)

    class Spread:
        def __init__(self, sems, slots, source, first, peers, entry, entry_in, at):
            (self.e_s, self.e_r, self.n_s, self.y_r, self.r_s, self.s_s, self.s_r) = sems
            self.slots, self.source, self.first, self.peers = slots, source, first, peers
            self.entry, self.entry_in, self.at = entry, entry_in, at

        def enter(self, k):
            return send(self.source, self.entry, self.e_s.at[k], self.e_r.at[k], self.first(k))

        def enter_in(self, k):
            at = self.entry_in(k)
            return send(at, at, self.e_s.at[k], self.e_r.at[k], self.first(k))

        def near(self, k, j):
            at = self.at(dp, k)
            return send(at, at, self.n_s.at[k, j], self.y_r.at[k, j], {"dp": da(2 * j)})

        def near_in(self, k, j):
            at = self.at(da(NDP - 2 * j), k)
            return send(at, at, self.n_s.at[k, j], self.y_r.at[k, j], {"dp": da(2 * j)})

        def way(self, k):
            return 1 + 2 * lax.div(k, self.slots // 2)

        def relay(self, k):
            j = self.way(k)
            at = self.at(da(NDP - 2 * j), k)
            return send(at, at, self.r_s.at[k], self.y_r.at[k, 2], {"dp": da(2 * j)})

        def relay_in(self, k):
            at = self.at(da(4), k)
            return send(at, at, self.r_s.at[k], self.y_r.at[k, 2], {"dp": da(2)})

        def side(self, k, j):
            at = self.at(da(NDP - 2 * j), k)
            return send(at, at, self.s_s.at[k, j], self.s_r.at[k, j], {"dp": sib})

        def side_in(self, k, j):
            at = self.at(lax.rem(sib + NDP - 2 * j, NDP), k)
            return send(at, at, self.s_s.at[k, j], self.s_r.at[k, j], {"dp": sib})

        def start(self):
            each(1, self.peers, lambda k: self.enter(k).start())

        def go_near(self, k):
            self.near(k, 1).start()
            self.near(k, 3).start()
            self.side(k, 0).start()

        def step_near(self, k):
            self.near_in(k, 1).wait_recv()
            self.near_in(k, 3).wait_recv()
            self.relay(k).start()
            self.side(k, 1).start()
            self.side(k, 3).start()

        def step_far(self, k):
            self.relay_in(k).wait_recv()
            self.side(k, 2).start()

        def arrive(self):
            each(0, self.slots, lambda k: each(0, NY, lambda j: self.side_in(k, j).wait_recv()))

        def finish(self):
            each(1, self.peers, lambda k: self.enter(k).wait_send())

            def one(k):
                self.near(k, 1).wait_send()
                self.near(k, 3).wait_send()
                self.relay(k).wait_send()
                each(0, NY, lambda j: self.side(k, j).wait_send())

            each(0, self.slots, one)

    def x_slot(buf):
        return lambda d, k: buf.at[d, xa(NX - k)]

    qkv_w = Spread(
        w4_sems, NX, w4, xdev, NX, w4buf.at[dp, x], lambda k: w4buf.at[dp, xa(NX - k)],
        x_slot(w4buf),
    )
    ffn_w = Spread(
        wm_sems, NX, wm, xdev, NX, wbuf.at[dp, x], lambda k: wbuf.at[dp, xa(NX - k)],
        x_slot(wbuf),
    )
    out_w = Spread(
        wo_sems, 2, wo, zdev, NZ, wobuf.at[dp, z], lambda k: wobuf.at[dp, za(NZ - k)],
        lambda d, k: wobuf.at[d, pl.ds(4 * k, 4)],
    )

    def hz(k):
        return send(hidden, hid.at[z], hz_s.at[k], hz_r.at[k], zdev(k))

    def hz_in(k):
        at = hid.at[za(NZ - k)]
        return send(at, at, hz_s.at[k], hz_r.at[k], zdev(k))

    def columns(at):
        return pl.ds(pl.multiple_of(at * PART, PART), PART)

    def key_rows(at):
        return pl.ds(pl.multiple_of(at * CTX, 128), CTX)

    def kx(k):
        return send(keys.at[:, columns(xa(k))], kraw.at[x], k_s.at[k], k_r.at[k], xdev(k))

    def kx_in(k):
        at = kraw.at[xa(NX - k)]
        return send(at, at, k_s.at[k], k_r.at[k], xdev(k))

    def vx(k):
        return send(
            values.at[:, columns(xa(k))], vall.at[key_rows(x)], v_s.at[k], v_r.at[k], xdev(k)
        )

    def vx_in(k):
        at = vall.at[key_rows(xa(NX - k))]
        return send(at, at, v_s.at[k], v_r.at[k], xdev(k))

    def px(k):
        return send(psend.at[xa(k)], precv.at[x], p_s.at[k], p_r.at[k], xdev(k))

    def px_in(k):
        at = precv.at[xa(NX - k)]
        return send(at, at, p_s.at[k], p_r.at[k], xdev(k))

    def qz(k):
        return send(qpk, qrecv.at[z], q_s.at[k], q_r.at[k], zdev(k))

    def qz_in(k):
        at = qrecv.at[za(NZ - k)]
        return send(at, at, q_s.at[k], q_r.at[k], zdev(k))

    def cz(k):
        return send(kvs.at[za(k)], kvrecv.at[z], c_s.at[k], c_r.at[k], zdev(k))

    def cz_in(k):
        at = kvrecv.at[za(NZ - k)]
        return send(at, at, c_s.at[k], c_r.at[k], zdev(k))

    def stx(k):
        return send(stat.at[x], stat.at[x], st_s.at[k], st_r.at[k], xdev(k))

    def stx_in(k):
        at = stat.at[xa(NX - k)]
        return send(at, at, st_s.at[k], st_r.at[k], xdev(k))

    def fx(k):
        return send(kf.at[xa(k)], frecv.at[x], f_s.at[k], f_r.at[k], xdev(k))

    def fx_in(k):
        at = frecv.at[xa(NX - k)]
        return send(at, at, f_s.at[k], f_r.at[k], xdev(k))

    def oex(k):
        return send(obuf.at[za(k)], orecv.at[z], o_s.at[k], o_r.at[k], zdev(k))

    def oex_in(k):
        at = orecv.at[za(NZ - k)]
        return send(at, at, o_s.at[k], o_r.at[k], zdev(k))

    def yx(k):
        return send(ysend.at[xa(k)], yrecv.at[x], y_s.at[k], y_r.at[k], xdev(k))

    def yx_in(k):
        at = yrecv.at[xa(NX - k)]
        return send(at, at, y_s.at[k], y_r.at[k], xdev(k))

    def nz(k):
        return send(hn, hbuf.at[z], n_s.at[k], n_r.at[k], zdev(k))

    def nz_in(k):
        at = hbuf.at[za(NZ - k)]
        return send(at, at, n_s.at[k], n_r.at[k], zdev(k))

    def dz(half, k):
        return send(
            dsend.at[half, za(k)], drecv.at[half, z], d_s.at[half, k], d_r.at[half, k], zdev(k)
        )

    def dz_in(half, k):
        at = drecv.at[half, za(NZ - k)]
        return send(at, at, d_s.at[half, k], d_r.at[half, k], zdev(k))

    own_copies = [
        pltpu.make_async_copy(hidden, hid.at[z], loc.at[0]),
        pltpu.make_async_copy(w4, w4buf.at[dp, x], loc.at[1]),
        pltpu.make_async_copy(wo, wobuf.at[dp, z], loc.at[2]),
        pltpu.make_async_copy(wm, wbuf.at[dp, x], loc.at[3]),
        pltpu.make_async_copy(keys.at[:, columns(x)], kraw.at[x], loc.at[4]),
        pltpu.make_async_copy(values.at[:, columns(x)], vall.at[key_rows(x)], loc.at[5]),
    ]
    for copy in own_copies:
        copy.start()

    barrier = pltpu.get_barrier_semaphore()

    def greet(dev):
        pl.semaphore_signal(barrier, inc=1, device_id=dev, device_id_type=MESH)

    each(1, NZ, lambda k: greet(zdev(k)))
    each(1, NX, lambda k: greet(xdev(k)))
    greet({"dp": da(2)})
    greet({"dp": da(6)})
    greet({"dp": sib})
    pl.semaphore_wait(barrier, NZ + NX + 1)

    qkv_w.start()
    own_copies[1].wait()
    qkv_w.go_near(0)
    each(1, NZ, lambda k: hz(k).start())
    ffn_w.start()

    def qkv_on(k):
        qkv_w.enter_in(k).wait_recv()
        qkv_w.go_near(k)

    each(1, NX, qkv_on)
    each(1, NX, lambda k: kx(k).start())
    each(1, NX, lambda k: vx(k).start())
    out_w.start()

    for block in range(NX):
        first = (block * NZ + z) * CTX
        slot = lax.div(first, CH)
        later = lax.min(slot + 1, NCH - 1)
        row = first + lax.broadcasted_iota(jnp.int32, (1, CTX), 1)
        code = jnp.where(
            row < (slot + 1) * CH, sbase[slot] - slot * CH, sbase[later] - (slot + 1) * CH
        ) + row
        hit = jnp.max(
            jnp.where(qmeta[:, 2:3] == row, 1, 0), axis=0, keepdims=True
        )
        kcode[:, block * CTX : (block + 1) * CTX] = jnp.where(hit > 0, DEAD, code)
    kcode[:, CACHED:KEYS] = fcode[pl.ds(z, 1), :]
    kall[CACHED:KEYS, :] = jnp.zeros((KEYS - CACHED, PART), BF16)
    vall[CACHED:KEYS, :] = jnp.zeros((KEYS - CACHED, PART), BF16)

    each(0, NX, qkv_w.step_near)
    own_copies[2].wait()
    own_copies[3].wait()
    each(1, NZ, lambda k: out_w.enter_in(k).wait_recv())
    each(0, NX, qkv_w.step_far)
    each(0, 2, out_w.go_near)
    ffn_w.go_near(0)

    own_copies[0].wait()
    each(1, NZ, lambda k: hz_in(k).wait_recv())
    qkv_w.arrive()

    def project(i):
        k = lax.rem(i + 1, NX)
        at = xa(k)
        rows = hid[...].reshape(NZ * OWN, D)
        got = jnp.dot(rows, w4buf[:, at].reshape(D, 256), preferred_element_type=F32)
        psend[at] = got.astype(BF16)
        return k

    def project_send(i):
        k = project(i)
        px(k).start()

    each(0, NX - 1, project_send)
    project(NX - 1)
    precv[pl.ds(x, 1)] = psend[pl.ds(x, 1)]

    def ffn_on(k):
        ffn_w.enter_in(k).wait_recv()
        ffn_w.go_near(k)

    each(1, NX, ffn_on)
    each(1, NX, lambda k: px_in(k).wait_recv())
    low = lanes(SEL // 2) < HEAD_DIM // 2
    for g in range(NZ // 2):
        two = []
        for gg in (g, g + NZ // 2):
            rows = jnp.concatenate(
                [precv[p, gg * OWN : (gg + 1) * OWN] for p in range(NX)], axis=0
            )
            kvs[gg] = rows[:, :HEAD_DIM]
            two.append(rows[:, HEAD_DIM:].astype(F32))
        qpk[g * GRP : (g + 1) * GRP, :] = jnp.where(low[:GRP], two[0], two[1]).astype(BF16)
    each(1, NZ, lambda k: qz(k).start())
    each(1, NZ, lambda k: cz(k).start())
    qrecv[pl.ds(z, 1)] = qpk[...][None]
    kvrecv[pl.ds(z, 1)] = kvs[pl.ds(z, 1)]
    each(0, 2, out_w.step_near)

    each(1, NZ, lambda k: qz_in(k).wait_recv())
    each(1, NZ, lambda k: cz_in(k).wait_recv())
    low_f = lanes(GRP) < HEAD_DIM // 2

    def q_head(h):
        a = qrecv[2 * h].astype(F32)
        b = qrecv[2 * h + 1].astype(F32)
        top = jnp.where(low, a, pltpu.roll(b, 64, 1))
        bottom = jnp.where(low, pltpu.roll(a, 64, 1), b)
        return top, bottom

    def f_head(h):
        a = kvrecv[2 * h].astype(F32)
        b = kvrecv[2 * h + 1].astype(F32)
        return jnp.where(low_f, a, pltpu.roll(b, 64, 1)), jnp.where(low_f, pltpu.roll(a, 64, 1), b)

    sq[...] = jnp.zeros_like(sq)
    for h in range(HEADS):
        top, bottom = q_head(h)
        sq[: SEL // 2] += top * top
        sq[SEL // 2 : SEL] += bottom * bottom
        key, value = f_head(h)
        sq[SEL : SEL + GRP] += key * key
        vall[CACHED : CACHED + GRP, h * HEAD_DIM : (h + 1) * HEAD_DIM] = value.astype(BF16)
    stat[pl.ds(x, 1)] = lax.dot_general(
        jnp.ones((8, HEAD_DIM), F32), sq[...], (((1,), (1,)), ((), ())),
        precision=HIGH, preferred_element_type=F32,
    )[None]
    each(1, NX, lambda k: stx(k).start())
    each(0, 2, out_w.step_far)
    each(1, NX, lambda k: stx_in(k).wait_recv())
    total = stat[0] + stat[1] + stat[2] + stat[3]
    factor = lax.rsqrt(total * (1.0 / D) + EPSILON)
    sq[...] = lax.dot_general(
        factor, jnp.full((8, HEAD_DIM), 0.125, F32), (((0,), (0,)), ((), ())),
        precision=HIGH, preferred_element_type=F32,
    )
    grp_rows = pl.ds(pl.multiple_of(z * GRP, GRP), GRP)
    for h in range(HEADS):
        cols = pl.ds(pl.multiple_of(x * PART + h * HEAD_DIM, HEAD_DIM), HEAD_DIM)
        top, bottom = q_head(h)
        gain = gains[0:1, cols]
        for part, rows in ((top, slice(0, SEL // 2)), (bottom, slice(SEL // 2, SEL))):
            v = part * sq[rows] * gain
            qh[h, rows] = (v * qcos[rows] + pltpu.roll(v, 64, 1) * qsin[rows]).astype(BF16)
        key, _ = f_head(h)
        v = key * sq[SEL : SEL + GRP] * gains[1:2, cols]
        v = (v * qcos[grp_rows] + pltpu.roll(v, 64, 1) * qsin[grp_rows]).astype(BF16)
        kall[CACHED : CACHED + GRP, h * HEAD_DIM : (h + 1) * HEAD_DIM] = v
        kf[:, :, h * HEAD_DIM : (h + 1) * HEAD_DIM] = v.reshape(NX, OWN, HEAD_DIM)
    each(1, NX, lambda k: fx(k).start())
    frecv[pl.ds(x, 1)] = kf[pl.ds(x, 1)]
    ffn_w.step_near(0)

    own_copies[4].wait()
    each(1, NX, lambda k: kx_in(k).wait_recv())

    def turn(block):
        first = (block * NZ + z) * CTX
        slot = lax.div(first, CH)
        later = lax.min(slot + 1, NCH - 1)
        row = first + lax.broadcasted_iota(jnp.int32, (CTX, HEAD_DIM), 0)
        here = row < (slot + 1) * CH
        cosine = jnp.where(here, scos[pl.ds(slot, 1), :], scos[pl.ds(later, 1), :])
        sine = jnp.where(here, ssin[pl.ds(slot, 1), :], ssin[pl.ds(later, 1), :])
        for h in range(HEADS):
            cols = slice(h * HEAD_DIM, (h + 1) * HEAD_DIM)
            v = kraw[block, :, cols].astype(F32)
            kall[key_rows(block), cols] = (v * cosine + pltpu.roll(v, 64, 1) * sine).astype(BF16)

    each(0, NX, turn)
    own_copies[5].wait()
    each(1, NX, lambda k: vx_in(k).wait_recv())

    lane = lanes(128)

    def attend(part):
        rows = pl.ds(pl.multiple_of(part * 128, 128), 128)
        two = pl.ds(part * 2, 2)

        def head(h, marks):
            cols = pl.ds(pl.multiple_of(h * HEAD_DIM, HEAD_DIM), HEAD_DIM)
            scores = lax.dot_general(
                qh[h, rows], kall[:, cols], (((1,), (1,)), ((), ())), preferred_element_type=F32
            )
            code = kcode[...]
            usable = (code <= qmeta[rows, 0:1]) & (code >= qmeta[rows, 1:2])
            scores = jnp.where(usable, scores * SCORE, NEGATIVE)
            most = jnp.maximum(jnp.max(scores, axis=1, keepdims=True), FLOOR)
            most = most.astype(BF16).astype(F32)
            weight = jnp.exp2(scores - most)
            mass = jnp.sum(weight, axis=1, keepdims=True)
            mixed = jnp.dot(weight.astype(BF16), vall[:, cols], preferred_element_type=F32)
            obuf[two, :, cols] = mixed.astype(BF16).reshape(2, GRP, HEAD_DIM)
            high = mass.astype(BF16).astype(F32)
            marks = jnp.where(lane == h, most, marks)
            marks = jnp.where(lane == h + HEADS, high, marks)
            return jnp.where(lane == h + 2 * HEADS, mass - high, marks)

        marks = lax.fori_loop(0, HEADS, head, jnp.zeros((128, HEAD_DIM), F32))
        obuf[two, :, PART:] = marks.astype(BF16).reshape(2, GRP, HEAD_DIM)

    for turn_at, shift in enumerate((2, 1, 3)):
        part = lax.rem(lax.div(z, 2) + shift, NZ // 2)
        attend(part)
        offset = lax.rem(2 * part + NZ - z, NZ)
        oex(offset).start()
        oex(lax.rem(offset + 1, NZ)).start()
        if turn_at > 0:
            ffn_w.step_near(turn_at)
    attend(lax.div(z, 2))
    beside = lax.rem(NZ + 1 - 2 * lax.rem(z, 2), NZ)
    oex(beside).start()
    orecv[pl.ds(z, 1)] = obuf[pl.ds(z, 1)]
    out_w.arrive()
    ffn_w.step_near(3)
    each(1, NZ, lambda k: oex_in(k).wait_recv())

    def marks_of(p):
        return orecv[p, :, PART:].astype(F32)

    peak = marks_of(0)
    for p in range(1, NZ):
        peak = jnp.maximum(peak, marks_of(p))
    mass = jnp.zeros((GRP, HEAD_DIM), F32)
    for p in range(NZ):
        marks = marks_of(p)
        amount = pltpu.roll(marks, HEAD_DIM - HEADS, 1) + pltpu.roll(
            marks, HEAD_DIM - 2 * HEADS, 1
        )
        mass += jnp.exp2(marks - peak) * amount
    valid = lanes(GRP) < HEADS
    inverse = 1.0 / jnp.where(valid, mass, 1.0)
    heads = [jnp.zeros((GRP, HEAD_DIM), F32) for _ in range(HEADS)]
    for p in range(NZ):
        share = jnp.exp2(marks_of(p) - peak) * inverse
        for h in range(HEADS):
            part = orecv[p, :, h * HEAD_DIM : (h + 1) * HEAD_DIM].astype(F32)
            heads[h] += part * share[:, h : h + 1]
    attn = jnp.concatenate(heads, axis=1).astype(BF16)

    def out_block(c):
        got = jnp.dot(attn, wobuf[c].reshape(PART, 256), preferred_element_type=F32)
        cols = pl.ds(pl.multiple_of(c * 256, 256), 256)
        ysend[:, :, cols] = got.astype(BF16).reshape(NX, OWN, 256)

    each(0, NDP, out_block)
    each(1, NX, lambda k: yx(k).start())
    yrecv[pl.ds(x, 1)] = ysend[pl.ds(x, 1)]
    each(1, NX, lambda k: yx_in(k).wait_recv())
    y = yrecv[0].astype(F32)
    for p in range(1, NX):
        y += yrecv[p].astype(F32)
    y = y * lax.rsqrt(jnp.mean(y * y, axis=1, keepdims=True) + EPSILON) * gains[2:3, :]
    following = (hid[z].astype(F32) + y).astype(BF16)
    hn[...] = following
    each(1, NZ, lambda k: nz(k).start())
    hbuf[pl.ds(z, 1)] = following[None]
    each(0, NX, ffn_w.step_far)

    each(1, NZ, lambda k: nz_in(k).wait_recv())
    ffn_w.arrive()

    def gate(c):
        rows = hbuf[...].reshape(NZ * OWN, D)
        g = jnp.dot(rows, wbuf[:, c, 0].reshape(D, 256), preferred_element_type=F32)
        u = jnp.dot(rows, wbuf[:, c, 1].reshape(D, 256), preferred_element_type=F32)
        cols = pl.ds(pl.multiple_of(c * 256, 256), 256)
        act[:, cols] = (jax.nn.silu(g) * u).astype(BF16)

    each(0, NX, gate)

    def down_half(half):
        def down(c):
            weights = wbuf[half * 4 + c, :, 2].reshape(NX * 256, 256)
            got = jnp.dot(act[...], weights, preferred_element_type=F32)
            cols = pl.ds(pl.multiple_of(c * 256, 256), 256)
            dsend[half, :, :, cols] = got.astype(BF16).reshape(NZ, OWN, 256)

        each(0, 4, down)
        each(1, NZ, lambda k: dz(half, k).start())

    each(0, 2, down_half)
    for half in range(2):
        drecv[half, pl.ds(z, 1)] = dsend[half, pl.ds(z, 1)]

    each(1, NX, lambda k: fx_in(k).wait_recv())
    for p in range(NX):
        fresh[:, p * PART : (p + 1) * PART] = frecv[p]

    each(0, 2, lambda half: each(1, NZ, lambda k: dz_in(half, k).wait_recv()))
    halves = []
    for half in range(2):
        t = drecv[half, 0].astype(F32)
        for p in range(1, NZ):
            t += drecv[half, p].astype(F32)
        halves.append(t)
    t = jnp.concatenate(halves, axis=1)
    t = t * lax.rsqrt(jnp.mean(t * t, axis=1, keepdims=True) + EPSILON) * gains[3:4, :]
    out[...] = (hn[...].astype(F32) + t).astype(BF16)

    for copy in (hz, qz, cz, oex, nz):
        each(1, NZ, lambda k, copy=copy: copy(k).wait_send())
    for copy in (kx, vx, px, stx, fx, yx):
        each(1, NX, lambda k, copy=copy: copy(k).wait_send())
    each(0, 2, lambda half: each(1, NZ, lambda k: dz(half, k).wait_send()))
    for weights in (qkv_w, out_w, ffn_w):
        weights.finish()


def frequencies(index_float):
    return jnp.exp(index_float * (-2.0 * math.log(THETA) / HEAD_DIM))


def tables(position):
    half = jnp.arange(HEAD_DIM // 2, dtype=jnp.int32).astype(F32)
    angles = position.astype(F32)[:, None] * frequencies(half)[None, :]
    cosine, sine = jnp.cos(angles), jnp.sin(angles)
    return jnp.concatenate([cosine, cosine], axis=1), jnp.concatenate([-sine, sine], axis=1)


def layer(
    hidden_sel, picked, order, lengths, offsets, cache_keys, cache_values, w_qkv, w_out,
    w_gate_up, w_down, gains,
):
    order_row, length_row, offset_row = order[0], lengths[0], offsets[0]
    ends = jnp.cumsum(length_row)
    request = jnp.sum((order_row[:, None] >= ends[None, :]).astype(jnp.int32), axis=1)
    mine = request[:, None] == jnp.arange(REQS, dtype=jnp.int32)[None, :]
    start = jnp.sum(jnp.where(mine, (ends - length_row)[None, :], 0), axis=1)
    shift = jnp.sum(jnp.where(mine, offset_row[None, :], 0), axis=1)
    base = shift + (order_row - start) * CH
    code = request * SPAN + base
    scos, ssin = tables(jnp.pad(base, (0, 16 - NCH)))
    rows = picked[0].reshape(NX, NZ, OWN).transpose(1, 0, 2).reshape(SEL)
    chosen = (rows // CH)[:, None] == jnp.arange(NCH, dtype=jnp.int32)[None, :]
    in_span = rows % CH
    q_code = jnp.sum(jnp.where(chosen, code[None, :], 0), axis=1) + in_span
    q_low = (q_code // SPAN) * SPAN
    qcos, qsin = tables(q_code - q_low)
    qmeta = jnp.stack([q_code, q_low, rows, rows], axis=1)
    fcode = jnp.pad(q_code.reshape(NZ, GRP), ((0, 0), (0, HEAD_DIM - GRP)), constant_values=DEAD)
    w4 = jnp.concatenate([w_qkv[1], w_qkv[2], w_qkv[0], w_qkv[0]], axis=1)
    wm = jnp.concatenate([w_gate_up, w_down[None]], axis=0)

    vmem = pl.BlockSpec(memory_space=pltpu.VMEM)
    far = pl.BlockSpec(memory_space=pl.ANY)
    smem = pl.BlockSpec(memory_space=pltpu.SMEM)
    dma = pltpu.SemaphoreType.DMA

    def spread(peers, slots):
        return (
            dma((peers,)), dma((peers,)), dma((slots, NY)), dma((slots, NY)), dma((slots,)),
            dma((slots, NY)), dma((slots, NY)),
        )

    out, fresh = pl.pallas_call(
        kernel,
        out_shape=(
            jax.ShapeDtypeStruct((OWN, D), BF16),
            jax.ShapeDtypeStruct((OWN, D), BF16),
        ),
        in_specs=[vmem, far, far, far, far, far, vmem, vmem, vmem, vmem, vmem, vmem, vmem, smem],
        out_specs=(vmem, vmem),
        scratch_shapes=[
            pltpu.VMEM((NZ, OWN, D), BF16),
            pltpu.VMEM((NDP, NX, 256, 256), BF16),
            pltpu.VMEM((NDP, NZ, 64, 256), BF16),
            pltpu.VMEM((NDP, NX, 3, 256, 256), BF16),
            pltpu.VMEM((NX, CTX, PART), BF16),
            pltpu.VMEM((KEYS, PART), BF16),
            pltpu.VMEM((KEYS, PART), BF16),
            pltpu.VMEM((1, KEYS), jnp.int32),
            pltpu.VMEM((NX, NZ * OWN, 256), BF16),
            pltpu.VMEM((NX, NZ * OWN, 256), BF16),
            pltpu.VMEM((SEL // 2, HEAD_DIM), BF16),
            pltpu.VMEM((NZ, GRP, HEAD_DIM), BF16),
            pltpu.VMEM((NZ, SEL // 2, HEAD_DIM), BF16),
            pltpu.VMEM((NZ, GRP, HEAD_DIM), BF16),
            pltpu.VMEM((SEL + 128, HEAD_DIM), F32),
            pltpu.VMEM((NX, 8, SEL + 128), F32),
            pltpu.VMEM((HEADS, SEL, HEAD_DIM), BF16),
            pltpu.VMEM((NX, OWN, PART), BF16),
            pltpu.VMEM((NX, OWN, PART), BF16),
            pltpu.VMEM((NZ, GRP, PART + HEAD_DIM), BF16),
            pltpu.VMEM((NZ, GRP, PART + HEAD_DIM), BF16),
            pltpu.VMEM((NX, OWN, D), BF16),
            pltpu.VMEM((NX, OWN, D), BF16),
            pltpu.VMEM((OWN, D), BF16),
            pltpu.VMEM((NZ, OWN, D), BF16),
            pltpu.VMEM((NZ * OWN, NX * 256), BF16),
            pltpu.VMEM((2, NZ, OWN, D // 2), BF16),
            pltpu.VMEM((2, NZ, OWN, D // 2), BF16),
            dma((NZ,)), dma((NZ,)),
            spread(NX, NX),
            spread(NZ, 2),
            spread(NX, NX),
            dma((NX,)), dma((NX,)),
            dma((NX,)), dma((NX,)),
            dma((NX,)), dma((NX,)),
            dma((NZ,)), dma((NZ,)),
            dma((NZ,)), dma((NZ,)),
            dma((NX,)), dma((NX,)),
            dma((NX,)), dma((NX,)),
            dma((NZ,)), dma((NZ,)),
            dma((NX,)), dma((NX,)),
            dma((NZ,)), dma((NZ,)),
            dma((2, NZ)), dma((2, NZ)),
            dma((6,)),
        ],
        compiler_params=pltpu.CompilerParams(
            collective_id=0, has_side_effects=True, vmem_limit_bytes=56 << 20
        ),
    )(
        hidden_sel[0], cache_keys[0], cache_values[0], w4, w_out, wm, gains, qmeta, fcode,
        qcos, qsin, scos, ssin, code,
    )
    return (out[None], fresh[None])


def solution(mesh):
    placed = (
        P("dp", "tensor", None),
        P("dp", None),
        P("dp", None),
        P("dp", None),
        P("dp", None),
        P("dp", "tensor", None),
        P("dp", "tensor", None),
        P(None, "dp", "tensor"),
        P("tensor", "dp"),
        P(None, "dp", "tensor"),
        P("tensor", "dp"),
        P(),
    )
    return jax.shard_map(
        layer,
        mesh=mesh,
        in_specs=placed,
        out_specs=(P("dp", "tensor", None), P("dp", "tensor", None)),
        check_vma=False,
    )
```

```python
import math

import jax
import jax.numpy as jnp
import numpy as np
from jax import lax
from jax.experimental import pallas as pl
from jax.experimental.pallas import tpu as pltpu
from jax.sharding import PartitionSpec as P

HEAD_DIM = 128
CH = 1024
NCH = 12
REQS = 3
NX = 4
NZ = 8
NDP = 8
NY = 4
D = 2048
PART = D // NX
HEADS = PART // HEAD_DIM
OWN = 16
GRP = NX * OWN
SEL = NZ * GRP
CTX = 384
CACHED = NX * CTX
KEYS = CACHED + 128
SPAN = 1 << 14
DEAD = 1 << 30

THETA = 500000.0
EPSILON = 1e-06
NEGATIVE = -1e30
FLOOR = -1e20
SCORE = HEAD_DIM ** (-0.5) * math.log2(math.e)
LAP_A = 6.28125
LAP_B = 0.0019340515136718750
LAP_C = 2.0 * math.pi - LAP_A - LAP_B
MESH = pl.DeviceIdType.MESH
F32, BF16 = jnp.float32, jnp.bfloat16
HIGH = lax.Precision.HIGHEST


def lanes(rows):
    return lax.broadcasted_iota(jnp.int32, (rows, HEAD_DIM), 1)


def kernel(
    hidden,
    keys,
    values,
    w4,
    wo,
    wgu,
    wd,
    gains,
    picked,
    rates,
    order,
    lengths,
    offsets,
    out,
    fresh,
    hid,
    w4buf,
    wobuf,
    wbuf,
    kraw,
    kall,
    vall,
    kcode,
    psend,
    precv,
    qpk,
    kvs,
    qrecv,
    kvrecv,
    sq,
    stat,
    qh,
    kf,
    frecv,
    obuf,
    orecv,
    ysend,
    yrecv,
    hn,
    hbuf,
    act,
    dsend,
    drecv,
    natural,
    rows_of,
    codes,
    lows,
    qcos,
    qsin,
    scos,
    ssin,
    sbase,
    bias,
    hz_s,
    hz_r,
    w4_sems,
    wo_sems,
    wm_sems,
    k_s,
    k_r,
    v_s,
    v_r,
    p_s,
    p_r,
    q_s,
    q_r,
    c_s,
    c_r,
    st_s,
    st_r,
    f_s,
    f_r,
    o_s,
    o_r,
    y_s,
    y_r,
    n_s,
    n_r,
    d_s,
    d_r,
    loc,
):
    tens = lax.axis_index("tensor")
    dp = lax.axis_index("dp")
    x = lax.div(tens, NZ)
    z = lax.rem(tens, NZ)
    core = lax.rem(dp, 2)
    sib = dp + 1 - 2 * core

    def xa(k):
        return lax.rem(x + k, NX)

    def za(k):
        return lax.rem(z + k, NZ)

    def da(k):
        return lax.rem(dp + k, NDP)

    def zdev(k):
        return {"tensor": x * NZ + za(k)}

    def xdev(k):
        return {"tensor": xa(k) * NZ + z}

    def send(src, dst, ssem, rsem, dev):
        return pltpu.make_async_remote_copy(
            src_ref=src, dst_ref=dst, send_sem=ssem, recv_sem=rsem, device_id=dev,
            device_id_type=MESH,
        )

    def each(first, last, body):
        def step(k, carry):
            body(k)
            return carry

        lax.fori_loop(first, last, step, 0)

    class Spread:
        def __init__(self, sems, slots, source, first, peers, entry, entry_in, at):
            (self.e_s, self.e_r, self.n_s, self.y_r, self.r_s, self.s_s, self.s_r) = sems
            self.slots, self.source, self.first, self.peers = slots, source, first, peers
            self.entry, self.entry_in, self.at = entry, entry_in, at

        def enter(self, k):
            return send(self.source, self.entry, self.e_s.at[k], self.e_r.at[k], self.first(k))

        def enter_in(self, k):
            at = self.entry_in(k)
            return send(at, at, self.e_s.at[k], self.e_r.at[k], self.first(k))

        def near(self, k, j):
            at = self.at(dp, k)
            return send(at, at, self.n_s.at[k, j], self.y_r.at[k, j], {"dp": da(2 * j)})

        def near_in(self, k, j):
            at = self.at(da(NDP - 2 * j), k)
            return send(at, at, self.n_s.at[k, j], self.y_r.at[k, j], {"dp": da(2 * j)})

        def way(self, k):
            return 1 + 2 * lax.div(k, self.slots // 2)

        def relay(self, k):
            j = self.way(k)
            at = self.at(da(NDP - 2 * j), k)
            return send(at, at, self.r_s.at[k], self.y_r.at[k, 2], {"dp": da(2 * j)})

        def relay_in(self, k):
            at = self.at(da(4), k)
            return send(at, at, self.r_s.at[k], self.y_r.at[k, 2], {"dp": da(2)})

        def side(self, k, j):
            at = self.at(da(NDP - 2 * j), k)
            return send(at, at, self.s_s.at[k, j], self.s_r.at[k, j], {"dp": sib})

        def side_in(self, k, j):
            at = self.at(lax.rem(sib + NDP - 2 * j, NDP), k)
            return send(at, at, self.s_s.at[k, j], self.s_r.at[k, j], {"dp": sib})

        def start(self):
            each(1, self.peers, lambda k: self.enter(k).start())

        def go_near(self, k):
            self.near(k, 1).start()
            self.near(k, 3).start()
            self.side(k, 0).start()

        def step_near(self, k):
            self.near_in(k, 1).wait_recv()
            self.near_in(k, 3).wait_recv()
            self.relay(k).start()
            self.side(k, 1).start()
            self.side(k, 3).start()

        def step_far(self, k):
            self.relay_in(k).wait_recv()
            self.side(k, 2).start()

        def arrive(self):
            each(0, self.slots, lambda k: each(0, NY, lambda j: self.side_in(k, j).wait_recv()))

        def finish(self):
            each(1, self.peers, lambda k: self.enter(k).wait_send())

            def one(k):
                self.near(k, 1).wait_send()
                self.near(k, 3).wait_send()
                self.relay(k).wait_send()
                each(0, NY, lambda j: self.side(k, j).wait_send())

            each(0, self.slots, one)

    def x_slot(buf):
        return lambda d, k: buf.at[d, xa(NX - k)]

    qkv_w = Spread(
        w4_sems, NX, w4, xdev, NX, w4buf.at[dp, x], lambda k: w4buf.at[dp, xa(NX - k)],
        x_slot(w4buf),
    )
    ffn_w = Spread(
        wm_sems, NX, wbuf.at[dp, x], xdev, NX, wbuf.at[dp, x], lambda k: wbuf.at[dp, xa(NX - k)],
        x_slot(wbuf),
    )
    out_w = Spread(
        wo_sems, 2, wo, zdev, NZ, wobuf.at[dp, z], lambda k: wobuf.at[dp, za(NZ - k)],
        lambda d, k: wobuf.at[d, pl.ds(4 * k, 4)],
    )

    def hz(k):
        return send(hidden, hid.at[z], hz_s.at[k], hz_r.at[k], zdev(k))

    def hz_in(k):
        at = hid.at[za(NZ - k)]
        return send(at, at, hz_s.at[k], hz_r.at[k], zdev(k))

    def columns(at):
        return pl.ds(pl.multiple_of(at * PART, PART), PART)

    def key_rows(at):
        return pl.ds(pl.multiple_of(at * CTX, 128), CTX)

    def kx(k):
        return send(keys.at[:, columns(xa(k))], kraw.at[x], k_s.at[k], k_r.at[k], xdev(k))

    def kx_in(k):
        at = kraw.at[xa(NX - k)]
        return send(at, at, k_s.at[k], k_r.at[k], xdev(k))

    def vx(k):
        return send(
            values.at[:, columns(xa(k))], vall.at[key_rows(x)], v_s.at[k], v_r.at[k], xdev(k)
        )

    def vx_in(k):
        at = vall.at[key_rows(xa(NX - k))]
        return send(at, at, v_s.at[k], v_r.at[k], xdev(k))

    def px(k):
        return send(psend.at[xa(k)], precv.at[x], p_s.at[k], p_r.at[k], xdev(k))

    def px_in(k):
        at = precv.at[xa(NX - k)]
        return send(at, at, p_s.at[k], p_r.at[k], xdev(k))

    def qz(k):
        return send(qpk, qrecv.at[z], q_s.at[k], q_r.at[k], zdev(k))

    def qz_in(k):
        at = qrecv.at[za(NZ - k)]
        return send(at, at, q_s.at[k], q_r.at[k], zdev(k))

    def cz(k):
        return send(kvs.at[za(k)], kvrecv.at[z], c_s.at[k], c_r.at[k], zdev(k))

    def cz_in(k):
        at = kvrecv.at[za(NZ - k)]
        return send(at, at, c_s.at[k], c_r.at[k], zdev(k))

    def stx(k):
        return send(stat.at[x], stat.at[x], st_s.at[k], st_r.at[k], xdev(k))

    def stx_in(k):
        at = stat.at[xa(NX - k)]
        return send(at, at, st_s.at[k], st_r.at[k], xdev(k))

    def fx(k):
        return send(kf.at[xa(k)], frecv.at[x], f_s.at[k], f_r.at[k], xdev(k))

    def fx_in(k):
        at = frecv.at[xa(NX - k)]
        return send(at, at, f_s.at[k], f_r.at[k], xdev(k))

    def oex(k):
        return send(obuf.at[za(k)], orecv.at[z], o_s.at[k], o_r.at[k], zdev(k))

    def oex_in(k):
        at = orecv.at[za(NZ - k)]
        return send(at, at, o_s.at[k], o_r.at[k], zdev(k))

    def yx(k):
        return send(ysend.at[xa(k)], yrecv.at[x], y_s.at[k], y_r.at[k], xdev(k))

    def yx_in(k):
        at = yrecv.at[xa(NX - k)]
        return send(at, at, y_s.at[k], y_r.at[k], xdev(k))

    def nz(k):
        return send(hn, hbuf.at[z], n_s.at[k], n_r.at[k], zdev(k))

    def nz_in(k):
        at = hbuf.at[za(NZ - k)]
        return send(at, at, n_s.at[k], n_r.at[k], zdev(k))

    def dz(half, k):
        return send(
            dsend.at[half, za(k)], drecv.at[half, z], d_s.at[half, k], d_r.at[half, k], zdev(k)
        )

    def dz_in(half, k):
        at = drecv.at[half, za(NZ - k)]
        return send(at, at, d_s.at[half, k], d_r.at[half, k], zdev(k))

    own_copies = [
        pltpu.make_async_copy(hidden, hid.at[z], loc.at[0]),
        pltpu.make_async_copy(w4, w4buf.at[dp, x], loc.at[1]),
        pltpu.make_async_copy(wo, wobuf.at[dp, z], loc.at[2]),
        pltpu.make_async_copy(wgu, wbuf.at[dp, x, pl.ds(0, 2)], loc.at[3]),
        pltpu.make_async_copy(keys.at[:, columns(x)], kraw.at[x], loc.at[4]),
        pltpu.make_async_copy(values.at[:, columns(x)], vall.at[key_rows(x)], loc.at[5]),
        pltpu.make_async_copy(wd, wbuf.at[dp, x, 2], loc.at[6]),
    ]
    for copy in own_copies:
        copy.start()

    barrier = pltpu.get_barrier_semaphore()

    def greet(dev):
        pl.semaphore_signal(barrier, inc=1, device_id=dev, device_id_type=MESH)

    each(1, NZ, lambda k: greet(zdev(k)))
    each(1, NX, lambda k: greet(xdev(k)))
    greet({"dp": da(2)})
    greet({"dp": da(6)})
    greet({"dp": sib})
    pl.semaphore_wait(barrier, NZ + NX + 1)

    qkv_w.start()
    own_copies[1].wait()
    qkv_w.go_near(0)
    each(1, NZ, lambda k: hz(k).start())
    own_copies[3].wait()
    own_copies[6].wait()
    ffn_w.enter(1).start()
    ffn_w.enter(3).start()
    each(1, NX, lambda k: kx(k).start())
    out_w.start()

    end_a = lengths[0, 0]
    end_b = end_a + lengths[0, 1]
    span = lax.broadcasted_iota(jnp.int32, (16, HEAD_DIM), 0)
    turns = jnp.zeros((16, HEAD_DIM), jnp.int32)
    shifts, bottoms = [], []
    for slot in range(NCH):
        place = order[0, slot]
        second, third = place >= end_a, place >= end_b
        start = jnp.where(third, end_b, jnp.where(second, end_a, 0))
        moved = jnp.where(third, offsets[0, 2], jnp.where(second, offsets[0, 1], offsets[0, 0]))
        bottom = jnp.where(third, 2 * SPAN, jnp.where(second, SPAN, 0))
        base = moved + (place - start) * CH
        sbase[slot] = base + bottom - slot * CH
        shifts.append(base + bottom - slot * CH)
        bottoms.append(bottom)
        turns = jnp.where(span == slot, base, turns)

    def circle(position):
        angle = position.astype(F32) * rates[0:1, :]
        laps = jnp.floor(angle * (0.5 / math.pi) + 0.5)
        angle = ((angle - laps * LAP_A) - laps * LAP_B) - laps * LAP_C
        sine = jnp.sin(angle)
        left = lax.broadcasted_iota(jnp.int32, position.shape, 1) < HEAD_DIM // 2
        return jnp.cos(angle), jnp.where(left, -sine, sine)

    scos[...], ssin[...] = circle(turns)

    def qkv_on(k):
        qkv_w.enter_in(k).wait_recv()
        qkv_w.go_near(k)

    each(1, NX, qkv_on)

    natural[...] = lax.dot_general(
        jnp.broadcast_to(picked[...].astype(F32), (8, SEL)),
        jnp.full((8, HEAD_DIM), 0.125, F32), (((0,), (0,)), ((), ())),
        precision=HIGH, preferred_element_type=F32,
    )
    for zz in range(NZ):
        for xx in range(NX):
            at = (zz * NX + xx) * OWN
            back = (xx * NZ + zz) * OWN
            rows_of[at : at + OWN] = natural[back : back + OWN].astype(jnp.int32)

    def tokens(i):
        rows = pl.ds(pl.multiple_of(i * 128, 128), 128)
        row = rows_of[rows]
        slot_of = lax.shift_right_logical(row, 10)
        shift = jnp.zeros_like(row)
        bottom = jnp.zeros_like(row)
        for slot in range(NCH):
            mine = slot_of == slot
            shift = jnp.where(mine, shifts[slot], shift)
            bottom = jnp.where(mine, bottoms[slot], bottom)
        codes[rows] = row + shift
        lows[rows] = bottom
        qcos[rows], qsin[rows] = circle(row + shift - bottom)

    each(0, SEL // 128, tokens)
    grp_rows = pl.ds(pl.multiple_of(z * GRP, GRP), GRP)

    for block in range(NX):
        first = (block * NZ + z) * CTX
        slot = lax.div(first, CH)
        later = lax.min(slot + 1, NCH - 1)
        row = first + lax.broadcasted_iota(jnp.int32, (1, CTX), 1)
        code = jnp.where(row < (slot + 1) * CH, sbase[slot], sbase[later]) + row
        hit = jnp.max(
            jnp.where(rows_of[:, 0:1] == row, 1, 0), axis=0, keepdims=True
        )
        kcode[:, block * CTX : (block + 1) * CTX] = jnp.where(hit > 0, DEAD, code)
    corner = lax.broadcasted_iota(jnp.int32, (GRP, HEAD_DIM), 0) == lanes(GRP)
    kcode[:, CACHED:KEYS] = jnp.where(
        lanes(1) < GRP,
        jnp.sum(jnp.where(corner, codes[grp_rows], 0), axis=0, keepdims=True),
        DEAD,
    )
    kall[CACHED:KEYS, :] = jnp.zeros((KEYS - CACHED, PART), BF16)
    vall[CACHED:KEYS, :] = jnp.zeros((KEYS - CACHED, PART), BF16)

    each(0, NX, qkv_w.step_near)
    own_copies[2].wait()
    each(1, NZ, lambda k: out_w.enter_in(k).wait_recv())
    each(0, NX, qkv_w.step_far)
    each(0, 2, out_w.go_near)
    ffn_w.go_near(0)

    own_copies[0].wait()
    each(1, NZ, lambda k: hz_in(k).wait_recv())
    qkv_w.arrive()

    def project(i):
        k = lax.rem(i + 1, NX)
        at = xa(k)
        rows = hid[...].reshape(NZ * OWN, D)
        got = jnp.dot(rows, w4buf[:, at].reshape(D, 256), preferred_element_type=F32)
        psend[at] = got.astype(BF16)
        return k

    def project_send(i):
        k = project(i)
        px(k).start()

    each(0, NX - 1, project_send)
    project(NX - 1)
    precv[pl.ds(x, 1)] = psend[pl.ds(x, 1)]

    each(1, NX, lambda k: vx(k).start())
    ffn_w.enter(2).start()
    for k in (1, 3):
        ffn_w.enter_in(k).wait_recv()
        ffn_w.go_near(k)
    each(1, NX, lambda k: px_in(k).wait_recv())
    low = lanes(SEL // 2) < HEAD_DIM // 2
    for g in range(NZ // 2):
        two = []
        for gg in (g, g + NZ // 2):
            rows = jnp.concatenate(
                [precv[p, gg * OWN : (gg + 1) * OWN] for p in range(NX)], axis=0
            )
            kvs[gg] = rows[:, :HEAD_DIM]
            two.append(rows[:, HEAD_DIM:].astype(F32))
        qpk[g * GRP : (g + 1) * GRP, :] = jnp.where(low[:GRP], two[0], two[1]).astype(BF16)
    each(1, NZ, lambda k: qz(k).start())
    each(1, NZ, lambda k: cz(k).start())
    qrecv[pl.ds(z, 1)] = qpk[...][None]
    kvrecv[pl.ds(z, 1)] = kvs[pl.ds(z, 1)]
    each(0, 2, out_w.step_near)

    each(1, NZ, lambda k: qz_in(k).wait_recv())
    each(1, NZ, lambda k: cz_in(k).wait_recv())
    low_f = lanes(GRP) < HEAD_DIM // 2

    def q_head(h):
        a = qrecv[2 * h].astype(F32)
        b = qrecv[2 * h + 1].astype(F32)
        top = jnp.where(low, a, pltpu.roll(b, 64, 1))
        bottom = jnp.where(low, pltpu.roll(a, 64, 1), b)
        return top, bottom

    def f_head(h):
        a = kvrecv[2 * h].astype(F32)
        b = kvrecv[2 * h + 1].astype(F32)
        return jnp.where(low_f, a, pltpu.roll(b, 64, 1)), jnp.where(low_f, pltpu.roll(a, 64, 1), b)

    sq[...] = jnp.zeros_like(sq)
    for h in range(HEADS):
        top, bottom = q_head(h)
        sq[: SEL // 2] += top * top
        sq[SEL // 2 : SEL] += bottom * bottom
        key, value = f_head(h)
        sq[SEL : SEL + GRP] += key * key
        vall[CACHED : CACHED + GRP, h * HEAD_DIM : (h + 1) * HEAD_DIM] = value.astype(BF16)
    stat[pl.ds(x, 1)] = lax.dot_general(
        jnp.ones((8, HEAD_DIM), F32), sq[...], (((1,), (1,)), ((), ())),
        precision=HIGH, preferred_element_type=F32,
    )[None]
    each(1, NX, lambda k: stx(k).start())
    each(0, 2, out_w.step_far)
    each(1, NX, lambda k: stx_in(k).wait_recv())
    total = stat[0] + stat[1] + stat[2] + stat[3]
    factor = lax.rsqrt(total * (1.0 / D) + EPSILON)
    sq[...] = lax.dot_general(
        factor, jnp.full((8, HEAD_DIM), 0.125, F32), (((0,), (0,)), ((), ())),
        precision=HIGH, preferred_element_type=F32,
    )
    for h in range(HEADS):
        cols = pl.ds(pl.multiple_of(x * PART + h * HEAD_DIM, HEAD_DIM), HEAD_DIM)
        top, bottom = q_head(h)
        gain = gains[0:1, cols]
        for part, rows in ((top, slice(0, SEL // 2)), (bottom, slice(SEL // 2, SEL))):
            v = part * (sq[rows] * SCORE) * gain
            qh[h, rows] = (v * qcos[rows] + pltpu.roll(v, 64, 1) * qsin[rows]).astype(BF16)
        key, _ = f_head(h)
        v = key * sq[SEL : SEL + GRP] * gains[1:2, cols]
        v = (v * qcos[grp_rows] + pltpu.roll(v, 64, 1) * qsin[grp_rows]).astype(BF16)
        kall[CACHED : CACHED + GRP, h * HEAD_DIM : (h + 1) * HEAD_DIM] = v
        kf[:, :, h * HEAD_DIM : (h + 1) * HEAD_DIM] = v.reshape(NX, OWN, HEAD_DIM)
    each(1, NX, lambda k: fx(k).start())
    frecv[pl.ds(x, 1)] = kf[pl.ds(x, 1)]

    own_copies[4].wait()
    each(1, NX, lambda k: kx_in(k).wait_recv())

    def turn(block):
        first = (block * NZ + z) * CTX
        slot = lax.div(first, CH)
        later = lax.min(slot + 1, NCH - 1)
        row = first + lax.broadcasted_iota(jnp.int32, (CTX, HEAD_DIM), 0)
        here = row < (slot + 1) * CH
        cosine = jnp.where(here, scos[pl.ds(slot, 1), :], scos[pl.ds(later, 1), :])
        sine = jnp.where(here, ssin[pl.ds(slot, 1), :], ssin[pl.ds(later, 1), :])
        for h in range(HEADS):
            cols = slice(h * HEAD_DIM, (h + 1) * HEAD_DIM)
            v = kraw[block, :, cols].astype(F32)
            kall[key_rows(block), cols] = (v * cosine + pltpu.roll(v, 64, 1) * sine).astype(BF16)

    each(0, NX, turn)
    own_copies[5].wait()
    each(1, NX, lambda k: vx_in(k).wait_recv())

    lane = lanes(128)

    def attend(part):
        rows = pl.ds(pl.multiple_of(part * 128, 128), 128)
        two = pl.ds(part * 2, 2)
        code = kcode[...]
        usable = (code <= codes[rows, 0:1]) & (code >= lows[rows, 0:1])
        bias[...] = jnp.where(usable, 0.0, NEGATIVE)
        marks = jnp.zeros((128, HEAD_DIM), F32)
        for h in range(HEADS):
            cols = slice(h * HEAD_DIM, (h + 1) * HEAD_DIM)
            scores = lax.dot_general(
                qh[h, rows], kall[:, cols], (((1,), (1,)), ((), ())), preferred_element_type=F32
            ) + bias[...]
            most = jnp.maximum(jnp.max(scores, axis=1, keepdims=True), FLOOR)
            most = most.astype(BF16).astype(F32)
            weight = jnp.exp2(scores - most)
            mass = jnp.sum(weight, axis=1, keepdims=True)
            mixed = jnp.dot(weight.astype(BF16), vall[:, cols], preferred_element_type=F32)
            obuf[two, :, cols] = mixed.astype(BF16).reshape(2, GRP, HEAD_DIM)
            high = mass.astype(BF16).astype(F32)
            marks = jnp.where(lane == h, most, marks)
            marks = jnp.where(lane == h + HEADS, high, marks)
            marks = jnp.where(lane == h + 2 * HEADS, mass - high, marks)
        obuf[two, :, PART:] = marks.astype(BF16).reshape(2, GRP, HEAD_DIM)

    def attend_far(i):
        part = lax.rem(lax.div(z, 2) + 1 + lax.rem(i + 1, 3), NZ // 2)
        attend(part)
        offset = lax.rem(2 * part + NZ - z, NZ)
        oex(offset).start()
        oex(lax.rem(offset + 1, NZ)).start()
        ffn_w.step_near(i + lax.div(i, 2))

    each(0, 3, attend_far)
    attend(lax.div(z, 2))
    beside = lax.rem(NZ + 1 - 2 * lax.rem(z, 2), NZ)
    oex(beside).start()
    orecv[pl.ds(z, 1)] = obuf[pl.ds(z, 1)]
    ffn_w.enter_in(2).wait_recv()
    ffn_w.go_near(2)
    out_w.arrive()
    each(1, NZ, lambda k: oex_in(k).wait_recv())

    def marks_of(p):
        return orecv[p, :, PART:].astype(F32)

    peak = marks_of(0)
    for p in range(1, NZ):
        peak = jnp.maximum(peak, marks_of(p))
    mass = jnp.zeros((GRP, HEAD_DIM), F32)
    for p in range(NZ):
        marks = marks_of(p)
        amount = pltpu.roll(marks, HEAD_DIM - HEADS, 1) + pltpu.roll(
            marks, HEAD_DIM - 2 * HEADS, 1
        )
        mass += jnp.exp2(marks - peak) * amount
    valid = lanes(GRP) < HEADS
    inverse = 1.0 / jnp.where(valid, mass, 1.0)
    heads = [jnp.zeros((GRP, HEAD_DIM), F32) for _ in range(HEADS)]
    for p in range(NZ):
        share = jnp.exp2(marks_of(p) - peak) * inverse
        for h in range(HEADS):
            part = orecv[p, :, h * HEAD_DIM : (h + 1) * HEAD_DIM].astype(F32)
            heads[h] += part * share[:, h : h + 1]
    attn = jnp.concatenate(heads, axis=1).astype(BF16)

    def out_block(c):
        got = jnp.dot(attn, wobuf[c].reshape(PART, 256), preferred_element_type=F32)
        cols = pl.ds(pl.multiple_of(c * 256, 256), 256)
        ysend[:, :, cols] = got.astype(BF16).reshape(NX, OWN, 256)

    each(0, NDP, out_block)
    each(1, NX, lambda k: yx(k).start())
    yrecv[pl.ds(x, 1)] = ysend[pl.ds(x, 1)]
    for k in (0, 1, 3):
        ffn_w.step_far(k)
    each(1, NX, lambda k: yx_in(k).wait_recv())
    y = yrecv[0].astype(F32)
    for p in range(1, NX):
        y += yrecv[p].astype(F32)
    y = y * lax.rsqrt(jnp.mean(y * y, axis=1, keepdims=True) + EPSILON) * gains[2:3, :]
    following = (hid[z].astype(F32) + y).astype(BF16)
    hn[...] = following
    each(1, NZ, lambda k: nz(k).start())
    hbuf[pl.ds(z, 1)] = following[None]
    ffn_w.step_near(2)
    ffn_w.step_far(2)

    each(1, NZ, lambda k: nz_in(k).wait_recv())
    ffn_w.arrive()

    def gate(c):
        rows = hbuf[...].reshape(NZ * OWN, D)
        g = jnp.dot(rows, wbuf[:, c, 0].reshape(D, 256), preferred_element_type=F32)
        u = jnp.dot(rows, wbuf[:, c, 1].reshape(D, 256), preferred_element_type=F32)
        cols = pl.ds(pl.multiple_of(c * 256, 256), 256)
        act[:, cols] = (jax.nn.silu(g) * u).astype(BF16)

    each(0, NX, gate)

    def down_half(half):
        def down(c):
            weights = wbuf[half * 4 + c, :, 2].reshape(NX * 256, 256)
            got = jnp.dot(act[...], weights, preferred_element_type=F32)
            cols = pl.ds(pl.multiple_of(c * 256, 256), 256)
            dsend[half, :, :, cols] = got.astype(BF16).reshape(NZ, OWN, 256)

        each(0, 4, down)
        each(1, NZ, lambda k: dz(half, k).start())

    each(0, 2, down_half)
    for half in range(2):
        drecv[half, pl.ds(z, 1)] = dsend[half, pl.ds(z, 1)]

    each(1, NX, lambda k: fx_in(k).wait_recv())
    for p in range(NX):
        fresh[:, p * PART : (p + 1) * PART] = frecv[p]

    each(0, 2, lambda half: each(1, NZ, lambda k: dz_in(half, k).wait_recv()))
    halves = []
    for half in range(2):
        t = drecv[half, 0].astype(F32)
        for p in range(1, NZ):
            t += drecv[half, p].astype(F32)
        halves.append(t)
    t = jnp.concatenate(halves, axis=1)
    t = t * lax.rsqrt(jnp.mean(t * t, axis=1, keepdims=True) + EPSILON) * gains[3:4, :]
    out[...] = (hn[...].astype(F32) + t).astype(BF16)

    for copy in (hz, qz, cz, oex, nz):
        each(1, NZ, lambda k, copy=copy: copy(k).wait_send())
    for copy in (kx, vx, px, stx, fx, yx):
        each(1, NX, lambda k, copy=copy: copy(k).wait_send())
    each(0, 2, lambda half: each(1, NZ, lambda k: dz(half, k).wait_send()))
    for weights in (qkv_w, out_w, ffn_w):
        weights.finish()


def layer(
    hidden_sel, picked, order, lengths, offsets, cache_keys, cache_values, w_qkv, w_out,
    w_gate_up, w_down, gains,
):
    w4 = jnp.concatenate([w_qkv[1], w_qkv[2], w_qkv[0], w_qkv[0]], axis=1)
    half = np.arange(HEAD_DIM // 2, dtype=np.float64)
    rate = np.exp(half * (-2.0 * math.log(THETA) / HEAD_DIM)).astype(np.float32)
    rates = jnp.asarray(np.broadcast_to(np.concatenate([rate, rate]), (8, HEAD_DIM)))

    vmem = pl.BlockSpec(memory_space=pltpu.VMEM)
    far = pl.BlockSpec(memory_space=pl.ANY)
    smem = pl.BlockSpec(memory_space=pltpu.SMEM)
    dma = pltpu.SemaphoreType.DMA

    def spread(peers, slots):
        return (
            dma((peers,)), dma((peers,)), dma((slots, NY)), dma((slots, NY)), dma((slots,)),
            dma((slots, NY)), dma((slots, NY)),
        )

    out, fresh = pl.pallas_call(
        kernel,
        out_shape=(
            jax.ShapeDtypeStruct((OWN, D), BF16),
            jax.ShapeDtypeStruct((OWN, D), BF16),
        ),
        in_specs=[vmem, far, far, far, far, far, far, vmem, vmem, vmem, smem, smem, smem],
        out_specs=(vmem, vmem),
        scratch_shapes=[
            pltpu.VMEM((NZ, OWN, D), BF16),
            pltpu.VMEM((NDP, NX, 256, 256), BF16),
            pltpu.VMEM((NDP, NZ, 64, 256), BF16),
            pltpu.VMEM((NDP, NX, 3, 256, 256), BF16),
            pltpu.VMEM((NX, CTX, PART), BF16),
            pltpu.VMEM((KEYS, PART), BF16),
            pltpu.VMEM((KEYS, PART), BF16),
            pltpu.VMEM((1, KEYS), jnp.int32),
            pltpu.VMEM((NX, NZ * OWN, 256), BF16),
            pltpu.VMEM((NX, NZ * OWN, 256), BF16),
            pltpu.VMEM((SEL // 2, HEAD_DIM), BF16),
            pltpu.VMEM((NZ, GRP, HEAD_DIM), BF16),
            pltpu.VMEM((NZ, SEL // 2, HEAD_DIM), BF16),
            pltpu.VMEM((NZ, GRP, HEAD_DIM), BF16),
            pltpu.VMEM((SEL + 128, HEAD_DIM), F32),
            pltpu.VMEM((NX, 8, SEL + 128), F32),
            pltpu.VMEM((HEADS, SEL, HEAD_DIM), BF16),
            pltpu.VMEM((NX, OWN, PART), BF16),
            pltpu.VMEM((NX, OWN, PART), BF16),
            pltpu.VMEM((NZ, GRP, PART + HEAD_DIM), BF16),
            pltpu.VMEM((NZ, GRP, PART + HEAD_DIM), BF16),
            pltpu.VMEM((NX, OWN, D), BF16),
            pltpu.VMEM((NX, OWN, D), BF16),
            pltpu.VMEM((OWN, D), BF16),
            pltpu.VMEM((NZ, OWN, D), BF16),
            pltpu.VMEM((NZ * OWN, NX * 256), BF16),
            pltpu.VMEM((2, NZ, OWN, D // 2), BF16),
            pltpu.VMEM((2, NZ, OWN, D // 2), BF16),
            pltpu.VMEM((SEL, HEAD_DIM), F32),
            pltpu.VMEM((SEL, HEAD_DIM), jnp.int32),
            pltpu.VMEM((SEL, HEAD_DIM), jnp.int32),
            pltpu.VMEM((SEL, HEAD_DIM), jnp.int32),
            pltpu.VMEM((SEL, HEAD_DIM), F32),
            pltpu.VMEM((SEL, HEAD_DIM), F32),
            pltpu.VMEM((16, HEAD_DIM), F32),
            pltpu.VMEM((16, HEAD_DIM), F32),
            pltpu.SMEM((16,), jnp.int32),
            pltpu.VMEM((128, KEYS), F32),
            dma((NZ,)), dma((NZ,)),
            spread(NX, NX),
            spread(NZ, 2),
            spread(NX, NX),
            dma((NX,)), dma((NX,)),
            dma((NX,)), dma((NX,)),
            dma((NX,)), dma((NX,)),
            dma((NZ,)), dma((NZ,)),
            dma((NZ,)), dma((NZ,)),
            dma((NX,)), dma((NX,)),
            dma((NX,)), dma((NX,)),
            dma((NZ,)), dma((NZ,)),
            dma((NX,)), dma((NX,)),
            dma((NZ,)), dma((NZ,)),
            dma((2, NZ)), dma((2, NZ)),
            dma((7,)),
        ],
        compiler_params=pltpu.CompilerParams(
            collective_id=0, has_side_effects=True, vmem_limit_bytes=56 << 20
        ),
    )(
        hidden_sel[0], cache_keys[0], cache_values[0], w4, w_out, w_gate_up, w_down, gains,
        picked, rates, order, lengths, offsets,
    )
    return (out[None], fresh[None])


def solution(mesh):
    placed = (
        P("dp", "tensor", None),
        P("dp", None),
        P("dp", None),
        P("dp", None),
        P("dp", None),
        P("dp", "tensor", None),
        P("dp", "tensor", None),
        P(None, "dp", "tensor"),
        P("tensor", "dp"),
        P(None, "dp", "tensor"),
        P("tensor", "dp"),
        P(),
    )
    return jax.shard_map(
        layer,
        mesh=mesh,
        in_specs=placed,
        out_specs=(P("dp", "tensor", None), P("dp", "tensor", None)),
        check_vma=False,
    )
```

```python
import math

import jax
import jax.numpy as jnp
import numpy as np
from jax import lax
from jax.experimental import pallas as pl
from jax.experimental.pallas import tpu as pltpu
from jax.sharding import PartitionSpec as P

HEAD_DIM = 128
CH = 1024
NCH = 12
REQS = 3
NX = 4
NZ = 8
NDP = 8
NY = 4
D = 2048
PART = D // NX
HEADS = PART // HEAD_DIM
OWN = 16
GRP = NX * OWN
SEL = NZ * GRP
CTX = 384
CACHED = NX * CTX
KEYS = CACHED + 128
SPAN = 1 << 14
DEAD = 1 << 30

THETA = 500000.0
EPSILON = 1e-06
NEGATIVE = -1e30
FLOOR = -1e20
SCORE = HEAD_DIM ** (-0.5) * math.log2(math.e)
LAP_A = 6.28125
LAP_B = 0.0019340515136718750
LAP_C = 2.0 * math.pi - LAP_A - LAP_B
RATES = [
    float(np.float32(math.exp(-2.0 * j / HEAD_DIM * math.log(THETA)))) for j in range(HEAD_DIM // 2)
]
MESH = pl.DeviceIdType.MESH
F32, BF16 = jnp.float32, jnp.bfloat16
HIGH = lax.Precision.HIGHEST


def lanes(rows):
    return lax.broadcasted_iota(jnp.int32, (rows, HEAD_DIM), 1)


def kernel(
    hidden,
    keys,
    values,
    w4,
    wo,
    wgu,
    wd,
    gains,
    picked,
    order,
    lengths,
    offsets,
    out,
    fresh,
    hid,
    w4buf,
    wobuf,
    wbuf,
    kraw,
    kall,
    vall,
    kcode,
    psend,
    precv,
    qpk,
    kvs,
    qrecv,
    kvrecv,
    sq,
    stat,
    qh,
    kf,
    frecv,
    obuf,
    orecv,
    ysend,
    yrecv,
    hn,
    hbuf,
    act,
    dsend,
    drecv,
    natural,
    rows_of,
    codes,
    lows,
    qcos,
    qsin,
    scos,
    ssin,
    sbase,
    bias,
    squares,
    hz_s,
    hz_r,
    w4_sems,
    wo_sems,
    wm_sems,
    k_s,
    k_r,
    v_s,
    v_r,
    p_s,
    p_r,
    q_s,
    q_r,
    c_s,
    c_r,
    st_s,
    st_r,
    f_s,
    f_r,
    o_s,
    o_r,
    y_s,
    y_r,
    n_s,
    n_r,
    d_s,
    d_r,
    loc,
):
    tens = lax.axis_index("tensor")
    dp = lax.axis_index("dp")
    x = lax.div(tens, NZ)
    z = lax.rem(tens, NZ)
    core = lax.rem(dp, 2)
    sib = dp + 1 - 2 * core

    def xa(k):
        return lax.rem(x + k, NX)

    def za(k):
        return lax.rem(z + k, NZ)

    def da(k):
        return lax.rem(dp + k, NDP)

    def zdev(k):
        return {"tensor": x * NZ + za(k)}

    def xdev(k):
        return {"tensor": xa(k) * NZ + z}

    def send(src, dst, ssem, rsem, dev):
        return pltpu.make_async_remote_copy(
            src_ref=src, dst_ref=dst, send_sem=ssem, recv_sem=rsem, device_id=dev,
            device_id_type=MESH,
        )

    def each(first, last, body):
        def step(k, carry):
            body(k)
            return carry

        lax.fori_loop(first, last, step, 0)

    class Spread:
        def __init__(self, sems, slots, source, first, peers, entry, entry_in, at):
            (self.e_s, self.e_r, self.n_s, self.y_r, self.r_s, self.s_s, self.s_r) = sems
            self.slots, self.source, self.first, self.peers = slots, source, first, peers
            self.entry, self.entry_in, self.at = entry, entry_in, at

        def enter(self, k):
            return send(self.source, self.entry, self.e_s.at[k], self.e_r.at[k], self.first(k))

        def enter_in(self, k):
            at = self.entry_in(k)
            return send(at, at, self.e_s.at[k], self.e_r.at[k], self.first(k))

        def near(self, k, j):
            at = self.at(dp, k)
            return send(at, at, self.n_s.at[k, j], self.y_r.at[k, j], {"dp": da(2 * j)})

        def near_in(self, k, j):
            at = self.at(da(NDP - 2 * j), k)
            return send(at, at, self.n_s.at[k, j], self.y_r.at[k, j], {"dp": da(2 * j)})

        def way(self, k):
            return 1 + 2 * lax.div(k, self.slots // 2)

        def relay(self, k):
            j = self.way(k)
            at = self.at(da(NDP - 2 * j), k)
            return send(at, at, self.r_s.at[k], self.y_r.at[k, 2], {"dp": da(2 * j)})

        def relay_in(self, k):
            at = self.at(da(4), k)
            return send(at, at, self.r_s.at[k], self.y_r.at[k, 2], {"dp": da(2)})

        def side(self, k, j):
            at = self.at(da(NDP - 2 * j), k)
            return send(at, at, self.s_s.at[k, j], self.s_r.at[k, j], {"dp": sib})

        def side_in(self, k, j):
            at = self.at(lax.rem(sib + NDP - 2 * j, NDP), k)
            return send(at, at, self.s_s.at[k, j], self.s_r.at[k, j], {"dp": sib})

        def start(self):
            each(1, self.peers, lambda k: self.enter(k).start())

        def go_near(self, k):
            self.near(k, 1).start()
            self.near(k, 3).start()
            self.side(k, 0).start()

        def step_near(self, k):
            self.near_in(k, 1).wait_recv()
            self.near_in(k, 3).wait_recv()
            self.relay(k).start()
            self.side(k, 1).start()
            self.side(k, 3).start()

        def step_far(self, k):
            self.relay_in(k).wait_recv()
            self.side(k, 2).start()

        def arrive(self):
            each(0, self.slots, lambda k: each(0, NY, lambda j: self.side_in(k, j).wait_recv()))

        def finish(self):
            each(1, self.peers, lambda k: self.enter(k).wait_send())

            def one(k):
                self.near(k, 1).wait_send()
                self.near(k, 3).wait_send()
                self.relay(k).wait_send()
                each(0, NY, lambda j: self.side(k, j).wait_send())

            each(0, self.slots, one)

    def x_slot(buf):
        return lambda d, k: buf.at[d, xa(NX - k)]

    qkv_w = Spread(
        w4_sems, NX, w4, xdev, NX, w4buf.at[dp, x], lambda k: w4buf.at[dp, xa(NX - k)],
        x_slot(w4buf),
    )
    ffn_w = Spread(
        wm_sems, NX, wbuf.at[dp, x], xdev, NX, wbuf.at[dp, x], lambda k: wbuf.at[dp, xa(NX - k)],
        x_slot(wbuf),
    )
    out_w = Spread(
        wo_sems, 2, wo, zdev, NZ, wobuf.at[dp, z], lambda k: wobuf.at[dp, za(NZ - k)],
        lambda d, k: wobuf.at[d, pl.ds(4 * k, 4)],
    )

    def hz(k):
        return send(hidden, hid.at[z], hz_s.at[k], hz_r.at[k], zdev(k))

    def hz_in(k):
        at = hid.at[za(NZ - k)]
        return send(at, at, hz_s.at[k], hz_r.at[k], zdev(k))

    def columns(at):
        return pl.ds(pl.multiple_of(at * PART, PART), PART)

    def key_rows(at):
        return pl.ds(pl.multiple_of(at * CTX, 128), CTX)

    def kx(k):
        return send(keys.at[:, columns(xa(k))], kraw.at[x], k_s.at[k], k_r.at[k], xdev(k))

    def kx_in(k):
        at = kraw.at[xa(NX - k)]
        return send(at, at, k_s.at[k], k_r.at[k], xdev(k))

    def vx(k):
        return send(
            values.at[:, columns(xa(k))], vall.at[key_rows(x)], v_s.at[k], v_r.at[k], xdev(k)
        )

    def vx_in(k):
        at = vall.at[key_rows(xa(NX - k))]
        return send(at, at, v_s.at[k], v_r.at[k], xdev(k))

    def px(k):
        return send(psend.at[xa(k)], precv.at[x], p_s.at[k], p_r.at[k], xdev(k))

    def px_in(k):
        at = precv.at[xa(NX - k)]
        return send(at, at, p_s.at[k], p_r.at[k], xdev(k))

    def qz(k):
        return send(qpk, qrecv.at[z], q_s.at[k], q_r.at[k], zdev(k))

    def qz_in(k):
        at = qrecv.at[za(NZ - k)]
        return send(at, at, q_s.at[k], q_r.at[k], zdev(k))

    def cz(k):
        return send(kvs.at[za(k)], kvrecv.at[z], c_s.at[k], c_r.at[k], zdev(k))

    def cz_in(k):
        at = kvrecv.at[za(NZ - k)]
        return send(at, at, c_s.at[k], c_r.at[k], zdev(k))

    def stx(k):
        return send(stat.at[x], stat.at[x], st_s.at[k], st_r.at[k], xdev(k))

    def stx_in(k):
        at = stat.at[xa(NX - k)]
        return send(at, at, st_s.at[k], st_r.at[k], xdev(k))

    def fx(k):
        return send(kf.at[xa(k)], frecv.at[x], f_s.at[k], f_r.at[k], xdev(k))

    def fx_in(k):
        at = frecv.at[xa(NX - k)]
        return send(at, at, f_s.at[k], f_r.at[k], xdev(k))

    def oex(k):
        return send(obuf.at[za(k)], orecv.at[z], o_s.at[k], o_r.at[k], zdev(k))

    def oex_in(k):
        at = orecv.at[za(NZ - k)]
        return send(at, at, o_s.at[k], o_r.at[k], zdev(k))

    def yx(k):
        return send(ysend.at[xa(k)], yrecv.at[x], y_s.at[k], y_r.at[k], xdev(k))

    def yx_in(k):
        at = yrecv.at[xa(NX - k)]
        return send(at, at, y_s.at[k], y_r.at[k], xdev(k))

    def nz(k):
        return send(hn, hbuf.at[z], n_s.at[k], n_r.at[k], zdev(k))

    def nz_in(k):
        at = hbuf.at[za(NZ - k)]
        return send(at, at, n_s.at[k], n_r.at[k], zdev(k))

    def dz(half, k):
        return send(
            dsend.at[half, za(k)], drecv.at[half, z], d_s.at[half, k], d_r.at[half, k], zdev(k)
        )

    def dz_in(half, k):
        at = drecv.at[half, za(NZ - k)]
        return send(at, at, d_s.at[half, k], d_r.at[half, k], zdev(k))

    own_copies = [
        pltpu.make_async_copy(hidden, hid.at[z], loc.at[0]),
        pltpu.make_async_copy(w4, w4buf.at[dp, x], loc.at[1]),
        pltpu.make_async_copy(wo, wobuf.at[dp, z], loc.at[2]),
        pltpu.make_async_copy(wgu, wbuf.at[dp, x, pl.ds(0, 2)], loc.at[3]),
        pltpu.make_async_copy(keys.at[:, columns(x)], kraw.at[x], loc.at[4]),
        pltpu.make_async_copy(values.at[:, columns(x)], vall.at[key_rows(x)], loc.at[5]),
        pltpu.make_async_copy(wd, wbuf.at[dp, x, 2], loc.at[6]),
    ]
    for copy in own_copies:
        copy.start()

    barrier = pltpu.get_barrier_semaphore()

    def greet(dev):
        pl.semaphore_signal(barrier, inc=1, device_id=dev, device_id_type=MESH)

    each(1, NZ, lambda k: greet(zdev(k)))
    each(1, NX, lambda k: greet(xdev(k)))
    greet({"dp": da(2)})
    greet({"dp": da(6)})
    greet({"dp": sib})
    pl.semaphore_wait(barrier, NZ + NX + 1)

    qkv_w.start()
    own_copies[1].wait()
    qkv_w.go_near(0)
    each(1, NZ, lambda k: hz(k).start())
    own_copies[3].wait()
    own_copies[6].wait()
    ffn_w.enter(1).start()
    ffn_w.enter(3).start()
    each(1, NX, lambda k: kx(k).start())
    out_w.start()

    end_a = lengths[0, 0]
    end_b = end_a + lengths[0, 1]
    span = lax.broadcasted_iota(jnp.int32, (16, HEAD_DIM), 0)
    turns = jnp.zeros((16, HEAD_DIM), jnp.int32)
    shifts, bottoms = [], []
    for slot in range(NCH):
        place = order[0, slot]
        second, third = place >= end_a, place >= end_b
        start = jnp.where(third, end_b, jnp.where(second, end_a, 0))
        moved = jnp.where(third, offsets[0, 2], jnp.where(second, offsets[0, 1], offsets[0, 0]))
        bottom = jnp.where(third, 2 * SPAN, jnp.where(second, SPAN, 0))
        base = moved + (place - start) * CH
        sbase[slot] = base + bottom - slot * CH
        shifts.append(base + bottom - slot * CH)
        bottoms.append(bottom)
        turns = jnp.where(span == slot, base, turns)

    turn_lane = lax.rem(lanes(8), HEAD_DIM // 2)
    rates = jnp.zeros((8, HEAD_DIM), F32)
    for j in range(HEAD_DIM // 2):
        rates = jnp.where(turn_lane == j, RATES[j], rates)

    def circle(position):
        angle = position.astype(F32) * rates[0:1, :]
        laps = jnp.floor(angle * (0.5 / math.pi) + 0.5)
        angle = ((angle - laps * LAP_A) - laps * LAP_B) - laps * LAP_C
        sine = jnp.sin(angle)
        left = lax.broadcasted_iota(jnp.int32, position.shape, 1) < HEAD_DIM // 2
        return jnp.cos(angle), jnp.where(left, -sine, sine)

    scos[...], ssin[...] = circle(turns)

    def qkv_on(k):
        qkv_w.enter_in(k).wait_recv()
        qkv_w.go_near(k)

    each(1, NX, qkv_on)

    natural[...] = lax.dot_general(
        jnp.broadcast_to(picked[...].astype(F32), (8, SEL)),
        jnp.full((8, HEAD_DIM), 0.125, F32), (((0,), (0,)), ((), ())),
        precision=HIGH, preferred_element_type=F32,
    )
    for zz in range(NZ):
        for xx in range(NX):
            at = (zz * NX + xx) * OWN
            back = (xx * NZ + zz) * OWN
            rows_of[at : at + OWN] = natural[back : back + OWN].astype(jnp.int32)

    def tokens(i):
        rows = pl.ds(pl.multiple_of(i * 128, 128), 128)
        row = rows_of[rows]
        slot_of = lax.shift_right_logical(row, 10)
        shift = jnp.zeros_like(row)
        bottom = jnp.zeros_like(row)
        for slot in range(NCH):
            mine = slot_of == slot
            shift = jnp.where(mine, shifts[slot], shift)
            bottom = jnp.where(mine, bottoms[slot], bottom)
        codes[rows] = row + shift
        lows[rows] = bottom
        qcos[rows], qsin[rows] = circle(row + shift - bottom)

    each(0, SEL // 128, tokens)
    grp_rows = pl.ds(pl.multiple_of(z * GRP, GRP), GRP)

    for block in range(NX):
        first = (block * NZ + z) * CTX
        slot = lax.div(first, CH)
        later = lax.min(slot + 1, NCH - 1)
        row = first + lax.broadcasted_iota(jnp.int32, (1, CTX), 1)
        code = jnp.where(row < (slot + 1) * CH, sbase[slot], sbase[later]) + row
        hit = jnp.max(
            jnp.where(rows_of[:, 0:1] == row, 1, 0), axis=0, keepdims=True
        )
        kcode[:, block * CTX : (block + 1) * CTX] = jnp.where(hit > 0, DEAD, code)
    corner = lax.broadcasted_iota(jnp.int32, (GRP, HEAD_DIM), 0) == lanes(GRP)
    kcode[:, CACHED:KEYS] = jnp.where(
        lanes(1) < GRP,
        jnp.sum(jnp.where(corner, codes[grp_rows], 0), axis=0, keepdims=True),
        DEAD,
    )
    kall[CACHED:KEYS, :] = jnp.zeros((KEYS - CACHED, PART), BF16)
    vall[CACHED:KEYS, :] = jnp.zeros((KEYS - CACHED, PART), BF16)

    each(0, NX, qkv_w.step_near)
    own_copies[2].wait()
    each(1, NZ, lambda k: out_w.enter_in(k).wait_recv())
    each(0, NX, qkv_w.step_far)
    each(0, 2, out_w.go_near)
    ffn_w.go_near(0)

    own_copies[0].wait()
    each(1, NZ, lambda k: hz_in(k).wait_recv())
    qkv_w.arrive()

    low_x = lanes(NZ * OWN) < HEAD_DIM // 2

    def project(i):
        k = lax.rem(i + 1, NX)
        at = xa(k)
        rows = hid[...].reshape(NZ * OWN, D)
        kv = jnp.dot(
            rows, w4buf[:, at, :256].reshape(D, HEAD_DIM), preferred_element_type=F32
        )
        packed = w4buf[:, at, 256:].reshape(D // 2, HEAD_DIM)
        upper = jnp.concatenate(
            [rows[:, c * 256 : c * 256 + 128] for c in range(NDP)], axis=1
        )
        lower = jnp.concatenate(
            [rows[:, c * 256 + 128 : (c + 1) * 256] for c in range(NDP)], axis=1
        )
        a = jnp.dot(upper, packed, preferred_element_type=F32)
        b = jnp.dot(lower, packed, preferred_element_type=F32)
        q = a + pltpu.roll(b, 64, 1)
        psend[at, :, :HEAD_DIM] = kv.astype(BF16)
        psend[at, :, HEAD_DIM:] = jnp.where(low_x, q, pltpu.roll(q, 64, 1)).astype(BF16)
        squares[0] += jnp.where(low_x, q * q, 0.0)
        squares[1] += jnp.where(low_x, kv * kv, 0.0)
        return k

    def project_send(i):
        k = project(i)
        px(k).start()

    squares[...] = jnp.zeros_like(squares)
    each(0, NX - 1, project_send)
    project(NX - 1)
    lane_own = lanes(OWN)
    mine = jnp.zeros((OWN, HEAD_DIM), F32)
    for kind in range(2):
        sums = jnp.sum(squares[kind], axis=1, keepdims=True)
        for g in range(NZ):
            mine = jnp.where(lane_own == 4 * g + 2 * kind, sums[g * OWN : (g + 1) * OWN], mine)
    stat[pl.ds(x, 1)] = mine[None]
    each(1, NX, lambda k: stx(k).start())
    precv[pl.ds(x, 1)] = psend[pl.ds(x, 1)]

    each(1, NX, lambda k: vx(k).start())
    ffn_w.enter(2).start()
    for k in (1, 3):
        ffn_w.enter_in(k).wait_recv()
        ffn_w.go_near(k)
    each(1, NX, lambda k: px_in(k).wait_recv())
    low = lanes(SEL // 2) < HEAD_DIM // 2
    for g in range(NZ // 2):
        two = []
        for gg in (g, g + NZ // 2):
            rows = jnp.concatenate(
                [precv[p, gg * OWN : (gg + 1) * OWN] for p in range(NX)], axis=0
            )
            kvs[gg] = rows[:, :HEAD_DIM]
            two.append(rows[:, HEAD_DIM:].astype(F32))
        qpk[g * GRP : (g + 1) * GRP, :] = jnp.where(low[:GRP], two[0], two[1]).astype(BF16)
    each(1, NX, lambda k: stx_in(k).wait_recv())
    both = stat[0]
    for p in range(1, NX):
        both += pltpu.roll(stat[p], 32 * p, 1)
    high = both.astype(BF16).astype(F32)
    qpk[SEL // 2 :, :] = (high + pltpu.roll(both - high, 1, 1)).astype(BF16)
    each(1, NZ, lambda k: qz(k).start())
    each(1, NZ, lambda k: cz(k).start())
    qrecv[pl.ds(z, 1)] = qpk[...][None]
    kvrecv[pl.ds(z, 1)] = kvs[pl.ds(z, 1)]
    each(0, 2, out_w.step_near)

    own_copies[4].wait()
    each(1, NX, lambda k: kx_in(k).wait_recv())

    def turn(block):
        first = (block * NZ + z) * CTX
        slot = lax.div(first, CH)
        later = lax.min(slot + 1, NCH - 1)
        row = first + lax.broadcasted_iota(jnp.int32, (CTX, HEAD_DIM), 0)
        here = row < (slot + 1) * CH
        cosine = jnp.where(here, scos[pl.ds(slot, 1), :], scos[pl.ds(later, 1), :])
        sine = jnp.where(here, ssin[pl.ds(slot, 1), :], ssin[pl.ds(later, 1), :])
        for h in range(HEADS):
            cols = slice(h * HEAD_DIM, (h + 1) * HEAD_DIM)
            v = kraw[block, :, cols].astype(F32)
            kall[key_rows(block), cols] = (v * cosine + pltpu.roll(v, 64, 1) * sine).astype(BF16)

    each(0, NX, turn)
    def mask(i):
        rows = pl.ds(pl.multiple_of(i * 128, 128), 128)
        code = kcode[...]
        usable = (code <= codes[rows, 0:1]) & (code >= lows[rows, 0:1])
        bias[rows] = jnp.where(usable, 0.0, NEGATIVE)

    each(0, SEL // 128, mask)

    each(1, NZ, lambda k: qz_in(k).wait_recv())
    each(1, NZ, lambda k: cz_in(k).wait_recv())
    low_f = lanes(GRP) < HEAD_DIM // 2

    def q_head(h):
        a = qrecv[2 * h, : SEL // 2].astype(F32)
        b = qrecv[2 * h + 1, : SEL // 2].astype(F32)
        top = jnp.where(low, a, pltpu.roll(b, 64, 1))
        bottom = jnp.where(low, pltpu.roll(a, 64, 1), b)
        return top, bottom

    def f_head(h):
        a = kvrecv[2 * h].astype(F32)
        b = kvrecv[2 * h + 1].astype(F32)
        return jnp.where(low_f, a, pltpu.roll(b, 64, 1)), jnp.where(low_f, pltpu.roll(a, 64, 1), b)

    each(0, 2, out_w.step_far)
    total = jnp.zeros((OWN, HEAD_DIM), F32)
    for p in range(NZ):
        total += qrecv[p, SEL // 2 :].astype(F32)
    total = total + pltpu.roll(total, HEAD_DIM - 1, 1)
    even = lax.rem(lane_own, 2) == 0
    factor = lax.rsqrt(jnp.where(even, total, 1.0) * (1.0 / D) + EPSILON)
    for g in range(NZ):
        for p in range(NX):
            at = (g * NX + p) * OWN
            col = 32 * p + 4 * g
            sq[0, at : at + OWN] = jnp.broadcast_to(
                factor[:, col : col + 1] * SCORE, (OWN, HEAD_DIM)
            )
            sq[1, at : at + OWN] = jnp.broadcast_to(factor[:, col + 2 : col + 3], (OWN, HEAD_DIM))
    for h in range(HEADS):
        cols = pl.ds(pl.multiple_of(x * PART + h * HEAD_DIM, HEAD_DIM), HEAD_DIM)
        top, bottom = q_head(h)
        gain = gains[0:1, cols]
        for part, rows in ((top, slice(0, SEL // 2)), (bottom, slice(SEL // 2, SEL))):
            v = part * sq[0, rows] * gain
            qh[h, rows] = (v * qcos[rows] + pltpu.roll(v, 64, 1) * qsin[rows]).astype(BF16)
        key, value = f_head(h)
        vall[CACHED : CACHED + GRP, h * HEAD_DIM : (h + 1) * HEAD_DIM] = value.astype(BF16)
        v = key * sq[1, grp_rows] * gains[1:2, cols]
        v = (v * qcos[grp_rows] + pltpu.roll(v, 64, 1) * qsin[grp_rows]).astype(BF16)
        kall[CACHED : CACHED + GRP, h * HEAD_DIM : (h + 1) * HEAD_DIM] = v
        kf[:, :, h * HEAD_DIM : (h + 1) * HEAD_DIM] = v.reshape(NX, OWN, HEAD_DIM)
    each(1, NX, lambda k: fx(k).start())
    frecv[pl.ds(x, 1)] = kf[pl.ds(x, 1)]

    own_copies[5].wait()
    each(1, NX, lambda k: vx_in(k).wait_recv())

    lane = lanes(128)

    def attend(part):
        rows = pl.ds(pl.multiple_of(part * 128, 128), 128)
        two = pl.ds(part * 2, 2)
        marks = jnp.zeros((128, HEAD_DIM), F32)
        for h in range(HEADS):
            cols = slice(h * HEAD_DIM, (h + 1) * HEAD_DIM)
            scores = lax.dot_general(
                qh[h, rows], kall[:, cols], (((1,), (1,)), ((), ())), preferred_element_type=F32
            ) + bias[rows]
            most = jnp.maximum(jnp.max(scores, axis=1, keepdims=True), FLOOR)
            most = most.astype(BF16).astype(F32)
            weight = jnp.exp2(scores - most)
            mass = jnp.sum(weight, axis=1, keepdims=True)
            mixed = jnp.dot(weight.astype(BF16), vall[:, cols], preferred_element_type=F32)
            obuf[two, h * GRP : (h + 1) * GRP, :] = mixed.astype(BF16).reshape(2, GRP, HEAD_DIM)
            high = mass.astype(BF16).astype(F32)
            marks = jnp.where(lane == h, most, marks)
            marks = jnp.where(lane == h + HEADS, high, marks)
            marks = jnp.where(lane == h + 2 * HEADS, mass - high, marks)
        for side in range(2):
            packed = marks[side * GRP : side * GRP + OWN]
            for g in range(1, NX):
                at = side * GRP + g * OWN
                packed += pltpu.roll(marks[at : at + OWN], 32 * g, 1)
            obuf[part * 2 + side, HEADS * GRP :, :] = packed.astype(BF16)

    def attend_far(i):
        part = lax.rem(lax.div(z, 2) + 1 + lax.rem(i + 1, 3), NZ // 2)
        attend(part)
        offset = lax.rem(2 * part + NZ - z, NZ)
        oex(offset).start()
        oex(lax.rem(offset + 1, NZ)).start()
        ffn_w.step_near(i + lax.div(i, 2))

    each(0, 3, attend_far)
    attend(lax.div(z, 2))
    beside = lax.rem(NZ + 1 - 2 * lax.rem(z, 2), NZ)
    oex(beside).start()
    orecv[pl.ds(z, 1)] = obuf[pl.ds(z, 1)]
    ffn_w.enter_in(2).wait_recv()
    ffn_w.go_near(2)
    out_w.arrive()
    each(1, NZ, lambda k: oex_in(k).wait_recv())

    def marks_of(p):
        return orecv[p, HEADS * GRP :, :].astype(F32)

    peak = marks_of(0)
    for p in range(1, NZ):
        peak = jnp.maximum(peak, marks_of(p))
    mass = jnp.zeros((OWN, HEAD_DIM), F32)
    for p in range(NZ):
        marks = marks_of(p)
        amount = pltpu.roll(marks, HEAD_DIM - HEADS, 1) + pltpu.roll(
            marks, HEAD_DIM - 2 * HEADS, 1
        )
        mass += jnp.exp2(marks - peak) * amount
    valid = lax.rem(lane_own, 32) < HEADS
    inverse = 1.0 / jnp.where(valid, mass, 1.0)
    heads = [jnp.zeros((GRP, HEAD_DIM), F32) for _ in range(HEADS)]
    for p in range(NZ):
        share = jnp.exp2(marks_of(p) - peak) * inverse
        for h in range(HEADS):
            part = orecv[p, h * GRP : (h + 1) * GRP, :].astype(F32)
            weight = jnp.concatenate(
                [
                    jnp.broadcast_to(
                        share[:, 32 * g + h : 32 * g + h + 1], (OWN, HEAD_DIM)
                    )
                    for g in range(NX)
                ],
                axis=0,
            )
            heads[h] += part * weight
    attn = jnp.concatenate(heads, axis=1).astype(BF16)

    def out_block(c):
        got = jnp.dot(attn, wobuf[c].reshape(PART, 256), preferred_element_type=F32)
        cols = pl.ds(pl.multiple_of(c * 256, 256), 256)
        ysend[:, :, cols] = got.astype(BF16).reshape(NX, OWN, 256)

    each(0, NDP, out_block)
    each(1, NX, lambda k: yx(k).start())
    yrecv[pl.ds(x, 1)] = ysend[pl.ds(x, 1)]
    for k in (0, 1, 3):
        ffn_w.step_far(k)
    each(1, NX, lambda k: yx_in(k).wait_recv())
    y = yrecv[0].astype(F32)
    for p in range(1, NX):
        y += yrecv[p].astype(F32)
    y = y * lax.rsqrt(jnp.mean(y * y, axis=1, keepdims=True) + EPSILON) * gains[2:3, :]
    following = (hid[z].astype(F32) + y).astype(BF16)
    hn[...] = following
    each(1, NZ, lambda k: nz(k).start())
    hbuf[pl.ds(z, 1)] = following[None]
    ffn_w.step_near(2)
    ffn_w.step_far(2)

    each(1, NZ, lambda k: nz_in(k).wait_recv())
    ffn_w.arrive()

    def gate(c):
        rows = hbuf[...].reshape(NZ * OWN, D)
        g = jnp.dot(rows, wbuf[:, c, 0].reshape(D, 256), preferred_element_type=F32)
        u = jnp.dot(rows, wbuf[:, c, 1].reshape(D, 256), preferred_element_type=F32)
        cols = pl.ds(pl.multiple_of(c * 256, 256), 256)
        act[:, cols] = (jax.nn.silu(g) * u).astype(BF16)

    each(0, NX, gate)

    def down_half(half):
        def down(c):
            weights = wbuf[half * 4 + c, :, 2].reshape(NX * 256, 256)
            got = jnp.dot(act[...], weights, preferred_element_type=F32)
            cols = pl.ds(pl.multiple_of(c * 256, 256), 256)
            dsend[half, :, :, cols] = got.astype(BF16).reshape(NZ, OWN, 256)

        each(0, 4, down)
        each(1, NZ, lambda k: dz(half, k).start())

    each(0, 2, down_half)
    for half in range(2):
        drecv[half, pl.ds(z, 1)] = dsend[half, pl.ds(z, 1)]

    each(1, NX, lambda k: fx_in(k).wait_recv())
    for p in range(NX):
        fresh[:, p * PART : (p + 1) * PART] = frecv[p]

    each(0, 2, lambda half: each(1, NZ, lambda k: dz_in(half, k).wait_recv()))
    halves = []
    for half in range(2):
        t = drecv[half, 0].astype(F32)
        for p in range(1, NZ):
            t += drecv[half, p].astype(F32)
        halves.append(t)
    t = jnp.concatenate(halves, axis=1)
    t = t * lax.rsqrt(jnp.mean(t * t, axis=1, keepdims=True) + EPSILON) * gains[3:4, :]
    out[...] = (hn[...].astype(F32) + t).astype(BF16)

    for copy in (hz, qz, cz, oex, nz):
        each(1, NZ, lambda k, copy=copy: copy(k).wait_send())
    for copy in (kx, vx, px, stx, fx, yx):
        each(1, NX, lambda k, copy=copy: copy(k).wait_send())
    each(0, 2, lambda half: each(1, NZ, lambda k: dz(half, k).wait_send()))
    for weights in (qkv_w, out_w, ffn_w):
        weights.finish()


def layer(
    hidden_sel, picked, order, lengths, offsets, cache_keys, cache_values, w_qkv, w_out,
    w_gate_up, w_down, gains,
):
    w4 = jnp.concatenate(
        [
            jnp.concatenate([w_qkv[1], w_qkv[2]], axis=1),
            jnp.concatenate([w_qkv[0, :128], w_qkv[0, 128:]], axis=1),
        ],
        axis=0,
    )

    vmem = pl.BlockSpec(memory_space=pltpu.VMEM)
    far = pl.BlockSpec(memory_space=pl.ANY)
    smem = pl.BlockSpec(memory_space=pltpu.SMEM)
    dma = pltpu.SemaphoreType.DMA

    def spread(peers, slots):
        return (
            dma((peers,)), dma((peers,)), dma((slots, NY)), dma((slots, NY)), dma((slots,)),
            dma((slots, NY)), dma((slots, NY)),
        )

    out, fresh = pl.pallas_call(
        kernel,
        out_shape=(
            jax.ShapeDtypeStruct((OWN, D), BF16),
            jax.ShapeDtypeStruct((OWN, D), BF16),
        ),
        in_specs=[vmem, far, far, far, far, far, far, vmem, vmem, smem, smem, smem],
        out_specs=(vmem, vmem),
        scratch_shapes=[
            pltpu.VMEM((NZ, OWN, D), BF16),
            pltpu.VMEM((NDP, NX, 384, HEAD_DIM), BF16),
            pltpu.VMEM((NDP, NZ, 64, 256), BF16),
            pltpu.VMEM((NDP, NX, 3, 256, 256), BF16),
            pltpu.VMEM((NX, CTX, PART), BF16),
            pltpu.VMEM((KEYS, PART), BF16),
            pltpu.VMEM((KEYS, PART), BF16),
            pltpu.VMEM((1, KEYS), jnp.int32),
            pltpu.VMEM((NX, NZ * OWN, 256), BF16),
            pltpu.VMEM((NX, NZ * OWN, 256), BF16),
            pltpu.VMEM((SEL // 2 + OWN, HEAD_DIM), BF16),
            pltpu.VMEM((NZ, GRP, HEAD_DIM), BF16),
            pltpu.VMEM((NZ, SEL // 2 + OWN, HEAD_DIM), BF16),
            pltpu.VMEM((NZ, GRP, HEAD_DIM), BF16),
            pltpu.VMEM((2, SEL, HEAD_DIM), F32),
            pltpu.VMEM((NX, OWN, HEAD_DIM), F32),
            pltpu.VMEM((HEADS, SEL, HEAD_DIM), BF16),
            pltpu.VMEM((NX, OWN, PART), BF16),
            pltpu.VMEM((NX, OWN, PART), BF16),
            pltpu.VMEM((NZ, HEADS * GRP + OWN, HEAD_DIM), BF16),
            pltpu.VMEM((NZ, HEADS * GRP + OWN, HEAD_DIM), BF16),
            pltpu.VMEM((NX, OWN, D), BF16),
            pltpu.VMEM((NX, OWN, D), BF16),
            pltpu.VMEM((OWN, D), BF16),
            pltpu.VMEM((NZ, OWN, D), BF16),
            pltpu.VMEM((NZ * OWN, NX * 256), BF16),
            pltpu.VMEM((2, NZ, OWN, D // 2), BF16),
            pltpu.VMEM((2, NZ, OWN, D // 2), BF16),
            pltpu.VMEM((SEL, HEAD_DIM), F32),
            pltpu.VMEM((SEL, HEAD_DIM), jnp.int32),
            pltpu.VMEM((SEL, HEAD_DIM), jnp.int32),
            pltpu.VMEM((SEL, HEAD_DIM), jnp.int32),
            pltpu.VMEM((SEL, HEAD_DIM), F32),
            pltpu.VMEM((SEL, HEAD_DIM), F32),
            pltpu.VMEM((16, HEAD_DIM), F32),
            pltpu.VMEM((16, HEAD_DIM), F32),
            pltpu.SMEM((16,), jnp.int32),
            pltpu.VMEM((SEL, KEYS), F32),
            pltpu.VMEM((2, NZ * OWN, HEAD_DIM), F32),
            dma((NZ,)), dma((NZ,)),
            spread(NX, NX),
            spread(NZ, 2),
            spread(NX, NX),
            dma((NX,)), dma((NX,)),
            dma((NX,)), dma((NX,)),
            dma((NX,)), dma((NX,)),
            dma((NZ,)), dma((NZ,)),
            dma((NZ,)), dma((NZ,)),
            dma((NX,)), dma((NX,)),
            dma((NX,)), dma((NX,)),
            dma((NZ,)), dma((NZ,)),
            dma((NX,)), dma((NX,)),
            dma((NZ,)), dma((NZ,)),
            dma((2, NZ)), dma((2, NZ)),
            dma((7,)),
        ],
        compiler_params=pltpu.CompilerParams(
            collective_id=0, has_side_effects=True, vmem_limit_bytes=56 << 20
        ),
    )(
        hidden_sel[0], cache_keys[0], cache_values[0], w4, w_out, w_gate_up, w_down, gains,
        picked, order, lengths, offsets,
    )
    return (out[None], fresh[None])


def solution(mesh):
    placed = (
        P("dp", "tensor", None),
        P("dp", None),
        P("dp", None),
        P("dp", None),
        P("dp", None),
        P("dp", "tensor", None),
        P("dp", "tensor", None),
        P(None, "dp", "tensor"),
        P("tensor", "dp"),
        P(None, "dp", "tensor"),
        P("tensor", "dp"),
        P(),
    )
    return jax.shard_map(
        layer,
        mesh=mesh,
        in_specs=placed,
        out_specs=(P("dp", "tensor", None), P("dp", "tensor", None)),
        check_vma=False,
    )
```

```python
import math

import jax
import jax.numpy as jnp
import numpy as np
from jax import lax
from jax.experimental import pallas as pl
from jax.experimental.pallas import tpu as pltpu
from jax.sharding import PartitionSpec as P

HEAD_DIM = 128
CH = 1024
NCH = 12
REQS = 3
NX = 4
NZ = 8
NDP = 8
NY = 4
D = 2048
PART = D // NX
HEADS = PART // HEAD_DIM
OWN = 16
GRP = NX * OWN
SEL = NZ * GRP
CTX = 384
CACHED = NX * CTX
KEYS = CACHED + 128
SPAN = 1 << 14
DEAD = 1 << 30

THETA = 500000.0
EPSILON = 1e-06
NEGATIVE = -1e30
FLOOR = -1e20
SCORE = HEAD_DIM ** (-0.5) * math.log2(math.e)
LAP_A = 6.28125
LAP_B = 0.0019340515136718750
LAP_C = 2.0 * math.pi - LAP_A - LAP_B
RATES = [
    float(np.float32(math.exp(-2.0 * j / HEAD_DIM * math.log(THETA)))) for j in range(HEAD_DIM // 2)
]
MESH = pl.DeviceIdType.MESH
F32, BF16 = jnp.float32, jnp.bfloat16
HIGH = lax.Precision.HIGHEST


def lanes(rows):
    return lax.broadcasted_iota(jnp.int32, (rows, HEAD_DIM), 1)


def kernel(
    hidden,
    keys,
    values,
    w4,
    wo,
    wgu,
    wd,
    gains,
    picked,
    order,
    lengths,
    offsets,
    out,
    fresh,
    hid,
    w4buf,
    wobuf,
    wbuf,
    kraw,
    kall,
    vall,
    kcode,
    psend,
    precv,
    qpk,
    kvs,
    qrecv,
    kvrecv,
    sq,
    stat,
    qh,
    kf,
    frecv,
    obuf,
    orecv,
    ysend,
    yrecv,
    hn,
    hbuf,
    act,
    dsend,
    drecv,
    natural,
    rows_of,
    codes,
    lows,
    qcos,
    qsin,
    scos,
    ssin,
    sbase,
    bias,
    squares,
    hz_s,
    hz_r,
    w4_sems,
    wo_sems,
    wm_sems,
    k_s,
    k_r,
    v_s,
    v_r,
    p_s,
    p_r,
    q_s,
    q_r,
    c_s,
    c_r,
    st_s,
    st_r,
    f_s,
    f_r,
    o_s,
    o_r,
    y_s,
    y_r,
    n_s,
    n_r,
    d_s,
    d_r,
    loc,
):
    tens = lax.axis_index("tensor")
    dp = lax.axis_index("dp")
    x = lax.div(tens, NZ)
    z = lax.rem(tens, NZ)
    core = lax.rem(dp, 2)
    sib = dp + 1 - 2 * core

    def xa(k):
        return lax.rem(x + k, NX)

    def za(k):
        return lax.rem(z + k, NZ)

    def da(k):
        return lax.rem(dp + k, NDP)

    def zdev(k):
        return {"tensor": x * NZ + za(k)}

    def xdev(k):
        return {"tensor": xa(k) * NZ + z}

    def send(src, dst, ssem, rsem, dev):
        return pltpu.make_async_remote_copy(
            src_ref=src, dst_ref=dst, send_sem=ssem, recv_sem=rsem, device_id=dev,
            device_id_type=MESH,
        )

    def each(first, last, body):
        def step(k, carry):
            body(k)
            return carry

        lax.fori_loop(first, last, step, 0)

    class Spread:
        def __init__(self, sems, slots, source, first, peers, entry, entry_in, at):
            (self.e_s, self.e_r, self.n_s, self.y_r, self.r_s, self.s_s, self.s_r) = sems
            self.slots, self.source, self.first, self.peers = slots, source, first, peers
            self.entry, self.entry_in, self.at = entry, entry_in, at

        def enter(self, k):
            return send(self.source, self.entry, self.e_s.at[k], self.e_r.at[k], self.first(k))

        def enter_in(self, k):
            at = self.entry_in(k)
            return send(at, at, self.e_s.at[k], self.e_r.at[k], self.first(k))

        def near(self, k, j):
            at = self.at(dp, k)
            return send(at, at, self.n_s.at[k, j], self.y_r.at[k, j], {"dp": da(2 * j)})

        def near_in(self, k, j):
            at = self.at(da(NDP - 2 * j), k)
            return send(at, at, self.n_s.at[k, j], self.y_r.at[k, j], {"dp": da(2 * j)})

        def way(self, k):
            return 1 + 2 * lax.div(k, self.slots // 2)

        def relay(self, k):
            j = self.way(k)
            at = self.at(da(NDP - 2 * j), k)
            return send(at, at, self.r_s.at[k], self.y_r.at[k, 2], {"dp": da(2 * j)})

        def relay_in(self, k):
            at = self.at(da(4), k)
            return send(at, at, self.r_s.at[k], self.y_r.at[k, 2], {"dp": da(2)})

        def side(self, k, j):
            at = self.at(da(NDP - 2 * j), k)
            return send(at, at, self.s_s.at[k, j], self.s_r.at[k, j], {"dp": sib})

        def side_in(self, k, j):
            at = self.at(lax.rem(sib + NDP - 2 * j, NDP), k)
            return send(at, at, self.s_s.at[k, j], self.s_r.at[k, j], {"dp": sib})

        def start(self):
            each(1, self.peers, lambda k: self.enter(k).start())

        def go_near(self, k):
            self.near(k, 1).start()
            self.near(k, 3).start()
            self.side(k, 0).start()

        def step_near(self, k):
            self.near_in(k, 1).wait_recv()
            self.near_in(k, 3).wait_recv()
            self.relay(k).start()
            self.side(k, 1).start()
            self.side(k, 3).start()

        def step_far(self, k):
            self.relay_in(k).wait_recv()
            self.side(k, 2).start()

        def arrive(self):
            each(0, self.slots, lambda k: each(0, NY, lambda j: self.side_in(k, j).wait_recv()))

        def finish(self):
            each(1, self.peers, lambda k: self.enter(k).wait_send())

            def one(k):
                self.near(k, 1).wait_send()
                self.near(k, 3).wait_send()
                self.relay(k).wait_send()
                each(0, NY, lambda j: self.side(k, j).wait_send())

            each(0, self.slots, one)

    def x_slot(buf):
        return lambda d, k: buf.at[d, xa(NX - k)]

    qkv_w = Spread(
        w4_sems, NX, w4, xdev, NX, w4buf.at[dp, x], lambda k: w4buf.at[dp, xa(NX - k)],
        x_slot(w4buf),
    )
    ffn_w = Spread(
        wm_sems, NX, wbuf.at[dp, x], xdev, NX, wbuf.at[dp, x], lambda k: wbuf.at[dp, xa(NX - k)],
        x_slot(wbuf),
    )
    out_w = Spread(
        wo_sems, 2, wo, zdev, NZ, wobuf.at[dp, z], lambda k: wobuf.at[dp, za(NZ - k)],
        lambda d, k: wobuf.at[d, pl.ds(4 * k, 4)],
    )

    def hz(k):
        return send(hidden, hid.at[z], hz_s.at[k], hz_r.at[k], zdev(k))

    def hz_in(k):
        at = hid.at[za(NZ - k)]
        return send(at, at, hz_s.at[k], hz_r.at[k], zdev(k))

    def columns(at):
        return pl.ds(pl.multiple_of(at * PART, PART), PART)

    def key_rows(at):
        return pl.ds(pl.multiple_of(at * CTX, 128), CTX)

    def kx(k):
        return send(keys.at[:, columns(xa(k))], kraw.at[x], k_s.at[k], k_r.at[k], xdev(k))

    def kx_in(k):
        at = kraw.at[xa(NX - k)]
        return send(at, at, k_s.at[k], k_r.at[k], xdev(k))

    def vx(k):
        return send(
            values.at[:, columns(xa(k))], vall.at[key_rows(x)], v_s.at[k], v_r.at[k], xdev(k)
        )

    def vx_in(k):
        at = vall.at[key_rows(xa(NX - k))]
        return send(at, at, v_s.at[k], v_r.at[k], xdev(k))

    def px(k):
        return send(psend.at[xa(k)], precv.at[x], p_s.at[k], p_r.at[k], xdev(k))

    def px_in(k):
        at = precv.at[xa(NX - k)]
        return send(at, at, p_s.at[k], p_r.at[k], xdev(k))

    def qz(j, k):
        p = xa(NX - j)
        return send(qpk.at[p], qrecv.at[z, p], q_s.at[j, k], q_r.at[j, k], zdev(k))

    def qz_in(j, k):
        at = qrecv.at[za(NZ - k), xa(NX - j)]
        return send(at, at, q_s.at[j, k], q_r.at[j, k], zdev(k))

    def cz(k):
        return send(kvs.at[za(k)], kvrecv.at[z], c_s.at[k], c_r.at[k], zdev(k))

    def cz_in(k):
        at = kvrecv.at[za(NZ - k)]
        return send(at, at, c_s.at[k], c_r.at[k], zdev(k))

    def stx(k):
        return send(stat.at[x], stat.at[x], st_s.at[k], st_r.at[k], xdev(k))

    def stx_in(k):
        at = stat.at[xa(NX - k)]
        return send(at, at, st_s.at[k], st_r.at[k], xdev(k))

    def fx(k):
        return send(kf.at[xa(k)], frecv.at[x], f_s.at[k], f_r.at[k], xdev(k))

    def fx_in(k):
        at = frecv.at[xa(NX - k)]
        return send(at, at, f_s.at[k], f_r.at[k], xdev(k))

    def oex(k):
        return send(obuf.at[za(k)], orecv.at[z], o_s.at[k], o_r.at[k], zdev(k))

    def oex_in(k):
        at = orecv.at[za(NZ - k)]
        return send(at, at, o_s.at[k], o_r.at[k], zdev(k))

    def yx(k):
        return send(ysend.at[xa(k)], yrecv.at[x], y_s.at[k], y_r.at[k], xdev(k))

    def yx_in(k):
        at = yrecv.at[xa(NX - k)]
        return send(at, at, y_s.at[k], y_r.at[k], xdev(k))

    def nz(k):
        return send(hn, hbuf.at[z], n_s.at[k], n_r.at[k], zdev(k))

    def nz_in(k):
        at = hbuf.at[za(NZ - k)]
        return send(at, at, n_s.at[k], n_r.at[k], zdev(k))

    def dz(half, k):
        return send(
            dsend.at[half, za(k)], drecv.at[half, z], d_s.at[half, k], d_r.at[half, k], zdev(k)
        )

    def dz_in(half, k):
        at = drecv.at[half, za(NZ - k)]
        return send(at, at, d_s.at[half, k], d_r.at[half, k], zdev(k))

    own_copies = [
        pltpu.make_async_copy(hidden, hid.at[z], loc.at[0]),
        pltpu.make_async_copy(w4, w4buf.at[dp, x], loc.at[1]),
        pltpu.make_async_copy(wo, wobuf.at[dp, z], loc.at[2]),
        pltpu.make_async_copy(wgu, wbuf.at[dp, x, pl.ds(0, 2)], loc.at[3]),
        pltpu.make_async_copy(keys.at[:, columns(x)], kraw.at[x], loc.at[4]),
        pltpu.make_async_copy(values.at[:, columns(x)], vall.at[key_rows(x)], loc.at[5]),
        pltpu.make_async_copy(wd, wbuf.at[dp, x, 2], loc.at[6]),
    ]
    for copy in own_copies:
        copy.start()

    barrier = pltpu.get_barrier_semaphore()

    def greet(dev):
        pl.semaphore_signal(barrier, inc=1, device_id=dev, device_id_type=MESH)

    each(1, NZ, lambda k: greet(zdev(k)))
    each(1, NX, lambda k: greet(xdev(k)))
    greet({"dp": da(2)})
    greet({"dp": da(6)})
    greet({"dp": sib})
    pl.semaphore_wait(barrier, NZ + NX + 1)

    qkv_w.start()
    own_copies[1].wait()
    qkv_w.go_near(0)
    each(1, NZ, lambda k: hz(k).start())
    own_copies[3].wait()
    own_copies[6].wait()
    ffn_w.enter(1).start()
    ffn_w.enter(3).start()
    each(1, NX, lambda k: kx(k).start())
    out_w.start()

    end_a = lengths[0, 0]
    end_b = end_a + lengths[0, 1]
    span = lax.broadcasted_iota(jnp.int32, (16, HEAD_DIM), 0)
    turns = jnp.zeros((16, HEAD_DIM), jnp.int32)
    shifts, bottoms = [], []
    for slot in range(NCH):
        place = order[0, slot]
        second, third = place >= end_a, place >= end_b
        start = jnp.where(third, end_b, jnp.where(second, end_a, 0))
        moved = jnp.where(third, offsets[0, 2], jnp.where(second, offsets[0, 1], offsets[0, 0]))
        bottom = jnp.where(third, 2 * SPAN, jnp.where(second, SPAN, 0))
        base = moved + (place - start) * CH
        sbase[slot] = base + bottom - slot * CH
        shifts.append(base + bottom - slot * CH)
        bottoms.append(bottom)
        turns = jnp.where(span == slot, base, turns)

    turn_lane = lax.rem(lanes(8), HEAD_DIM // 2)
    rates = jnp.zeros((8, HEAD_DIM), F32)
    for j in range(HEAD_DIM // 2):
        rates = jnp.where(turn_lane == j, RATES[j], rates)

    def circle(position):
        angle = position.astype(F32) * rates[0:1, :]
        laps = jnp.floor(angle * (0.5 / math.pi) + 0.5)
        angle = ((angle - laps * LAP_A) - laps * LAP_B) - laps * LAP_C
        sine = jnp.sin(angle)
        left = lax.broadcasted_iota(jnp.int32, position.shape, 1) < HEAD_DIM // 2
        return jnp.cos(angle), jnp.where(left, -sine, sine)

    scos[...], ssin[...] = circle(turns)

    natural[...] = lax.dot_general(
        jnp.broadcast_to(picked[...].astype(F32), (8, SEL)),
        jnp.full((8, HEAD_DIM), 0.125, F32), (((0,), (0,)), ((), ())),
        precision=HIGH, preferred_element_type=F32,
    )
    for zz in range(NZ):
        for xx in range(NX):
            at = (zz * NX + xx) * OWN
            back = (xx * NZ + zz) * OWN
            rows_of[at : at + OWN] = natural[back : back + OWN].astype(jnp.int32)

    def tokens(i):
        rows = pl.ds(pl.multiple_of(i * 128, 128), 128)
        row = rows_of[rows]
        slot_of = lax.shift_right_logical(row, 10)
        shift = jnp.zeros_like(row)
        bottom = jnp.zeros_like(row)
        for slot in range(NCH):
            mine = slot_of == slot
            shift = jnp.where(mine, shifts[slot], shift)
            bottom = jnp.where(mine, bottoms[slot], bottom)
        codes[rows] = row + shift
        lows[rows] = bottom
        qcos[rows], qsin[rows] = circle(row + shift - bottom)

    each(0, SEL // 128, tokens)

    def qkv_on(k):
        qkv_w.enter_in(k).wait_recv()
        qkv_w.go_near(k)

    each(1, NX, qkv_on)

    each(0, NX, qkv_w.step_near)
    own_copies[2].wait()
    each(1, NZ, lambda k: out_w.enter_in(k).wait_recv())
    each(0, NX, qkv_w.step_far)
    each(0, 2, out_w.go_near)
    ffn_w.go_near(0)

    own_copies[0].wait()
    each(1, NZ, lambda k: hz_in(k).wait_recv())
    qkv_w.arrive()

    low_x = lanes(NZ * OWN) < HEAD_DIM // 2

    def project(k):
        at = xa(k)
        rows = hid[...].reshape(NZ * OWN, D)
        kv = jnp.dot(
            rows, w4buf[:, at, :256].reshape(D, HEAD_DIM), preferred_element_type=F32
        )
        packed = w4buf[:, at, 256:].reshape(D // 2, HEAD_DIM)
        upper = jnp.concatenate(
            [rows[:, c * 256 : c * 256 + 128] for c in range(NDP)], axis=1
        )
        lower = jnp.concatenate(
            [rows[:, c * 256 + 128 : (c + 1) * 256] for c in range(NDP)], axis=1
        )
        a = jnp.dot(upper, packed, preferred_element_type=F32)
        b = jnp.dot(lower, packed, preferred_element_type=F32)
        q = a + pltpu.roll(b, 64, 1)
        psend[at, :, :HEAD_DIM] = kv.astype(BF16)
        psend[at, :, HEAD_DIM:] = jnp.where(low_x, q, pltpu.roll(q, 64, 1)).astype(BF16)
        squares[0] += jnp.where(low_x, q * q, 0.0)
        squares[1] += jnp.where(low_x, kv * kv, 0.0)

    low_f = lanes(GRP) < HEAD_DIM // 2

    def take(j, blocks):
        p = xa(NX - j)
        rows = blocks[p]
        q = rows[:, HEAD_DIM:].astype(F32)
        qpk[p] = jnp.where(low_f, q[:GRP], q[GRP:]).astype(BF16)
        at = pl.ds(pl.multiple_of(p * OWN, OWN), OWN)
        kvs[:, at] = rows[:, :HEAD_DIM].reshape(NZ, OWN, HEAD_DIM)
        each(1, NZ, lambda k: qz(j, k).start())

    def project_send(k):
        project(k)
        px(k).start()

    squares[...] = jnp.zeros_like(squares)
    project(0)
    take(0, psend)
    each(1, NX, project_send)
    lane_own = lanes(OWN)
    mine = jnp.zeros((OWN, HEAD_DIM), F32)
    for kind in range(2):
        sums = jnp.sum(squares[kind], axis=1, keepdims=True)
        for g in range(NZ):
            mine = jnp.where(lane_own == 4 * g + 2 * kind, sums[g * OWN : (g + 1) * OWN], mine)
    stat[pl.ds(x, 1)] = mine[None]
    each(1, NX, lambda k: stx(k).start())
    each(1, NX, lambda k: vx(k).start())
    ffn_w.enter(2).start()
    for k in (1, 3):
        ffn_w.enter_in(k).wait_recv()
        ffn_w.go_near(k)

    def taken(j):
        px_in(j).wait_recv()
        take(j, precv)

    each(1, NX, taken)
    each(1, NX, lambda k: stx_in(k).wait_recv())
    both = stat[0]
    for p in range(1, NX):
        both += pltpu.roll(stat[p], 32 * p, 1)
    high = both.astype(BF16).astype(F32)
    kvs[:, GRP:] = jnp.broadcast_to(
        (high + pltpu.roll(both - high, 1, 1)).astype(BF16)[None], (NZ, OWN, HEAD_DIM)
    )
    each(1, NZ, lambda k: cz(k).start())
    qrecv[pl.ds(z, 1)] = qpk[...][None]
    kvrecv[pl.ds(z, 1)] = kvs[pl.ds(z, 1)]
    each(0, 2, out_w.step_near)

    grp_rows = pl.ds(pl.multiple_of(z * GRP, GRP), GRP)
    for block in range(NX):
        first = (block * NZ + z) * CTX
        slot = lax.div(first, CH)
        later = lax.min(slot + 1, NCH - 1)
        row = first + lax.broadcasted_iota(jnp.int32, (1, CTX), 1)
        code = jnp.where(row < (slot + 1) * CH, sbase[slot], sbase[later]) + row
        hit = jnp.max(
            jnp.where(rows_of[:, 0:1] == row, 1, 0), axis=0, keepdims=True
        )
        kcode[:, block * CTX : (block + 1) * CTX] = jnp.where(hit > 0, DEAD, code)
    corner = lax.broadcasted_iota(jnp.int32, (GRP, HEAD_DIM), 0) == lanes(GRP)
    kcode[:, CACHED:KEYS] = jnp.where(
        lanes(1) < GRP,
        jnp.sum(jnp.where(corner, codes[grp_rows], 0), axis=0, keepdims=True),
        DEAD,
    )
    kall[CACHED:KEYS, :] = jnp.zeros((KEYS - CACHED, PART), BF16)
    vall[CACHED:KEYS, :] = jnp.zeros((KEYS - CACHED, PART), BF16)

    own_copies[4].wait()
    each(1, NX, lambda k: kx_in(k).wait_recv())

    def turn(block):
        first = (block * NZ + z) * CTX
        slot = lax.div(first, CH)
        later = lax.min(slot + 1, NCH - 1)
        row = first + lax.broadcasted_iota(jnp.int32, (CTX, HEAD_DIM), 0)
        here = row < (slot + 1) * CH
        cosine = jnp.where(here, scos[pl.ds(slot, 1), :], scos[pl.ds(later, 1), :])
        sine = jnp.where(here, ssin[pl.ds(slot, 1), :], ssin[pl.ds(later, 1), :])
        for h in range(HEADS):
            cols = slice(h * HEAD_DIM, (h + 1) * HEAD_DIM)
            v = kraw[block, :, cols].astype(F32)
            kall[key_rows(block), cols] = (v * cosine + pltpu.roll(v, 64, 1) * sine).astype(BF16)

    each(0, NX, turn)
    def mask(i):
        rows = pl.ds(pl.multiple_of(i * 128, 128), 128)
        code = kcode[...]
        usable = (code <= codes[rows, 0:1]) & (code >= lows[rows, 0:1])
        bias[rows] = jnp.where(usable, 0.0, NEGATIVE)

    each(0, SEL // 128, mask)

    each(0, NX, lambda j: each(1, NZ, lambda k: qz_in(j, k).wait_recv()))
    each(1, NZ, lambda k: cz_in(k).wait_recv())
    low = lanes(SEL // 2) < HEAD_DIM // 2

    def in_order(t):
        return jnp.concatenate(
            [
                t[p * GRP + g * OWN : p * GRP + (g + 1) * OWN]
                for g in range(NZ // 2)
                for p in range(NX)
            ],
            axis=0,
        )

    def q_head(h):
        a = qrecv[2 * h].reshape(SEL // 2, HEAD_DIM).astype(F32)
        b = qrecv[2 * h + 1].reshape(SEL // 2, HEAD_DIM).astype(F32)
        top = jnp.where(low, a, pltpu.roll(b, 64, 1))
        bottom = jnp.where(low, pltpu.roll(a, 64, 1), b)
        return in_order(top), in_order(bottom)

    def f_head(h):
        a = kvrecv[2 * h, :GRP].astype(F32)
        b = kvrecv[2 * h + 1, :GRP].astype(F32)
        return jnp.where(low_f, a, pltpu.roll(b, 64, 1)), jnp.where(low_f, pltpu.roll(a, 64, 1), b)

    each(0, 2, out_w.step_far)
    total = jnp.zeros((OWN, HEAD_DIM), F32)
    for p in range(NZ):
        total += kvrecv[p, GRP:].astype(F32)
    total = total + pltpu.roll(total, HEAD_DIM - 1, 1)
    even = lax.rem(lane_own, 2) == 0
    factor = lax.rsqrt(jnp.where(even, total, 1.0) * (1.0 / D) + EPSILON)
    for g in range(NZ):
        for p in range(NX):
            at = (g * NX + p) * OWN
            col = 32 * p + 4 * g
            sq[0, at : at + OWN] = jnp.broadcast_to(
                factor[:, col : col + 1] * SCORE, (OWN, HEAD_DIM)
            )
            sq[1, at : at + OWN] = jnp.broadcast_to(factor[:, col + 2 : col + 3], (OWN, HEAD_DIM))
    for h in range(HEADS):
        cols = pl.ds(pl.multiple_of(x * PART + h * HEAD_DIM, HEAD_DIM), HEAD_DIM)
        top, bottom = q_head(h)
        gain = gains[0:1, cols]
        for part, rows in ((top, slice(0, SEL // 2)), (bottom, slice(SEL // 2, SEL))):
            v = part * sq[0, rows] * gain
            qh[h, rows] = (v * qcos[rows] + pltpu.roll(v, 64, 1) * qsin[rows]).astype(BF16)
        key, value = f_head(h)
        vall[CACHED : CACHED + GRP, h * HEAD_DIM : (h + 1) * HEAD_DIM] = value.astype(BF16)
        v = key * sq[1, grp_rows] * gains[1:2, cols]
        v = (v * qcos[grp_rows] + pltpu.roll(v, 64, 1) * qsin[grp_rows]).astype(BF16)
        kall[CACHED : CACHED + GRP, h * HEAD_DIM : (h + 1) * HEAD_DIM] = v
        kf[:, :, h * HEAD_DIM : (h + 1) * HEAD_DIM] = v.reshape(NX, OWN, HEAD_DIM)
    each(1, NX, lambda k: fx(k).start())
    frecv[pl.ds(x, 1)] = kf[pl.ds(x, 1)]

    own_copies[5].wait()
    each(1, NX, lambda k: vx_in(k).wait_recv())

    lane = lanes(128)

    def attend(part):
        rows = pl.ds(pl.multiple_of(part * 128, 128), 128)
        two = pl.ds(part * 2, 2)
        marks = jnp.zeros((128, HEAD_DIM), F32)
        for h in range(HEADS):
            cols = slice(h * HEAD_DIM, (h + 1) * HEAD_DIM)
            scores = lax.dot_general(
                qh[h, rows], kall[:, cols], (((1,), (1,)), ((), ())), preferred_element_type=F32
            ) + bias[rows]
            most = jnp.maximum(jnp.max(scores, axis=1, keepdims=True), FLOOR)
            most = most.astype(BF16).astype(F32)
            weight = jnp.exp2(scores - most)
            mass = jnp.sum(weight, axis=1, keepdims=True)
            mixed = jnp.dot(weight.astype(BF16), vall[:, cols], preferred_element_type=F32)
            obuf[two, h * GRP : (h + 1) * GRP, :] = mixed.astype(BF16).reshape(2, GRP, HEAD_DIM)
            high = mass.astype(BF16).astype(F32)
            marks = jnp.where(lane == h, most, marks)
            marks = jnp.where(lane == h + HEADS, high, marks)
            marks = jnp.where(lane == h + 2 * HEADS, mass - high, marks)
        for side in range(2):
            packed = marks[side * GRP : side * GRP + OWN]
            for g in range(1, NX):
                at = side * GRP + g * OWN
                packed += pltpu.roll(marks[at : at + OWN], 32 * g, 1)
            obuf[part * 2 + side, HEADS * GRP :, :] = packed.astype(BF16)

    def attend_far(i):
        part = lax.rem(lax.div(z, 2) + 1 + lax.rem(i + 1, 3), NZ // 2)
        attend(part)
        offset = lax.rem(2 * part + NZ - z, NZ)
        oex(offset).start()
        oex(lax.rem(offset + 1, NZ)).start()
        ffn_w.step_near(i + lax.div(i, 2))

    attend_far(0)
    ffn_w.enter_in(2).wait_recv()
    ffn_w.go_near(2)
    each(1, 3, attend_far)
    attend(lax.div(z, 2))
    beside = lax.rem(NZ + 1 - 2 * lax.rem(z, 2), NZ)
    oex(beside).start()
    orecv[pl.ds(z, 1)] = obuf[pl.ds(z, 1)]
    out_w.arrive()
    each(1, NZ, lambda k: oex_in(k).wait_recv())

    def marks_of(p):
        return orecv[p, HEADS * GRP :, :].astype(F32)

    peak = marks_of(0)
    for p in range(1, NZ):
        peak = jnp.maximum(peak, marks_of(p))
    mass = jnp.zeros((OWN, HEAD_DIM), F32)
    for p in range(NZ):
        marks = marks_of(p)
        amount = pltpu.roll(marks, HEAD_DIM - HEADS, 1) + pltpu.roll(
            marks, HEAD_DIM - 2 * HEADS, 1
        )
        mass += jnp.exp2(marks - peak) * amount
    valid = lax.rem(lane_own, 32) < HEADS
    inverse = 1.0 / jnp.where(valid, mass, 1.0)
    heads = [jnp.zeros((GRP, HEAD_DIM), F32) for _ in range(HEADS)]
    for p in range(NZ):
        share = jnp.exp2(marks_of(p) - peak) * inverse
        for h in range(HEADS):
            part = orecv[p, h * GRP : (h + 1) * GRP, :].astype(F32)
            weight = jnp.concatenate(
                [
                    jnp.broadcast_to(
                        share[:, 32 * g + h : 32 * g + h + 1], (OWN, HEAD_DIM)
                    )
                    for g in range(NX)
                ],
                axis=0,
            )
            heads[h] += part * weight
    attn = jnp.concatenate(heads, axis=1).astype(BF16)

    def out_block(c):
        got = jnp.dot(attn, wobuf[c].reshape(PART, 256), preferred_element_type=F32)
        cols = pl.ds(pl.multiple_of(c * 256, 256), 256)
        ysend[:, :, cols] = got.astype(BF16).reshape(NX, OWN, 256)

    each(0, NDP, out_block)
    each(1, NX, lambda k: yx(k).start())
    yrecv[pl.ds(x, 1)] = ysend[pl.ds(x, 1)]
    ffn_w.step_near(2)
    for k in (0, 1, 3):
        ffn_w.step_far(k)
    each(1, NX, lambda k: yx_in(k).wait_recv())
    y = yrecv[0].astype(F32)
    for p in range(1, NX):
        y += yrecv[p].astype(F32)
    y = y * lax.rsqrt(jnp.mean(y * y, axis=1, keepdims=True) + EPSILON) * gains[2:3, :]
    following = (hid[z].astype(F32) + y).astype(BF16)
    hn[...] = following
    each(1, NZ, lambda k: nz(k).start())
    hbuf[pl.ds(z, 1)] = following[None]
    ffn_w.step_far(2)

    each(1, NZ, lambda k: nz_in(k).wait_recv())
    ffn_w.arrive()

    def gate(c):
        rows = hbuf[...].reshape(NZ * OWN, D)
        g = jnp.dot(rows, wbuf[:, c, 0].reshape(D, 256), preferred_element_type=F32)
        u = jnp.dot(rows, wbuf[:, c, 1].reshape(D, 256), preferred_element_type=F32)
        cols = pl.ds(pl.multiple_of(c * 256, 256), 256)
        act[:, cols] = (jax.nn.silu(g) * u).astype(BF16)

    each(0, NX, gate)

    def down_half(half):
        def down(c):
            weights = wbuf[half * 4 + c, :, 2].reshape(NX * 256, 256)
            got = jnp.dot(act[...], weights, preferred_element_type=F32)
            cols = pl.ds(pl.multiple_of(c * 256, 256), 256)
            dsend[half, :, :, cols] = got.astype(BF16).reshape(NZ, OWN, 256)

        each(0, 4, down)
        each(1, NZ, lambda k: dz(half, k).start())

    each(0, 2, down_half)
    for half in range(2):
        drecv[half, pl.ds(z, 1)] = dsend[half, pl.ds(z, 1)]

    each(1, NX, lambda k: fx_in(k).wait_recv())
    for p in range(NX):
        fresh[:, p * PART : (p + 1) * PART] = frecv[p]

    each(0, 2, lambda half: each(1, NZ, lambda k: dz_in(half, k).wait_recv()))
    halves = []
    for half in range(2):
        t = drecv[half, 0].astype(F32)
        for p in range(1, NZ):
            t += drecv[half, p].astype(F32)
        halves.append(t)
    t = jnp.concatenate(halves, axis=1)
    t = t * lax.rsqrt(jnp.mean(t * t, axis=1, keepdims=True) + EPSILON) * gains[3:4, :]
    out[...] = (hn[...].astype(F32) + t).astype(BF16)

    each(0, NX, lambda j: each(1, NZ, lambda k: qz(j, k).wait_send()))
    for copy in (hz, cz, oex, nz):
        each(1, NZ, lambda k, copy=copy: copy(k).wait_send())
    for copy in (kx, vx, px, stx, fx, yx):
        each(1, NX, lambda k, copy=copy: copy(k).wait_send())
    each(0, 2, lambda half: each(1, NZ, lambda k: dz(half, k).wait_send()))
    for weights in (qkv_w, out_w, ffn_w):
        weights.finish()


def layer(
    hidden_sel, picked, order, lengths, offsets, cache_keys, cache_values, w_qkv, w_out,
    w_gate_up, w_down, gains,
):
    w4 = jnp.concatenate(
        [
            jnp.concatenate([w_qkv[1], w_qkv[2]], axis=1),
            jnp.concatenate([w_qkv[0, :128], w_qkv[0, 128:]], axis=1),
        ],
        axis=0,
    )

    vmem = pl.BlockSpec(memory_space=pltpu.VMEM)
    far = pl.BlockSpec(memory_space=pl.ANY)
    smem = pl.BlockSpec(memory_space=pltpu.SMEM)
    dma = pltpu.SemaphoreType.DMA

    def spread(peers, slots):
        return (
            dma((peers,)), dma((peers,)), dma((slots, NY)), dma((slots, NY)), dma((slots,)),
            dma((slots, NY)), dma((slots, NY)),
        )

    out, fresh = pl.pallas_call(
        kernel,
        out_shape=(
            jax.ShapeDtypeStruct((OWN, D), BF16),
            jax.ShapeDtypeStruct((OWN, D), BF16),
        ),
        in_specs=[vmem, far, far, far, far, far, far, vmem, vmem, smem, smem, smem],
        out_specs=(vmem, vmem),
        scratch_shapes=[
            pltpu.VMEM((NZ, OWN, D), BF16),
            pltpu.VMEM((NDP, NX, 384, HEAD_DIM), BF16),
            pltpu.VMEM((NDP, NZ, 64, 256), BF16),
            pltpu.VMEM((NDP, NX, 3, 256, 256), BF16),
            pltpu.VMEM((NX, CTX, PART), BF16),
            pltpu.VMEM((KEYS, PART), BF16),
            pltpu.VMEM((KEYS, PART), BF16),
            pltpu.VMEM((1, KEYS), jnp.int32),
            pltpu.VMEM((NX, NZ * OWN, 256), BF16),
            pltpu.VMEM((NX, NZ * OWN, 256), BF16),
            pltpu.VMEM((NX, GRP, HEAD_DIM), BF16),
            pltpu.VMEM((NZ, GRP + OWN, HEAD_DIM), BF16),
            pltpu.VMEM((NZ, NX, GRP, HEAD_DIM), BF16),
            pltpu.VMEM((NZ, GRP + OWN, HEAD_DIM), BF16),
            pltpu.VMEM((2, SEL, HEAD_DIM), F32),
            pltpu.VMEM((NX, OWN, HEAD_DIM), F32),
            pltpu.VMEM((HEADS, SEL, HEAD_DIM), BF16),
            pltpu.VMEM((NX, OWN, PART), BF16),
            pltpu.VMEM((NX, OWN, PART), BF16),
            pltpu.VMEM((NZ, HEADS * GRP + OWN, HEAD_DIM), BF16),
            pltpu.VMEM((NZ, HEADS * GRP + OWN, HEAD_DIM), BF16),
            pltpu.VMEM((NX, OWN, D), BF16),
            pltpu.VMEM((NX, OWN, D), BF16),
            pltpu.VMEM((OWN, D), BF16),
            pltpu.VMEM((NZ, OWN, D), BF16),
            pltpu.VMEM((NZ * OWN, NX * 256), BF16),
            pltpu.VMEM((2, NZ, OWN, D // 2), BF16),
            pltpu.VMEM((2, NZ, OWN, D // 2), BF16),
            pltpu.VMEM((SEL, HEAD_DIM), F32),
            pltpu.VMEM((SEL, HEAD_DIM), jnp.int32),
            pltpu.VMEM((SEL, HEAD_DIM), jnp.int32),
            pltpu.VMEM((SEL, HEAD_DIM), jnp.int32),
            pltpu.VMEM((SEL, HEAD_DIM), F32),
            pltpu.VMEM((SEL, HEAD_DIM), F32),
            pltpu.VMEM((16, HEAD_DIM), F32),
            pltpu.VMEM((16, HEAD_DIM), F32),
            pltpu.SMEM((16,), jnp.int32),
            pltpu.VMEM((SEL, KEYS), F32),
            pltpu.VMEM((2, NZ * OWN, HEAD_DIM), F32),
            dma((NZ,)), dma((NZ,)),
            spread(NX, NX),
            spread(NZ, 2),
            spread(NX, NX),
            dma((NX,)), dma((NX,)),
            dma((NX,)), dma((NX,)),
            dma((NX,)), dma((NX,)),
            dma((NX, NZ)), dma((NX, NZ)),
            dma((NZ,)), dma((NZ,)),
            dma((NX,)), dma((NX,)),
            dma((NX,)), dma((NX,)),
            dma((NZ,)), dma((NZ,)),
            dma((NX,)), dma((NX,)),
            dma((NZ,)), dma((NZ,)),
            dma((2, NZ)), dma((2, NZ)),
            dma((7,)),
        ],
        compiler_params=pltpu.CompilerParams(
            collective_id=0, has_side_effects=True, vmem_limit_bytes=56 << 20
        ),
    )(
        hidden_sel[0], cache_keys[0], cache_values[0], w4, w_out, w_gate_up, w_down, gains,
        picked, order, lengths, offsets,
    )
    return (out[None], fresh[None])


def solution(mesh):
    placed = (
        P("dp", "tensor", None),
        P("dp", None),
        P("dp", None),
        P("dp", None),
        P("dp", None),
        P("dp", "tensor", None),
        P("dp", "tensor", None),
        P(None, "dp", "tensor"),
        P("tensor", "dp"),
        P(None, "dp", "tensor"),
        P("tensor", "dp"),
        P(),
    )
    return jax.shard_map(
        layer,
        mesh=mesh,
        in_specs=placed,
        out_specs=(P("dp", "tensor", None), P("dp", "tensor", None)),
        check_vma=False,
    )
```

```python
import math

import jax
import jax.numpy as jnp
import numpy as np
from jax import lax
from jax.experimental import pallas as pl
from jax.experimental.pallas import tpu as pltpu
from jax.sharding import PartitionSpec as P

HEAD_DIM = 128
CH = 1024
NCH = 12
REQS = 3
NX = 4
NZ = 8
NDP = 8
NY = 4
D = 2048
PART = D // NX
HEADS = PART // HEAD_DIM
OWN = 16
GRP = NX * OWN
SEL = NZ * GRP
CTX = 384
CACHED = NX * CTX
KEYS = CACHED + 128
SPAN = 1 << 14
DEAD = 1 << 30

THETA = 500000.0
EPSILON = 1e-06
NEGATIVE = -1e30
FLOOR = -1e20
SCORE = HEAD_DIM ** (-0.5) * math.log2(math.e)
LAP_A = 6.28125
LAP_B = 0.0019340515136718750
LAP_C = 2.0 * math.pi - LAP_A - LAP_B
RATES = [
    float(np.float32(math.exp(-2.0 * j / HEAD_DIM * math.log(THETA)))) for j in range(HEAD_DIM // 2)
]
MESH = pl.DeviceIdType.MESH
F32, BF16 = jnp.float32, jnp.bfloat16
HIGH = lax.Precision.HIGHEST


def lanes(rows):
    return lax.broadcasted_iota(jnp.int32, (rows, HEAD_DIM), 1)


def kernel(
    hidden,
    keys,
    values,
    w4,
    wo,
    wgu,
    wd,
    gains,
    picked,
    order,
    lengths,
    offsets,
    both_out,
    hid,
    w4buf,
    wobuf,
    wbuf,
    kraw,
    kall,
    vall,
    kcode,
    psend,
    precv,
    qpk,
    kvs,
    qrecv,
    kvrecv,
    sq,
    stat,
    qh,
    kf,
    frecv,
    obuf,
    orecv,
    ysend,
    yrecv,
    hn,
    hbuf,
    act,
    dsend,
    drecv,
    natural,
    rows_of,
    codes,
    lows,
    qcos,
    qsin,
    scos,
    ssin,
    sbase,
    bias,
    squares,
    hz_s,
    hz_r,
    w4_sems,
    wo_sems,
    wm_sems,
    k_s,
    k_r,
    v_s,
    v_r,
    p_s,
    p_r,
    q_s,
    q_r,
    c_s,
    c_r,
    st_s,
    st_r,
    f_s,
    f_r,
    o_s,
    o_r,
    y_s,
    y_r,
    n_s,
    n_r,
    d_s,
    d_r,
    loc,
):
    tens = lax.axis_index("tensor")
    dp = lax.axis_index("dp")
    x = lax.div(tens, NZ)
    z = lax.rem(tens, NZ)
    core = lax.rem(dp, 2)
    sib = dp + 1 - 2 * core

    def xa(k):
        return lax.rem(x + k, NX)

    def za(k):
        return lax.rem(z + k, NZ)

    def da(k):
        return lax.rem(dp + k, NDP)

    def zdev(k):
        return {"tensor": x * NZ + za(k)}

    def xdev(k):
        return {"tensor": xa(k) * NZ + z}

    def send(src, dst, ssem, rsem, dev):
        return pltpu.make_async_remote_copy(
            src_ref=src, dst_ref=dst, send_sem=ssem, recv_sem=rsem, device_id=dev,
            device_id_type=MESH,
        )

    def each(first, last, body):
        def step(k, carry):
            body(k)
            return carry

        lax.fori_loop(first, last, step, 0)

    class Spread:
        def __init__(self, sems, slots, source, first, peers, entry, entry_in, at):
            (self.e_s, self.e_r, self.n_s, self.y_r, self.r_s, self.s_s, self.s_r) = sems
            self.slots, self.source, self.first, self.peers = slots, source, first, peers
            self.entry, self.entry_in, self.at = entry, entry_in, at

        def enter(self, k):
            return send(self.source, self.entry, self.e_s.at[k], self.e_r.at[k], self.first(k))

        def enter_in(self, k):
            at = self.entry_in(k)
            return send(at, at, self.e_s.at[k], self.e_r.at[k], self.first(k))

        def near(self, k, j):
            at = self.at(dp, k)
            return send(at, at, self.n_s.at[k, j], self.y_r.at[k, j], {"dp": da(2 * j)})

        def near_in(self, k, j):
            at = self.at(da(NDP - 2 * j), k)
            return send(at, at, self.n_s.at[k, j], self.y_r.at[k, j], {"dp": da(2 * j)})

        def way(self, k):
            return 1 + 2 * lax.div(k, self.slots // 2)

        def relay(self, k):
            j = self.way(k)
            at = self.at(da(NDP - 2 * j), k)
            return send(at, at, self.r_s.at[k], self.y_r.at[k, 2], {"dp": da(2 * j)})

        def relay_in(self, k):
            at = self.at(da(4), k)
            return send(at, at, self.r_s.at[k], self.y_r.at[k, 2], {"dp": da(2)})

        def side(self, k, j):
            at = self.at(da(NDP - 2 * j), k)
            return send(at, at, self.s_s.at[k, j], self.s_r.at[k, j], {"dp": sib})

        def side_in(self, k, j):
            at = self.at(lax.rem(sib + NDP - 2 * j, NDP), k)
            return send(at, at, self.s_s.at[k, j], self.s_r.at[k, j], {"dp": sib})

        def start(self):
            each(1, self.peers, lambda k: self.enter(k).start())

        def go_near(self, k):
            self.near(k, 1).start()
            self.near(k, 3).start()
            self.side(k, 0).start()

        def step_near(self, k):
            self.near_in(k, 1).wait_recv()
            self.near_in(k, 3).wait_recv()
            self.relay(k).start()
            self.side(k, 1).start()
            self.side(k, 3).start()

        def step_far(self, k):
            self.relay_in(k).wait_recv()
            self.side(k, 2).start()

        def arrive(self):
            each(0, self.slots, lambda k: each(0, NY, lambda j: self.side_in(k, j).wait_recv()))

        def finish(self):
            each(1, self.peers, lambda k: self.enter(k).wait_send())

            def one(k):
                self.near(k, 1).wait_send()
                self.near(k, 3).wait_send()
                self.relay(k).wait_send()
                each(0, NY, lambda j: self.side(k, j).wait_send())

            each(0, self.slots, one)

    def x_slot(buf):
        return lambda d, k: buf.at[d, xa(NX - k)]

    qkv_w = Spread(
        w4_sems, NX, w4, xdev, NX, w4buf.at[dp, x], lambda k: w4buf.at[dp, xa(NX - k)],
        x_slot(w4buf),
    )
    ffn_w = Spread(
        wm_sems, NX, wbuf.at[dp, x], xdev, NX, wbuf.at[dp, x], lambda k: wbuf.at[dp, xa(NX - k)],
        x_slot(wbuf),
    )
    out_w = Spread(
        wo_sems, 2, wo, zdev, NZ, wobuf.at[dp, z], lambda k: wobuf.at[dp, za(NZ - k)],
        lambda d, k: wobuf.at[d, pl.ds(4 * k, 4)],
    )

    def hz(k):
        return send(hidden, hid.at[z], hz_s.at[k], hz_r.at[k], zdev(k))

    def hz_in(k):
        at = hid.at[za(NZ - k)]
        return send(at, at, hz_s.at[k], hz_r.at[k], zdev(k))

    def columns(at):
        return pl.ds(pl.multiple_of(at * PART, PART), PART)

    def key_rows(at):
        return pl.ds(pl.multiple_of(at * CTX, 128), CTX)

    def kx(k):
        return send(keys.at[:, columns(xa(k))], kraw.at[x], k_s.at[k], k_r.at[k], xdev(k))

    def kx_in(k):
        at = kraw.at[xa(NX - k)]
        return send(at, at, k_s.at[k], k_r.at[k], xdev(k))

    def vx(k):
        return send(
            values.at[:, columns(xa(k))], vall.at[key_rows(x)], v_s.at[k], v_r.at[k], xdev(k)
        )

    def vx_in(k):
        at = vall.at[key_rows(xa(NX - k))]
        return send(at, at, v_s.at[k], v_r.at[k], xdev(k))

    def px(k):
        return send(psend.at[xa(k)], precv.at[x], p_s.at[k], p_r.at[k], xdev(k))

    def px_in(k):
        at = precv.at[xa(NX - k)]
        return send(at, at, p_s.at[k], p_r.at[k], xdev(k))

    def qz(j, k):
        p = xa(NX - j)
        return send(qpk.at[p], qrecv.at[z, p], q_s.at[j, k], q_r.at[j, k], zdev(k))

    def qz_in(j, k):
        at = qrecv.at[za(NZ - k), xa(NX - j)]
        return send(at, at, q_s.at[j, k], q_r.at[j, k], zdev(k))

    def cz(k):
        return send(kvs.at[za(k)], kvrecv.at[z], c_s.at[k], c_r.at[k], zdev(k))

    def cz_in(k):
        at = kvrecv.at[za(NZ - k)]
        return send(at, at, c_s.at[k], c_r.at[k], zdev(k))

    def stx(k):
        return send(stat.at[x], stat.at[x], st_s.at[k], st_r.at[k], xdev(k))

    def stx_in(k):
        at = stat.at[xa(NX - k)]
        return send(at, at, st_s.at[k], st_r.at[k], xdev(k))

    def fx(k):
        return send(kf.at[xa(k)], frecv.at[x], f_s.at[k], f_r.at[k], xdev(k))

    def fx_in(k):
        at = frecv.at[xa(NX - k)]
        return send(at, at, f_s.at[k], f_r.at[k], xdev(k))

    def oex(k):
        return send(obuf.at[za(k)], orecv.at[z], o_s.at[k], o_r.at[k], zdev(k))

    def oex_in(k):
        at = orecv.at[za(NZ - k)]
        return send(at, at, o_s.at[k], o_r.at[k], zdev(k))

    def yx(k):
        return send(ysend.at[xa(k)], yrecv.at[x], y_s.at[k], y_r.at[k], xdev(k))

    def yx_in(k):
        at = yrecv.at[xa(NX - k)]
        return send(at, at, y_s.at[k], y_r.at[k], xdev(k))

    def nz(k):
        return send(hn, hbuf.at[z], n_s.at[k], n_r.at[k], zdev(k))

    def nz_in(k):
        at = hbuf.at[za(NZ - k)]
        return send(at, at, n_s.at[k], n_r.at[k], zdev(k))

    def dz(half, k):
        return send(
            dsend.at[half, za(k)], drecv.at[half, z], d_s.at[half, k], d_r.at[half, k], zdev(k)
        )

    def dz_in(half, k):
        at = drecv.at[half, za(NZ - k)]
        return send(at, at, d_s.at[half, k], d_r.at[half, k], zdev(k))

    own_copies = [
        pltpu.make_async_copy(hidden, hid.at[z], loc.at[0]),
        pltpu.make_async_copy(w4, w4buf.at[dp, x], loc.at[1]),
        pltpu.make_async_copy(wo, wobuf.at[dp, z], loc.at[2]),
        pltpu.make_async_copy(wgu, wbuf.at[dp, x, pl.ds(0, 2)], loc.at[3]),
        pltpu.make_async_copy(keys.at[:, columns(x)], kraw.at[x], loc.at[4]),
        pltpu.make_async_copy(values.at[:, columns(x)], vall.at[key_rows(x)], loc.at[5]),
        pltpu.make_async_copy(wd, wbuf.at[dp, x, 2], loc.at[6]),
    ]
    for copy in own_copies:
        copy.start()

    barrier = pltpu.get_barrier_semaphore()

    def greet(dev):
        pl.semaphore_signal(barrier, inc=1, device_id=dev, device_id_type=MESH)

    each(1, NZ, lambda k: greet(zdev(k)))
    each(1, NX, lambda k: greet(xdev(k)))
    greet({"dp": da(2)})
    greet({"dp": da(6)})
    greet({"dp": sib})
    pl.semaphore_wait(barrier, NZ + NX + 1)

    qkv_w.start()
    own_copies[1].wait()
    qkv_w.go_near(0)
    each(1, NZ, lambda k: hz(k).start())
    own_copies[3].wait()
    own_copies[6].wait()
    ffn_w.enter(1).start()
    ffn_w.enter(3).start()
    each(1, NX, lambda k: kx(k).start())
    out_w.start()

    end_a = lengths[0, 0]
    end_b = end_a + lengths[0, 1]
    span = lax.broadcasted_iota(jnp.int32, (16, HEAD_DIM), 0)
    turns = jnp.zeros((16, HEAD_DIM), jnp.int32)
    shifts, bottoms = [], []
    for slot in range(NCH):
        place = order[0, slot]
        second, third = place >= end_a, place >= end_b
        start = jnp.where(third, end_b, jnp.where(second, end_a, 0))
        moved = jnp.where(third, offsets[0, 2], jnp.where(second, offsets[0, 1], offsets[0, 0]))
        bottom = jnp.where(third, 2 * SPAN, jnp.where(second, SPAN, 0))
        base = moved + (place - start) * CH
        sbase[slot] = base + bottom - slot * CH
        shifts.append(base + bottom - slot * CH)
        bottoms.append(bottom)
        turns = jnp.where(span == slot, base, turns)

    turn_lane = lax.rem(lanes(8), HEAD_DIM // 2)
    rates = jnp.zeros((8, HEAD_DIM), F32)
    for j in range(HEAD_DIM // 2):
        rates = jnp.where(turn_lane == j, RATES[j], rates)

    def circle(position):
        angle = position.astype(F32) * rates[0:1, :]
        laps = jnp.floor(angle * (0.5 / math.pi) + 0.5)
        angle = ((angle - laps * LAP_A) - laps * LAP_B) - laps * LAP_C
        sine = jnp.sin(angle)
        left = lax.broadcasted_iota(jnp.int32, position.shape, 1) < HEAD_DIM // 2
        return jnp.cos(angle), jnp.where(left, -sine, sine)

    scos[...], ssin[...] = circle(turns)

    natural[...] = lax.dot_general(
        jnp.broadcast_to(picked[...].astype(F32), (8, SEL)),
        jnp.full((8, HEAD_DIM), 0.125, F32), (((0,), (0,)), ((), ())),
        precision=HIGH, preferred_element_type=F32,
    )
    for zz in range(NZ):
        for xx in range(NX):
            at = (zz * NX + xx) * OWN
            back = (xx * NZ + zz) * OWN
            rows_of[at : at + OWN] = natural[back : back + OWN].astype(jnp.int32)

    def tokens(i):
        rows = pl.ds(pl.multiple_of(i * 128, 128), 128)
        row = rows_of[rows]
        slot_of = lax.shift_right_logical(row, 10)
        shift = jnp.zeros_like(row)
        bottom = jnp.zeros_like(row)
        for slot in range(NCH):
            mine = slot_of == slot
            shift = jnp.where(mine, shifts[slot], shift)
            bottom = jnp.where(mine, bottoms[slot], bottom)
        codes[rows] = row + shift
        lows[rows] = bottom
        qcos[rows], qsin[rows] = circle(row + shift - bottom)

    each(0, SEL // 128, tokens)

    def qkv_on(k):
        qkv_w.enter_in(k).wait_recv()
        qkv_w.go_near(k)

    each(1, NX, qkv_on)

    each(0, NX, qkv_w.step_near)
    own_copies[2].wait()
    each(1, NZ, lambda k: out_w.enter_in(k).wait_recv())
    each(0, NX, qkv_w.step_far)
    each(0, 2, out_w.go_near)
    ffn_w.go_near(0)

    own_copies[0].wait()
    each(1, NZ, lambda k: hz_in(k).wait_recv())
    qkv_w.arrive()

    low_x = lanes(NZ * OWN) < HEAD_DIM // 2

    def project(k):
        at = xa(k)
        rows = hid[...].reshape(NZ * OWN, D)
        kv = jnp.zeros((NZ * OWN, HEAD_DIM), F32)
        qk = jnp.zeros((NZ * OWN, HEAD_DIM), F32)
        for c in range(NDP):
            left = rows[:, c * 256 : (c + 1) * 256]
            across = (((1,), (1,)), ((), ()))
            kv += lax.dot_general(
                left, w4buf[c, at, 1:].reshape(HEAD_DIM, 256), across, preferred_element_type=F32
            )
            qk += lax.dot_general(
                left, w4buf[c, at, :2].reshape(HEAD_DIM, 256), across, preferred_element_type=F32
            )
        psend[at, :, :HEAD_DIM] = kv.astype(BF16)
        psend[at, :, HEAD_DIM:] = jnp.where(low_x, qk, pltpu.roll(qk, 64, 1)).astype(BF16)
        squares[0] += jnp.where(low_x, qk * qk, 0.0)
        squares[1] += jnp.where(low_x, kv * kv, 0.0)

    low_f = lanes(GRP) < HEAD_DIM // 2

    def take(j, blocks):
        p = xa(NX - j)
        rows = blocks[p]
        q = rows[:, HEAD_DIM:].astype(F32)
        qpk[p] = jnp.where(low_f, q[:GRP], q[GRP:]).astype(BF16)
        at = pl.ds(pl.multiple_of(p * OWN, OWN), OWN)
        kvs[:, at] = rows[:, :HEAD_DIM].reshape(NZ, OWN, HEAD_DIM)
        each(1, NZ, lambda k: qz(j, k).start())

    def project_send(k):
        project(k)
        px(k).start()

    squares[...] = jnp.zeros_like(squares)
    project(0)
    take(0, psend)
    each(1, NX, project_send)
    lane_own = lanes(OWN)
    mine = jnp.zeros((OWN, HEAD_DIM), F32)
    for kind in range(2):
        sums = jnp.sum(squares[kind], axis=1, keepdims=True)
        for g in range(NZ):
            mine = jnp.where(lane_own == 4 * g + 2 * kind, sums[g * OWN : (g + 1) * OWN], mine)
    stat[pl.ds(x, 1)] = mine[None]
    each(1, NX, lambda k: stx(k).start())
    each(1, NX, lambda k: vx(k).start())
    ffn_w.enter(2).start()
    for k in (1, 3):
        ffn_w.enter_in(k).wait_recv()
        ffn_w.go_near(k)

    def taken(j):
        px_in(j).wait_recv()
        take(j, precv)

    each(1, NX, taken)
    each(1, NX, lambda k: stx_in(k).wait_recv())
    both = stat[0]
    for p in range(1, NX):
        both += pltpu.roll(stat[p], 32 * p, 1)
    high = both.astype(BF16).astype(F32)
    kvs[:, GRP:] = jnp.broadcast_to(
        (high + pltpu.roll(both - high, 1, 1)).astype(BF16)[None], (NZ, OWN, HEAD_DIM)
    )
    each(1, NZ, lambda k: cz(k).start())
    qrecv[pl.ds(z, 1)] = qpk[...][None]
    kvrecv[pl.ds(z, 1)] = kvs[pl.ds(z, 1)]
    each(0, 2, out_w.step_near)

    grp_rows = pl.ds(pl.multiple_of(z * GRP, GRP), GRP)
    for block in range(NX):
        first = (block * NZ + z) * CTX
        slot = lax.div(first, CH)
        later = lax.min(slot + 1, NCH - 1)
        row = first + lax.broadcasted_iota(jnp.int32, (1, CTX), 1)
        code = jnp.where(row < (slot + 1) * CH, sbase[slot], sbase[later]) + row
        hit = jnp.max(
            jnp.where(rows_of[:, 0:1] == row, 1, 0), axis=0, keepdims=True
        )
        kcode[:, block * CTX : (block + 1) * CTX] = jnp.where(hit > 0, DEAD, code)
    corner = lax.broadcasted_iota(jnp.int32, (GRP, HEAD_DIM), 0) == lanes(GRP)
    kcode[:, CACHED:KEYS] = jnp.where(
        lanes(1) < GRP,
        jnp.sum(jnp.where(corner, codes[grp_rows], 0), axis=0, keepdims=True),
        DEAD,
    )
    kall[CACHED:KEYS, :] = jnp.zeros((KEYS - CACHED, PART), BF16)
    vall[CACHED:KEYS, :] = jnp.zeros((KEYS - CACHED, PART), BF16)

    own_copies[4].wait()
    each(1, NX, lambda k: kx_in(k).wait_recv())

    def turn(block):
        first = (block * NZ + z) * CTX
        slot = lax.div(first, CH)
        later = lax.min(slot + 1, NCH - 1)
        row = first + lax.broadcasted_iota(jnp.int32, (CTX, HEAD_DIM), 0)
        here = row < (slot + 1) * CH
        cosine = jnp.where(here, scos[pl.ds(slot, 1), :], scos[pl.ds(later, 1), :])
        sine = jnp.where(here, ssin[pl.ds(slot, 1), :], ssin[pl.ds(later, 1), :])
        for h in range(HEADS):
            cols = slice(h * HEAD_DIM, (h + 1) * HEAD_DIM)
            v = kraw[block, :, cols].astype(F32)
            kall[key_rows(block), cols] = (v * cosine + pltpu.roll(v, 64, 1) * sine).astype(BF16)

    each(0, NX, turn)
    def mask(i):
        rows = pl.ds(pl.multiple_of(i * 128, 128), 128)
        code = kcode[...]
        usable = (code <= codes[rows, 0:1]) & (code >= lows[rows, 0:1])
        bias[rows] = jnp.where(usable, 0.0, NEGATIVE)

    each(0, SEL // 128, mask)

    each(0, NX, lambda j: each(1, NZ, lambda k: qz_in(j, k).wait_recv()))
    each(1, NZ, lambda k: cz_in(k).wait_recv())
    low = lanes(SEL // 2) < HEAD_DIM // 2

    def in_order(t):
        return jnp.concatenate(
            [
                t[p * GRP + g * OWN : p * GRP + (g + 1) * OWN]
                for g in range(NZ // 2)
                for p in range(NX)
            ],
            axis=0,
        )

    def q_head(h):
        a = qrecv[2 * h].reshape(SEL // 2, HEAD_DIM).astype(F32)
        b = qrecv[2 * h + 1].reshape(SEL // 2, HEAD_DIM).astype(F32)
        top = jnp.where(low, a, pltpu.roll(b, 64, 1))
        bottom = jnp.where(low, pltpu.roll(a, 64, 1), b)
        return in_order(top), in_order(bottom)

    def f_head(h):
        a = kvrecv[2 * h, :GRP].astype(F32)
        b = kvrecv[2 * h + 1, :GRP].astype(F32)
        return jnp.where(low_f, a, pltpu.roll(b, 64, 1)), jnp.where(low_f, pltpu.roll(a, 64, 1), b)

    each(0, 2, out_w.step_far)
    total = jnp.zeros((OWN, HEAD_DIM), F32)
    for p in range(NZ):
        total += kvrecv[p, GRP:].astype(F32)
    total = total + pltpu.roll(total, HEAD_DIM - 1, 1)
    even = lax.rem(lane_own, 2) == 0
    factor = lax.rsqrt(jnp.where(even, total, 1.0) * (1.0 / D) + EPSILON)
    for g in range(NZ):
        for p in range(NX):
            at = (g * NX + p) * OWN
            col = 32 * p + 4 * g
            sq[0, at : at + OWN] = jnp.broadcast_to(
                factor[:, col : col + 1] * SCORE, (OWN, HEAD_DIM)
            )
            sq[1, at : at + OWN] = jnp.broadcast_to(factor[:, col + 2 : col + 3], (OWN, HEAD_DIM))
    for h in range(HEADS):
        cols = pl.ds(pl.multiple_of(x * PART + h * HEAD_DIM, HEAD_DIM), HEAD_DIM)
        top, bottom = q_head(h)
        gain = gains[0:1, cols]
        for part, rows in ((top, slice(0, SEL // 2)), (bottom, slice(SEL // 2, SEL))):
            v = part * sq[0, rows] * gain
            qh[h, rows] = (v * qcos[rows] + pltpu.roll(v, 64, 1) * qsin[rows]).astype(BF16)
        key, value = f_head(h)
        vall[CACHED : CACHED + GRP, h * HEAD_DIM : (h + 1) * HEAD_DIM] = value.astype(BF16)
        v = key * sq[1, grp_rows] * gains[1:2, cols]
        v = (v * qcos[grp_rows] + pltpu.roll(v, 64, 1) * qsin[grp_rows]).astype(BF16)
        kall[CACHED : CACHED + GRP, h * HEAD_DIM : (h + 1) * HEAD_DIM] = v
        kf[:, :, h * HEAD_DIM : (h + 1) * HEAD_DIM] = v.reshape(NX, OWN, HEAD_DIM)
    each(1, NX, lambda k: fx(k).start())
    frecv[pl.ds(x, 1)] = kf[pl.ds(x, 1)]

    own_copies[5].wait()
    each(1, NX, lambda k: vx_in(k).wait_recv())

    lane = lanes(128)

    def attend(part):
        rows = pl.ds(pl.multiple_of(part * 128, 128), 128)
        two = pl.ds(part * 2, 2)
        marks = jnp.zeros((128, HEAD_DIM), F32)
        for h in range(HEADS):
            cols = slice(h * HEAD_DIM, (h + 1) * HEAD_DIM)
            scores = lax.dot_general(
                qh[h, rows], kall[:, cols], (((1,), (1,)), ((), ())), preferred_element_type=F32
            ) + bias[rows]
            most = jnp.maximum(jnp.max(scores, axis=1, keepdims=True), FLOOR)
            most = most.astype(BF16).astype(F32)
            weight = jnp.exp2(scores - most)
            mass = jnp.sum(weight, axis=1, keepdims=True)
            mixed = jnp.dot(weight.astype(BF16), vall[:, cols], preferred_element_type=F32)
            obuf[two, h * GRP : (h + 1) * GRP, :] = mixed.astype(BF16).reshape(2, GRP, HEAD_DIM)
            high = mass.astype(BF16).astype(F32)
            marks = jnp.where(lane == h, most, marks)
            marks = jnp.where(lane == h + HEADS, high, marks)
            marks = jnp.where(lane == h + 2 * HEADS, mass - high, marks)
        for side in range(2):
            packed = marks[side * GRP : side * GRP + OWN]
            for g in range(1, NX):
                at = side * GRP + g * OWN
                packed += pltpu.roll(marks[at : at + OWN], 32 * g, 1)
            obuf[part * 2 + side, HEADS * GRP :, :] = packed.astype(BF16)

    def attend_far(i):
        part = lax.rem(lax.div(z, 2) + 1 + lax.rem(i + 1, 3), NZ // 2)
        attend(part)
        offset = lax.rem(2 * part + NZ - z, NZ)
        oex(offset).start()
        oex(lax.rem(offset + 1, NZ)).start()
        ffn_w.step_near(i + lax.div(i, 2))

    each(0, 3, attend_far)
    attend(lax.div(z, 2))
    beside = lax.rem(NZ + 1 - 2 * lax.rem(z, 2), NZ)
    oex(beside).start()
    orecv[pl.ds(z, 1)] = obuf[pl.ds(z, 1)]
    ffn_w.enter_in(2).wait_recv()
    ffn_w.go_near(2)
    out_w.arrive()
    each(1, NZ, lambda k: oex_in(k).wait_recv())

    def marks_of(p):
        return orecv[p, HEADS * GRP :, :].astype(F32)

    peak = marks_of(0)
    for p in range(1, NZ):
        peak = jnp.maximum(peak, marks_of(p))
    mass = jnp.zeros((OWN, HEAD_DIM), F32)
    for p in range(NZ):
        marks = marks_of(p)
        amount = pltpu.roll(marks, HEAD_DIM - HEADS, 1) + pltpu.roll(
            marks, HEAD_DIM - 2 * HEADS, 1
        )
        mass += jnp.exp2(marks - peak) * amount
    valid = lax.rem(lane_own, 32) < HEADS
    inverse = 1.0 / jnp.where(valid, mass, 1.0)
    heads = [jnp.zeros((GRP, HEAD_DIM), F32) for _ in range(HEADS)]
    for p in range(NZ):
        share = jnp.exp2(marks_of(p) - peak) * inverse
        for h in range(HEADS):
            part = orecv[p, h * GRP : (h + 1) * GRP, :].astype(F32)
            weight = jnp.concatenate(
                [
                    jnp.broadcast_to(
                        share[:, 32 * g + h : 32 * g + h + 1], (OWN, HEAD_DIM)
                    )
                    for g in range(NX)
                ],
                axis=0,
            )
            heads[h] += part * weight
    attn = jnp.concatenate(heads, axis=1).astype(BF16)

    def out_block(c):
        got = jnp.dot(attn, wobuf[c].reshape(PART, 256), preferred_element_type=F32)
        cols = pl.ds(pl.multiple_of(c * 256, 256), 256)
        ysend[:, :, cols] = got.astype(BF16).reshape(NX, OWN, 256)

    each(0, NDP, out_block)
    each(1, NX, lambda k: yx(k).start())
    yrecv[pl.ds(x, 1)] = ysend[pl.ds(x, 1)]
    for k in (0, 1, 3):
        ffn_w.step_far(k)
    each(1, NX, lambda k: yx_in(k).wait_recv())
    y = yrecv[0].astype(F32)
    for p in range(1, NX):
        y += yrecv[p].astype(F32)
    y = y * lax.rsqrt(jnp.mean(y * y, axis=1, keepdims=True) + EPSILON) * gains[2:3, :]
    following = (hid[z].astype(F32) + y).astype(BF16)
    hn[...] = following
    each(1, NZ, lambda k: nz(k).start())
    hbuf[pl.ds(z, 1)] = following[None]
    ffn_w.step_near(2)
    ffn_w.step_far(2)

    each(1, NZ, lambda k: nz_in(k).wait_recv())
    ffn_w.arrive()

    def gate(c):
        rows = hbuf[...].reshape(NZ * OWN, D)
        g = jnp.dot(rows, wbuf[:, c, 0].reshape(D, 256), preferred_element_type=F32)
        u = jnp.dot(rows, wbuf[:, c, 1].reshape(D, 256), preferred_element_type=F32)
        cols = pl.ds(pl.multiple_of(c * 256, 256), 256)
        act[:, cols] = (jax.nn.silu(g) * u).astype(BF16)

    each(0, NX, gate)

    def down_half(half):
        def down(c):
            weights = wbuf[half * 4 + c, :, 2].reshape(NX * 256, 256)
            got = jnp.dot(act[...], weights, preferred_element_type=F32)
            cols = pl.ds(pl.multiple_of(c * 256, 256), 256)
            dsend[half, :, :, cols] = got.astype(BF16).reshape(NZ, OWN, 256)

        each(0, 4, down)
        each(1, NZ, lambda k: dz(half, k).start())

    each(0, 2, down_half)
    for half in range(2):
        drecv[half, pl.ds(z, 1)] = dsend[half, pl.ds(z, 1)]

    each(1, NX, lambda k: fx_in(k).wait_recv())
    for p in range(NX):
        both_out[1, :, p * PART : (p + 1) * PART] = frecv[p]

    each(0, 2, lambda half: each(1, NZ, lambda k: dz_in(half, k).wait_recv()))
    halves = []
    for half in range(2):
        t = drecv[half, 0].astype(F32)
        for p in range(1, NZ):
            t += drecv[half, p].astype(F32)
        halves.append(t)
    t = jnp.concatenate(halves, axis=1)
    t = t * lax.rsqrt(jnp.mean(t * t, axis=1, keepdims=True) + EPSILON) * gains[3:4, :]
    both_out[0] = (hn[...].astype(F32) + t).astype(BF16)

    each(0, NX, lambda j: each(1, NZ, lambda k: qz(j, k).wait_send()))
    for copy in (hz, cz, oex, nz):
        each(1, NZ, lambda k, copy=copy: copy(k).wait_send())
    for copy in (kx, vx, px, stx, fx, yx):
        each(1, NX, lambda k, copy=copy: copy(k).wait_send())
    each(0, 2, lambda half: each(1, NZ, lambda k: dz(half, k).wait_send()))
    for weights in (qkv_w, out_w, ffn_w):
        weights.finish()


def layer(
    hidden_sel, picked, order, lengths, offsets, cache_keys, cache_values, w_qkv, w_out,
    w_gate_up, w_down, gains,
):
    w4 = w_qkv.transpose(0, 2, 1)

    vmem = pl.BlockSpec(memory_space=pltpu.VMEM)
    far = pl.BlockSpec(memory_space=pl.ANY)
    smem = pl.BlockSpec(memory_space=pltpu.SMEM)
    dma = pltpu.SemaphoreType.DMA

    def spread(peers, slots):
        return (
            dma((peers,)), dma((peers,)), dma((slots, NY)), dma((slots, NY)), dma((slots,)),
            dma((slots, NY)), dma((slots, NY)),
        )

    both = pl.pallas_call(
        kernel,
        out_shape=jax.ShapeDtypeStruct((2, OWN, D), BF16),
        in_specs=[vmem, far, far, far, far, far, far, vmem, vmem, smem, smem, smem],
        out_specs=vmem,
        scratch_shapes=[
            pltpu.VMEM((NZ, OWN, D), BF16),
            pltpu.VMEM((NDP, NX, 3, 64, 256), BF16),
            pltpu.VMEM((NDP, NZ, 64, 256), BF16),
            pltpu.VMEM((NDP, NX, 3, 256, 256), BF16),
            pltpu.VMEM((NX, CTX, PART), BF16),
            pltpu.VMEM((KEYS, PART), BF16),
            pltpu.VMEM((KEYS, PART), BF16),
            pltpu.VMEM((1, KEYS), jnp.int32),
            pltpu.VMEM((NX, NZ * OWN, 256), BF16),
            pltpu.VMEM((NX, NZ * OWN, 256), BF16),
            pltpu.VMEM((NX, GRP, HEAD_DIM), BF16),
            pltpu.VMEM((NZ, GRP + OWN, HEAD_DIM), BF16),
            pltpu.VMEM((NZ, NX, GRP, HEAD_DIM), BF16),
            pltpu.VMEM((NZ, GRP + OWN, HEAD_DIM), BF16),
            pltpu.VMEM((2, SEL, HEAD_DIM), F32),
            pltpu.VMEM((NX, OWN, HEAD_DIM), F32),
            pltpu.VMEM((HEADS, SEL, HEAD_DIM), BF16),
            pltpu.VMEM((NX, OWN, PART), BF16),
            pltpu.VMEM((NX, OWN, PART), BF16),
            pltpu.VMEM((NZ, HEADS * GRP + OWN, HEAD_DIM), BF16),
            pltpu.VMEM((NZ, HEADS * GRP + OWN, HEAD_DIM), BF16),
            pltpu.VMEM((NX, OWN, D), BF16),
            pltpu.VMEM((NX, OWN, D), BF16),
            pltpu.VMEM((OWN, D), BF16),
            pltpu.VMEM((NZ, OWN, D), BF16),
            pltpu.VMEM((NZ * OWN, NX * 256), BF16),
            pltpu.VMEM((2, NZ, OWN, D // 2), BF16),
            pltpu.VMEM((2, NZ, OWN, D // 2), BF16),
            pltpu.VMEM((SEL, HEAD_DIM), F32),
            pltpu.VMEM((SEL, HEAD_DIM), jnp.int32),
            pltpu.VMEM((SEL, HEAD_DIM), jnp.int32),
            pltpu.VMEM((SEL, HEAD_DIM), jnp.int32),
            pltpu.VMEM((SEL, HEAD_DIM), F32),
            pltpu.VMEM((SEL, HEAD_DIM), F32),
            pltpu.VMEM((16, HEAD_DIM), F32),
            pltpu.VMEM((16, HEAD_DIM), F32),
            pltpu.SMEM((16,), jnp.int32),
            pltpu.VMEM((SEL, KEYS), F32),
            pltpu.VMEM((2, NZ * OWN, HEAD_DIM), F32),
            dma((NZ,)), dma((NZ,)),
            spread(NX, NX),
            spread(NZ, 2),
            spread(NX, NX),
            dma((NX,)), dma((NX,)),
            dma((NX,)), dma((NX,)),
            dma((NX,)), dma((NX,)),
            dma((NX, NZ)), dma((NX, NZ)),
            dma((NZ,)), dma((NZ,)),
            dma((NX,)), dma((NX,)),
            dma((NX,)), dma((NX,)),
            dma((NZ,)), dma((NZ,)),
            dma((NX,)), dma((NX,)),
            dma((NZ,)), dma((NZ,)),
            dma((2, NZ)), dma((2, NZ)),
            dma((7,)),
        ],
        compiler_params=pltpu.CompilerParams(
            collective_id=0, has_side_effects=True, vmem_limit_bytes=56 << 20
        ),
    )(
        hidden_sel[0], cache_keys[0], cache_values[0], w4, w_out, w_gate_up, w_down, gains,
        picked, order, lengths, offsets,
    )
    return (both[:1], both[1:])


def solution(mesh):
    placed = (
        P("dp", "tensor", None),
        P("dp", None),
        P("dp", None),
        P("dp", None),
        P("dp", None),
        P("dp", "tensor", None),
        P("dp", "tensor", None),
        P(None, "dp", "tensor"),
        P("tensor", "dp"),
        P(None, "dp", "tensor"),
        P("tensor", "dp"),
        P(),
    )
    return jax.shard_map(
        layer,
        mesh=mesh,
        in_specs=placed,
        out_specs=(P("dp", "tensor", None), P("dp", "tensor", None)),
        check_vma=False,
    )
```

```python
import math

import jax
import jax.numpy as jnp
import numpy as np
from jax import lax
from jax.experimental import pallas as pl
from jax.experimental.pallas import tpu as pltpu
from jax.sharding import PartitionSpec as P

HEAD_DIM = 128
CH = 1024
NCH = 12
REQS = 3
NX = 4
NZ = 8
NDP = 8
NY = 4
D = 2048
PART = D // NX
HEADS = PART // HEAD_DIM
OWN = 16
GRP = NX * OWN
SEL = NZ * GRP
CTX = 384
CACHED = NX * CTX
KEYS = CACHED + 128
SPAN = 1 << 14
DEAD = 1 << 30

THETA = 500000.0
EPSILON = 1e-06
NEGATIVE = -1e30
FLOOR = -1e20
SCORE = HEAD_DIM ** (-0.5) * math.log2(math.e)
LAP_A = 6.28125
LAP_B = 0.0019340515136718750
LAP_C = 2.0 * math.pi - LAP_A - LAP_B
RATES = [
    float(np.float32(math.exp(-2.0 * j / HEAD_DIM * math.log(THETA)))) for j in range(HEAD_DIM // 2)
]
MESH = pl.DeviceIdType.MESH
F32, BF16 = jnp.float32, jnp.bfloat16
HIGH = lax.Precision.HIGHEST


def lanes(rows):
    return lax.broadcasted_iota(jnp.int32, (rows, HEAD_DIM), 1)


def kernel(
    hidden,
    keys,
    values,
    w4,
    wo,
    wgu,
    wd,
    gains,
    picked,
    order,
    lengths,
    offsets,
    both_out,
    hid,
    w4buf,
    wobuf,
    wbuf,
    kraw,
    kall,
    vall,
    kcode,
    psend,
    precv,
    qpk,
    kvs,
    qrecv,
    kvrecv,
    sq,
    stat,
    qh,
    kf,
    frecv,
    obuf,
    orecv,
    ysend,
    yrecv,
    hn,
    hbuf,
    act,
    dsend,
    drecv,
    natural,
    rows_of,
    codes,
    lows,
    qcos,
    qsin,
    scos,
    ssin,
    sbase,
    bias,
    squares,
    hz_s,
    hz_r,
    w4_sems,
    wo_sems,
    wm_sems,
    k_s,
    k_r,
    v_s,
    v_r,
    p_s,
    p_r,
    q_s,
    q_r,
    c_s,
    c_r,
    st_s,
    st_r,
    f_s,
    f_r,
    o_s,
    o_r,
    y_s,
    y_r,
    n_s,
    n_r,
    d_s,
    d_r,
    loc,
):
    tens = lax.axis_index("tensor")
    dp = lax.axis_index("dp")
    x = lax.div(tens, NZ)
    z = lax.rem(tens, NZ)
    core = lax.rem(dp, 2)
    sib = dp + 1 - 2 * core

    def xa(k):
        return lax.rem(x + k, NX)

    def za(k):
        return lax.rem(z + k, NZ)

    def da(k):
        return lax.rem(dp + k, NDP)

    def zdev(k):
        return {"tensor": x * NZ + za(k)}

    def xdev(k):
        return {"tensor": xa(k) * NZ + z}

    def send(src, dst, ssem, rsem, dev):
        return pltpu.make_async_remote_copy(
            src_ref=src, dst_ref=dst, send_sem=ssem, recv_sem=rsem, device_id=dev,
            device_id_type=MESH,
        )

    def each(first, last, body):
        def step(k, carry):
            body(k)
            return carry

        lax.fori_loop(first, last, step, 0)

    class Spread:
        def __init__(self, sems, slots, source, first, peers, entry, entry_in, at):
            (self.e_s, self.e_r, self.n_s, self.y_r, self.r_s, self.s_s, self.s_r) = sems
            self.slots, self.source, self.first, self.peers = slots, source, first, peers
            self.entry, self.entry_in, self.at = entry, entry_in, at

        def enter(self, k):
            return send(self.source, self.entry, self.e_s.at[k], self.e_r.at[k], self.first(k))

        def enter_in(self, k):
            at = self.entry_in(k)
            return send(at, at, self.e_s.at[k], self.e_r.at[k], self.first(k))

        def near(self, k, j):
            at = self.at(dp, k)
            return send(at, at, self.n_s.at[k, j], self.y_r.at[k, j], {"dp": da(2 * j)})

        def near_in(self, k, j):
            at = self.at(da(NDP - 2 * j), k)
            return send(at, at, self.n_s.at[k, j], self.y_r.at[k, j], {"dp": da(2 * j)})

        def way(self, k):
            return 1 + 2 * lax.div(k, self.slots // 2)

        def relay(self, k):
            j = self.way(k)
            at = self.at(da(NDP - 2 * j), k)
            return send(at, at, self.r_s.at[k], self.y_r.at[k, 2], {"dp": da(2 * j)})

        def relay_in(self, k):
            at = self.at(da(4), k)
            return send(at, at, self.r_s.at[k], self.y_r.at[k, 2], {"dp": da(2)})

        def side(self, k, j):
            at = self.at(da(NDP - 2 * j), k)
            return send(at, at, self.s_s.at[k, j], self.s_r.at[k, j], {"dp": sib})

        def side_in(self, k, j):
            at = self.at(lax.rem(sib + NDP - 2 * j, NDP), k)
            return send(at, at, self.s_s.at[k, j], self.s_r.at[k, j], {"dp": sib})

        def start(self):
            each(1, self.peers, lambda k: self.enter(k).start())

        def go_near(self, k):
            self.near(k, 1).start()
            self.near(k, 3).start()
            self.side(k, 0).start()

        def step_near(self, k):
            self.near_in(k, 1).wait_recv()
            self.near_in(k, 3).wait_recv()
            self.relay(k).start()
            self.side(k, 1).start()
            self.side(k, 3).start()

        def step_far(self, k):
            self.relay_in(k).wait_recv()
            self.side(k, 2).start()

        def arrive(self):
            each(0, self.slots, lambda k: each(0, NY, lambda j: self.side_in(k, j).wait_recv()))

        def finish(self):
            each(1, self.peers, lambda k: self.enter(k).wait_send())

            def one(k):
                self.near(k, 1).wait_send()
                self.near(k, 3).wait_send()
                self.relay(k).wait_send()
                each(0, NY, lambda j: self.side(k, j).wait_send())

            each(0, self.slots, one)

    def x_slot(buf):
        return lambda d, k: buf.at[d, xa(NX - k)]

    qkv_w = Spread(
        w4_sems, NX, w4, xdev, NX, w4buf.at[dp, x], lambda k: w4buf.at[dp, xa(NX - k)],
        x_slot(w4buf),
    )
    ffn_w = Spread(
        wm_sems, NX, wbuf.at[dp, x], xdev, NX, wbuf.at[dp, x], lambda k: wbuf.at[dp, xa(NX - k)],
        x_slot(wbuf),
    )
    out_w = Spread(
        wo_sems, 2, wo, zdev, NZ, wobuf.at[dp, z], lambda k: wobuf.at[dp, za(NZ - k)],
        lambda d, k: wobuf.at[d, pl.ds(4 * k, 4)],
    )

    def hz(k):
        return send(hidden, hid.at[z], hz_s.at[k], hz_r.at[k], zdev(k))

    def hz_in(k):
        at = hid.at[za(NZ - k)]
        return send(at, at, hz_s.at[k], hz_r.at[k], zdev(k))

    def columns(at):
        return pl.ds(pl.multiple_of(at * PART, PART), PART)

    def key_rows(at):
        return pl.ds(pl.multiple_of(at * CTX, 128), CTX)

    def kx(k):
        return send(keys.at[:, columns(xa(k))], kraw.at[x], k_s.at[k], k_r.at[k], xdev(k))

    def kx_in(k):
        at = kraw.at[xa(NX - k)]
        return send(at, at, k_s.at[k], k_r.at[k], xdev(k))

    def vx(k):
        return send(
            values.at[:, columns(xa(k))], vall.at[key_rows(x)], v_s.at[k], v_r.at[k], xdev(k)
        )

    def vx_in(k):
        at = vall.at[key_rows(xa(NX - k))]
        return send(at, at, v_s.at[k], v_r.at[k], xdev(k))

    def px(k):
        return send(psend.at[xa(k)], precv.at[x], p_s.at[k], p_r.at[k], xdev(k))

    def px_in(k):
        at = precv.at[xa(NX - k)]
        return send(at, at, p_s.at[k], p_r.at[k], xdev(k))

    def qz(j, k):
        p = xa(NX - j)
        return send(qpk.at[p], qrecv.at[z, p], q_s.at[j, k], q_r.at[j, k], zdev(k))

    def qz_in(j, k):
        at = qrecv.at[za(NZ - k), xa(NX - j)]
        return send(at, at, q_s.at[j, k], q_r.at[j, k], zdev(k))

    def cz(k):
        return send(kvs.at[za(k)], kvrecv.at[z], c_s.at[k], c_r.at[k], zdev(k))

    def cz_in(k):
        at = kvrecv.at[za(NZ - k)]
        return send(at, at, c_s.at[k], c_r.at[k], zdev(k))

    def stx(k):
        return send(stat.at[x], stat.at[x], st_s.at[k], st_r.at[k], xdev(k))

    def stx_in(k):
        at = stat.at[xa(NX - k)]
        return send(at, at, st_s.at[k], st_r.at[k], xdev(k))

    def fx(k):
        return send(kf.at[xa(k)], frecv.at[x], f_s.at[k], f_r.at[k], xdev(k))

    def fx_in(k):
        at = frecv.at[xa(NX - k)]
        return send(at, at, f_s.at[k], f_r.at[k], xdev(k))

    def oex(k):
        return send(obuf.at[za(k)], orecv.at[z], o_s.at[k], o_r.at[k], zdev(k))

    def oex_in(k):
        at = orecv.at[za(NZ - k)]
        return send(at, at, o_s.at[k], o_r.at[k], zdev(k))

    def yx(k):
        return send(ysend.at[xa(k)], yrecv.at[x], y_s.at[k], y_r.at[k], xdev(k))

    def yx_in(k):
        at = yrecv.at[xa(NX - k)]
        return send(at, at, y_s.at[k], y_r.at[k], xdev(k))

    def nz(k):
        return send(hn, hbuf.at[z], n_s.at[k], n_r.at[k], zdev(k))

    def nz_in(k):
        at = hbuf.at[za(NZ - k)]
        return send(at, at, n_s.at[k], n_r.at[k], zdev(k))

    def dz(half, k):
        return send(
            dsend.at[half, za(k)], drecv.at[half, z], d_s.at[half, k], d_r.at[half, k], zdev(k)
        )

    def dz_in(half, k):
        at = drecv.at[half, za(NZ - k)]
        return send(at, at, d_s.at[half, k], d_r.at[half, k], zdev(k))

    own_copies = [
        pltpu.make_async_copy(hidden, hid.at[z], loc.at[0]),
        pltpu.make_async_copy(w4, w4buf.at[dp, x], loc.at[1]),
        pltpu.make_async_copy(wo, wobuf.at[dp, z], loc.at[2]),
        pltpu.make_async_copy(wgu, wbuf.at[dp, x, pl.ds(0, 2)], loc.at[3]),
        pltpu.make_async_copy(keys.at[:, columns(x)], kraw.at[x], loc.at[4]),
        pltpu.make_async_copy(values.at[:, columns(x)], vall.at[key_rows(x)], loc.at[5]),
        pltpu.make_async_copy(wd, wbuf.at[dp, x, 2], loc.at[6]),
    ]
    for copy in own_copies:
        copy.start()

    barrier = pltpu.get_barrier_semaphore()

    def greet(dev):
        pl.semaphore_signal(barrier, inc=1, device_id=dev, device_id_type=MESH)

    each(1, NZ, lambda k: greet(zdev(k)))
    each(1, NX, lambda k: greet(xdev(k)))
    greet({"dp": da(2)})
    greet({"dp": da(6)})
    greet({"dp": sib})
    pl.semaphore_wait(barrier, NZ + NX + 1)

    qkv_w.start()
    own_copies[1].wait()
    qkv_w.go_near(0)
    each(1, NZ, lambda k: hz(k).start())
    own_copies[3].wait()
    own_copies[6].wait()
    ffn_w.enter(1).start()
    ffn_w.enter(3).start()
    each(1, NX, lambda k: kx(k).start())
    out_w.start()

    end_a = lengths[0, 0]
    end_b = end_a + lengths[0, 1]
    span = lax.broadcasted_iota(jnp.int32, (16, HEAD_DIM), 0)
    turns = jnp.zeros((16, HEAD_DIM), jnp.int32)
    shifts, bottoms = [], []
    for slot in range(NCH):
        place = order[0, slot]
        second, third = place >= end_a, place >= end_b
        start = jnp.where(third, end_b, jnp.where(second, end_a, 0))
        moved = jnp.where(third, offsets[0, 2], jnp.where(second, offsets[0, 1], offsets[0, 0]))
        bottom = jnp.where(third, 2 * SPAN, jnp.where(second, SPAN, 0))
        base = moved + (place - start) * CH
        sbase[slot] = base + bottom - slot * CH
        shifts.append(base + bottom - slot * CH)
        bottoms.append(bottom)
        turns = jnp.where(span == slot, base, turns)

    turn_lane = lax.rem(lanes(8), HEAD_DIM // 2)
    rates = jnp.zeros((8, HEAD_DIM), F32)
    for j in range(HEAD_DIM // 2):
        rates = jnp.where(turn_lane == j, RATES[j], rates)

    def circle(position):
        angle = position.astype(F32) * rates[0:1, :]
        laps = jnp.floor(angle * (0.5 / math.pi) + 0.5)
        angle = ((angle - laps * LAP_A) - laps * LAP_B) - laps * LAP_C
        sine = jnp.sin(angle)
        left = lax.broadcasted_iota(jnp.int32, position.shape, 1) < HEAD_DIM // 2
        return jnp.cos(angle), jnp.where(left, -sine, sine)

    scos[...], ssin[...] = circle(turns)

    natural[...] = lax.dot_general(
        jnp.broadcast_to(picked[...].astype(F32), (8, SEL)),
        jnp.full((8, HEAD_DIM), 0.125, F32), (((0,), (0,)), ((), ())),
        precision=HIGH, preferred_element_type=F32,
    )
    for zz in range(NZ):
        for xx in range(NX):
            at = (zz * NX + xx) * OWN
            back = (xx * NZ + zz) * OWN
            rows_of[at : at + OWN] = natural[back : back + OWN].astype(jnp.int32)

    def tokens(i):
        rows = pl.ds(pl.multiple_of(i * 128, 128), 128)
        row = rows_of[rows]
        slot_of = lax.shift_right_logical(row, 10)
        shift = jnp.zeros_like(row)
        bottom = jnp.zeros_like(row)
        for slot in range(NCH):
            mine = slot_of == slot
            shift = jnp.where(mine, shifts[slot], shift)
            bottom = jnp.where(mine, bottoms[slot], bottom)
        codes[rows] = row + shift
        lows[rows] = bottom
        qcos[rows], qsin[rows] = circle(row + shift - bottom)

    each(0, SEL // 128, tokens)

    def qkv_on(k):
        qkv_w.enter_in(k).wait_recv()
        qkv_w.go_near(k)

    each(1, NX, qkv_on)

    each(0, NX, qkv_w.step_near)
    own_copies[2].wait()
    each(1, NZ, lambda k: out_w.enter_in(k).wait_recv())
    each(0, NX, qkv_w.step_far)
    each(0, 2, out_w.go_near)
    ffn_w.go_near(0)

    own_copies[0].wait()
    each(1, NZ, lambda k: hz_in(k).wait_recv())
    qkv_w.arrive()

    low_x = lanes(NZ * OWN) < HEAD_DIM // 2

    def project(k):
        at = xa(k)
        rows = hid[...].reshape(NZ * OWN, D)
        kv = jnp.zeros((NZ * OWN, HEAD_DIM), F32)
        qk = jnp.zeros((NZ * OWN, HEAD_DIM), F32)
        for c in range(NDP):
            left = rows[:, c * 256 : (c + 1) * 256]
            across = (((1,), (1,)), ((), ()))
            kv += lax.dot_general(
                left, w4buf[c, at, 1:].reshape(HEAD_DIM, 256), across, preferred_element_type=F32
            )
            qk += lax.dot_general(
                left, w4buf[c, at, :2].reshape(HEAD_DIM, 256), across, preferred_element_type=F32
            )
        psend[at, :, :HEAD_DIM] = kv.astype(BF16)
        psend[at, :, HEAD_DIM:] = jnp.where(low_x, qk, pltpu.roll(qk, 64, 1)).astype(BF16)
        squares[0] += jnp.where(low_x, qk * qk, 0.0)
        squares[1] += jnp.where(low_x, kv * kv, 0.0)

    low_f = lanes(GRP) < HEAD_DIM // 2

    def take(j, blocks):
        p = xa(NX - j)
        rows = blocks[p]
        q = rows[:, HEAD_DIM:].astype(F32)
        qpk[p] = jnp.where(low_f, q[:GRP], q[GRP:]).astype(BF16)
        at = pl.ds(pl.multiple_of(p * OWN, OWN), OWN)
        kvs[:, at] = rows[:, :HEAD_DIM].reshape(NZ, OWN, HEAD_DIM)
        each(1, NZ, lambda k: qz(j, k).start())

    def project_send(k):
        project(k)
        px(k).start()

    squares[...] = jnp.zeros_like(squares)
    project(0)
    take(0, psend)
    each(1, NX, project_send)
    lane_own = lanes(OWN)
    mine = jnp.zeros((OWN, HEAD_DIM), F32)
    for kind in range(2):
        sums = jnp.sum(squares[kind], axis=1, keepdims=True)
        for g in range(NZ):
            mine = jnp.where(lane_own == 4 * g + 2 * kind, sums[g * OWN : (g + 1) * OWN], mine)
    stat[pl.ds(x, 1)] = mine[None]
    each(1, NX, lambda k: stx(k).start())
    each(1, NX, lambda k: vx(k).start())
    ffn_w.enter(2).start()
    for k in (1, 3):
        ffn_w.enter_in(k).wait_recv()
        ffn_w.go_near(k)

    def taken(j):
        px_in(j).wait_recv()
        take(j, precv)

    each(1, NX, taken)
    each(1, NX, lambda k: stx_in(k).wait_recv())
    both = stat[0]
    for p in range(1, NX):
        both += pltpu.roll(stat[p], 32 * p, 1)
    high = both.astype(BF16).astype(F32)
    kvs[:, GRP:] = jnp.broadcast_to(
        (high + pltpu.roll(both - high, 1, 1)).astype(BF16)[None], (NZ, OWN, HEAD_DIM)
    )
    each(1, NZ, lambda k: cz(k).start())
    qrecv[pl.ds(z, 1)] = qpk[...][None]
    kvrecv[pl.ds(z, 1)] = kvs[pl.ds(z, 1)]
    each(0, 2, out_w.step_near)

    grp_rows = pl.ds(pl.multiple_of(z * GRP, GRP), GRP)
    for block in range(NX):
        first = (block * NZ + z) * CTX
        slot = lax.div(first, CH)
        later = lax.min(slot + 1, NCH - 1)
        row = first + lax.broadcasted_iota(jnp.int32, (1, CTX), 1)
        code = jnp.where(row < (slot + 1) * CH, sbase[slot], sbase[later]) + row
        hit = jnp.max(
            jnp.where(rows_of[:, 0:1] == row, 1, 0), axis=0, keepdims=True
        )
        kcode[:, block * CTX : (block + 1) * CTX] = jnp.where(hit > 0, DEAD, code)
    corner = lax.broadcasted_iota(jnp.int32, (GRP, HEAD_DIM), 0) == lanes(GRP)
    kcode[:, CACHED:KEYS] = jnp.where(
        lanes(1) < GRP,
        jnp.sum(jnp.where(corner, codes[grp_rows], 0), axis=0, keepdims=True),
        DEAD,
    )
    kall[CACHED:KEYS, :] = jnp.zeros((KEYS - CACHED, PART), BF16)
    vall[CACHED:KEYS, :] = jnp.zeros((KEYS - CACHED, PART), BF16)

    own_copies[4].wait()
    each(1, NX, lambda k: kx_in(k).wait_recv())

    def turn(block):
        first = (block * NZ + z) * CTX
        slot = lax.div(first, CH)
        later = lax.min(slot + 1, NCH - 1)
        row = first + lax.broadcasted_iota(jnp.int32, (CTX, HEAD_DIM), 0)
        here = row < (slot + 1) * CH
        cosine = jnp.where(here, scos[pl.ds(slot, 1), :], scos[pl.ds(later, 1), :])
        sine = jnp.where(here, ssin[pl.ds(slot, 1), :], ssin[pl.ds(later, 1), :])
        for h in range(HEADS):
            cols = slice(h * HEAD_DIM, (h + 1) * HEAD_DIM)
            v = kraw[block, :, cols].astype(F32)
            kall[key_rows(block), cols] = (v * cosine + pltpu.roll(v, 64, 1) * sine).astype(BF16)

    each(0, NX, turn)
    def mask(i):
        rows = pl.ds(pl.multiple_of(i * 128, 128), 128)
        code = kcode[...]
        usable = (code <= codes[rows, 0:1]) & (code >= lows[rows, 0:1])
        bias[rows] = jnp.where(usable, 0.0, NEGATIVE)

    each(0, SEL // 128, mask)

    each(0, NX, lambda j: each(1, NZ, lambda k: qz_in(j, k).wait_recv()))
    each(1, NZ, lambda k: cz_in(k).wait_recv())
    low = lanes(SEL // 2) < HEAD_DIM // 2

    def in_order(t):
        return jnp.concatenate(
            [
                t[p * GRP + g * OWN : p * GRP + (g + 1) * OWN]
                for g in range(NZ // 2)
                for p in range(NX)
            ],
            axis=0,
        )

    def q_head(h):
        a = qrecv[2 * h].reshape(SEL // 2, HEAD_DIM).astype(F32)
        b = qrecv[2 * h + 1].reshape(SEL // 2, HEAD_DIM).astype(F32)
        top = jnp.where(low, a, pltpu.roll(b, 64, 1))
        bottom = jnp.where(low, pltpu.roll(a, 64, 1), b)
        return in_order(top), in_order(bottom)

    def f_head(h):
        a = kvrecv[2 * h, :GRP].astype(F32)
        b = kvrecv[2 * h + 1, :GRP].astype(F32)
        return jnp.where(low_f, a, pltpu.roll(b, 64, 1)), jnp.where(low_f, pltpu.roll(a, 64, 1), b)

    each(0, 2, out_w.step_far)
    total = jnp.zeros((OWN, HEAD_DIM), F32)
    for p in range(NZ):
        total += kvrecv[p, GRP:].astype(F32)
    total = total + pltpu.roll(total, HEAD_DIM - 1, 1)
    even = lax.rem(lane_own, 2) == 0
    factor = lax.rsqrt(jnp.where(even, total, 1.0) * (1.0 / D) + EPSILON)
    for g in range(NZ):
        for p in range(NX):
            at = (g * NX + p) * OWN
            col = 32 * p + 4 * g
            sq[0, at : at + OWN] = jnp.broadcast_to(
                factor[:, col : col + 1] * SCORE, (OWN, HEAD_DIM)
            )
            sq[1, at : at + OWN] = jnp.broadcast_to(factor[:, col + 2 : col + 3], (OWN, HEAD_DIM))
    for h in range(HEADS):
        cols = pl.ds(pl.multiple_of(x * PART + h * HEAD_DIM, HEAD_DIM), HEAD_DIM)
        top, bottom = q_head(h)
        gain = gains[0:1, cols]
        for part, rows in ((top, slice(0, SEL // 2)), (bottom, slice(SEL // 2, SEL))):
            v = part * sq[0, rows] * gain
            qh[h, rows] = (v * qcos[rows] + pltpu.roll(v, 64, 1) * qsin[rows]).astype(BF16)
        key, value = f_head(h)
        vall[CACHED : CACHED + GRP, h * HEAD_DIM : (h + 1) * HEAD_DIM] = value.astype(BF16)
        v = key * sq[1, grp_rows] * gains[1:2, cols]
        v = (v * qcos[grp_rows] + pltpu.roll(v, 64, 1) * qsin[grp_rows]).astype(BF16)
        kall[CACHED : CACHED + GRP, h * HEAD_DIM : (h + 1) * HEAD_DIM] = v
        kf[:, :, h * HEAD_DIM : (h + 1) * HEAD_DIM] = v.reshape(NX, OWN, HEAD_DIM)
    each(1, NX, lambda k: fx(k).start())
    frecv[pl.ds(x, 1)] = kf[pl.ds(x, 1)]

    own_copies[5].wait()
    each(1, NX, lambda k: vx_in(k).wait_recv())

    lane = lanes(128)

    def attend(part):
        rows = pl.ds(pl.multiple_of(part * 128, 128), 128)
        two = pl.ds(part * 2, 2)
        marks = jnp.zeros((128, HEAD_DIM), F32)
        for h in range(HEADS):
            cols = slice(h * HEAD_DIM, (h + 1) * HEAD_DIM)
            scores = lax.dot_general(
                qh[h, rows], kall[:, cols], (((1,), (1,)), ((), ())), preferred_element_type=F32
            ) + bias[rows]
            most = jnp.maximum(jnp.max(scores, axis=1, keepdims=True), FLOOR)
            most = most.astype(BF16).astype(F32)
            weight = jnp.exp2(scores - most)
            mass = jnp.sum(weight, axis=1, keepdims=True)
            mixed = jnp.dot(weight.astype(BF16), vall[:, cols], preferred_element_type=F32)
            obuf[two, h * GRP : (h + 1) * GRP, :] = mixed.astype(BF16).reshape(2, GRP, HEAD_DIM)
            high = mass.astype(BF16).astype(F32)
            marks = jnp.where(lane == h, most, marks)
            marks = jnp.where(lane == h + HEADS, high, marks)
            marks = jnp.where(lane == h + 2 * HEADS, mass - high, marks)
        for side in range(2):
            packed = marks[side * GRP : side * GRP + OWN]
            for g in range(1, NX):
                at = side * GRP + g * OWN
                packed += pltpu.roll(marks[at : at + OWN], 32 * g, 1)
            obuf[part * 2 + side, HEADS * GRP :, :] = packed.astype(BF16)

    def attend_far(i):
        part = lax.rem(lax.div(z, 2) + 1 + lax.rem(i + 1, 3), NZ // 2)
        attend(part)
        offset = lax.rem(2 * part + NZ - z, NZ)
        oex(offset).start()
        oex(lax.rem(offset + 1, NZ)).start()
        ffn_w.step_near(i + lax.div(i, 2))

    each(0, 3, attend_far)
    attend(lax.div(z, 2))
    beside = lax.rem(NZ + 1 - 2 * lax.rem(z, 2), NZ)
    oex(beside).start()
    orecv[pl.ds(z, 1)] = obuf[pl.ds(z, 1)]
    ffn_w.enter_in(2).wait_recv()
    ffn_w.go_near(2)
    out_w.arrive()
    each(1, NZ, lambda k: oex_in(k).wait_recv())

    def marks_of(p):
        return orecv[p, HEADS * GRP :, :].astype(F32)

    peak = marks_of(0)
    for p in range(1, NZ):
        peak = jnp.maximum(peak, marks_of(p))
    mass = jnp.zeros((OWN, HEAD_DIM), F32)
    for p in range(NZ):
        marks = marks_of(p)
        amount = pltpu.roll(marks, HEAD_DIM - HEADS, 1) + pltpu.roll(
            marks, HEAD_DIM - 2 * HEADS, 1
        )
        mass += jnp.exp2(marks - peak) * amount
    valid = lax.rem(lane_own, 32) < HEADS
    inverse = 1.0 / jnp.where(valid, mass, 1.0)
    heads = [jnp.zeros((GRP, HEAD_DIM), F32) for _ in range(HEADS)]
    for p in range(NZ):
        share = jnp.exp2(marks_of(p) - peak) * inverse
        for h in range(HEADS):
            part = orecv[p, h * GRP : (h + 1) * GRP, :].astype(F32)
            weight = jnp.concatenate(
                [
                    jnp.broadcast_to(
                        share[:, 32 * g + h : 32 * g + h + 1], (OWN, HEAD_DIM)
                    )
                    for g in range(NX)
                ],
                axis=0,
            )
            heads[h] += part * weight
    attn = jnp.concatenate(heads, axis=1).astype(BF16)

    def out_block(c):
        got = jnp.dot(attn, wobuf[c].reshape(PART, 256), preferred_element_type=F32)
        cols = pl.ds(pl.multiple_of(c * 256, 256), 256)
        ysend[:, :, cols] = got.astype(BF16).reshape(NX, OWN, 256)

    each(0, NDP, out_block)
    each(1, NX, lambda k: yx(k).start())
    yrecv[pl.ds(x, 1)] = ysend[pl.ds(x, 1)]
    for k in (0, 1, 3):
        ffn_w.step_far(k)
    each(1, NX, lambda k: yx_in(k).wait_recv())
    y = yrecv[0].astype(F32)
    for p in range(1, NX):
        y += yrecv[p].astype(F32)
    y = y * lax.rsqrt(jnp.mean(y * y, axis=1, keepdims=True) + EPSILON) * gains[2:3, :]
    following = (hid[z].astype(F32) + y).astype(BF16)
    hn[...] = following
    each(1, NZ, lambda k: nz(k).start())
    hbuf[pl.ds(z, 1)] = following[None]
    ffn_w.step_near(2)
    ffn_w.step_far(2)

    each(1, NZ, lambda k: nz_in(k).wait_recv())
    ffn_w.arrive()

    def gate(c):
        rows = hbuf[...].reshape(NZ * OWN, D)
        g = jnp.dot(rows, wbuf[:, c, 0].reshape(D, 256), preferred_element_type=F32)
        u = jnp.dot(rows, wbuf[:, c, 1].reshape(D, 256), preferred_element_type=F32)
        cols = pl.ds(pl.multiple_of(c * 256, 256), 256)
        act[:, cols] = (jax.nn.silu(g) * u).astype(BF16)

    each(0, NX, gate)

    def down_half(half):
        def down(c):
            weights = wbuf[half * 4 + c, :, 2].reshape(NX * 256, 256)
            got = jnp.dot(act[...], weights, preferred_element_type=F32)
            cols = pl.ds(pl.multiple_of(c * 256, 256), 256)
            dsend[half, :, :, cols] = got.astype(BF16).reshape(NZ, OWN, 256)

        each(0, 4, down)
        each(1, NZ, lambda k: dz(half, k).start())

    each(0, 2, down_half)
    for half in range(2):
        drecv[half, pl.ds(z, 1)] = dsend[half, pl.ds(z, 1)]

    each(1, NX, lambda k: fx_in(k).wait_recv())
    for p in range(NX):
        both_out[1, :, p * PART : (p + 1) * PART] = frecv[p]

    each(0, NX, lambda j: each(1, NZ, lambda k: qz(j, k).wait_send()))
    for copy in (hz, cz, oex, nz):
        each(1, NZ, lambda k, copy=copy: copy(k).wait_send())
    for copy in (kx, vx, px, stx, fx, yx):
        each(1, NX, lambda k, copy=copy: copy(k).wait_send())
    for weights in (qkv_w, out_w, ffn_w):
        weights.finish()

    each(0, 2, lambda half: each(1, NZ, lambda k: dz_in(half, k).wait_recv()))
    halves = []
    for half in range(2):
        t = drecv[half, 0].astype(F32)
        for p in range(1, NZ):
            t += drecv[half, p].astype(F32)
        halves.append(t)
    t = jnp.concatenate(halves, axis=1)
    t = t * lax.rsqrt(jnp.mean(t * t, axis=1, keepdims=True) + EPSILON) * gains[3:4, :]
    both_out[0] = (hn[...].astype(F32) + t).astype(BF16)
    each(0, 2, lambda half: each(1, NZ, lambda k: dz(half, k).wait_send()))


def layer(
    hidden_sel, picked, order, lengths, offsets, cache_keys, cache_values, w_qkv, w_out,
    w_gate_up, w_down, gains,
):
    w4 = w_qkv.transpose(0, 2, 1)

    vmem = pl.BlockSpec(memory_space=pltpu.VMEM)
    far = pl.BlockSpec(memory_space=pl.ANY)
    smem = pl.BlockSpec(memory_space=pltpu.SMEM)
    dma = pltpu.SemaphoreType.DMA

    def spread(peers, slots):
        return (
            dma((peers,)), dma((peers,)), dma((slots, NY)), dma((slots, NY)), dma((slots,)),
            dma((slots, NY)), dma((slots, NY)),
        )

    both = pl.pallas_call(
        kernel,
        out_shape=jax.ShapeDtypeStruct((2, OWN, D), BF16),
        in_specs=[vmem, far, far, far, far, far, far, vmem, vmem, smem, smem, smem],
        out_specs=vmem,
        scratch_shapes=[
            pltpu.VMEM((NZ, OWN, D), BF16),
            pltpu.VMEM((NDP, NX, 3, 64, 256), BF16),
            pltpu.VMEM((NDP, NZ, 64, 256), BF16),
            pltpu.VMEM((NDP, NX, 3, 256, 256), BF16),
            pltpu.VMEM((NX, CTX, PART), BF16),
            pltpu.VMEM((KEYS, PART), BF16),
            pltpu.VMEM((KEYS, PART), BF16),
            pltpu.VMEM((1, KEYS), jnp.int32),
            pltpu.VMEM((NX, NZ * OWN, 256), BF16),
            pltpu.VMEM((NX, NZ * OWN, 256), BF16),
            pltpu.VMEM((NX, GRP, HEAD_DIM), BF16),
            pltpu.VMEM((NZ, GRP + OWN, HEAD_DIM), BF16),
            pltpu.VMEM((NZ, NX, GRP, HEAD_DIM), BF16),
            pltpu.VMEM((NZ, GRP + OWN, HEAD_DIM), BF16),
            pltpu.VMEM((2, SEL, HEAD_DIM), F32),
            pltpu.VMEM((NX, OWN, HEAD_DIM), F32),
            pltpu.VMEM((HEADS, SEL, HEAD_DIM), BF16),
            pltpu.VMEM((NX, OWN, PART), BF16),
            pltpu.VMEM((NX, OWN, PART), BF16),
            pltpu.VMEM((NZ, HEADS * GRP + OWN, HEAD_DIM), BF16),
            pltpu.VMEM((NZ, HEADS * GRP + OWN, HEAD_DIM), BF16),
            pltpu.VMEM((NX, OWN, D), BF16),
            pltpu.VMEM((NX, OWN, D), BF16),
            pltpu.VMEM((OWN, D), BF16),
            pltpu.VMEM((NZ, OWN, D), BF16),
            pltpu.VMEM((NZ * OWN, NX * 256), BF16),
            pltpu.VMEM((2, NZ, OWN, D // 2), BF16),
            pltpu.VMEM((2, NZ, OWN, D // 2), BF16),
            pltpu.VMEM((SEL, HEAD_DIM), F32),
            pltpu.VMEM((SEL, HEAD_DIM), jnp.int32),
            pltpu.VMEM((SEL, HEAD_DIM), jnp.int32),
            pltpu.VMEM((SEL, HEAD_DIM), jnp.int32),
            pltpu.VMEM((SEL, HEAD_DIM), F32),
            pltpu.VMEM((SEL, HEAD_DIM), F32),
            pltpu.VMEM((16, HEAD_DIM), F32),
            pltpu.VMEM((16, HEAD_DIM), F32),
            pltpu.SMEM((16,), jnp.int32),
            pltpu.VMEM((SEL, KEYS), F32),
            pltpu.VMEM((2, NZ * OWN, HEAD_DIM), F32),
            dma((NZ,)), dma((NZ,)),
            spread(NX, NX),
            spread(NZ, 2),
            spread(NX, NX),
            dma((NX,)), dma((NX,)),
            dma((NX,)), dma((NX,)),
            dma((NX,)), dma((NX,)),
            dma((NX, NZ)), dma((NX, NZ)),
            dma((NZ,)), dma((NZ,)),
            dma((NX,)), dma((NX,)),
            dma((NX,)), dma((NX,)),
            dma((NZ,)), dma((NZ,)),
            dma((NX,)), dma((NX,)),
            dma((NZ,)), dma((NZ,)),
            dma((2, NZ)), dma((2, NZ)),
            dma((7,)),
        ],
        compiler_params=pltpu.CompilerParams(
            collective_id=0, has_side_effects=True, vmem_limit_bytes=56 << 20
        ),
    )(
        hidden_sel[0], cache_keys[0], cache_values[0], w4, w_out, w_gate_up, w_down, gains,
        picked, order, lengths, offsets,
    )
    return (both[:1], both[1:])


def solution(mesh):
    placed = (
        P("dp", "tensor", None),
        P("dp", None),
        P("dp", None),
        P("dp", None),
        P("dp", None),
        P("dp", "tensor", None),
        P("dp", "tensor", None),
        P(None, "dp", "tensor"),
        P("tensor", "dp"),
        P(None, "dp", "tensor"),
        P("tensor", "dp"),
        P(),
    )
    return jax.shard_map(
        layer,
        mesh=mesh,
        in_specs=placed,
        out_specs=(P("dp", "tensor", None), P("dp", "tensor", None)),
        check_vma=False,
    )
```

```python
import math

import jax
import jax.numpy as jnp
import numpy as np
from jax import lax
from jax.experimental import pallas as pl
from jax.experimental.pallas import tpu as pltpu
from jax.sharding import PartitionSpec as P

HEAD_DIM = 128
CH = 1024
NCH = 12
REQS = 3
NX = 4
NZ = 8
NDP = 8
NY = 4
D = 2048
PART = D // NX
HEADS = PART // HEAD_DIM
OWN = 16
GRP = NX * OWN
SEL = NZ * GRP
CTX = 384
CACHED = NX * CTX
KEYS = CACHED + 128
SPAN = 1 << 14
DEAD = 1 << 30

THETA = 500000.0
EPSILON = 1e-06
NEGATIVE = -1e30
FLOOR = -1e20
SCORE = HEAD_DIM ** (-0.5) * math.log2(math.e)
LAP_A = 6.28125
LAP_B = 0.0019340515136718750
LAP_C = 2.0 * math.pi - LAP_A - LAP_B
RATES = [
    float(np.float32(math.exp(-2.0 * j / HEAD_DIM * math.log(THETA)))) for j in range(HEAD_DIM // 2)
]
MESH = pl.DeviceIdType.MESH
F32, BF16 = jnp.float32, jnp.bfloat16
HIGH = lax.Precision.HIGHEST


def lanes(rows):
    return lax.broadcasted_iota(jnp.int32, (rows, HEAD_DIM), 1)


def kernel(
    hidden,
    keys,
    values,
    w4,
    wo,
    wgu,
    wd,
    gains,
    picked,
    order,
    lengths,
    offsets,
    both_out,
    hid,
    w4buf,
    wobuf,
    wbuf,
    kraw,
    kall,
    vall,
    kcode,
    psend,
    precv,
    qpk,
    kvs,
    qrecv,
    kvrecv,
    sq,
    stat,
    qh,
    kf,
    frecv,
    obuf,
    orecv,
    ysend,
    yrecv,
    hn,
    hbuf,
    act,
    dsend,
    drecv,
    natural,
    rows_of,
    codes,
    lows,
    qcos,
    qsin,
    scos,
    ssin,
    sbase,
    bias,
    squares,
    hz_s,
    hz_r,
    w4_sems,
    wo_sems,
    wm_sems,
    k_s,
    k_r,
    v_s,
    v_r,
    p_s,
    p_r,
    q_s,
    q_r,
    c_s,
    c_r,
    st_s,
    st_r,
    f_s,
    f_r,
    o_s,
    o_r,
    y_s,
    y_r,
    n_s,
    n_r,
    d_s,
    d_r,
    loc,
):
    tens = lax.axis_index("tensor")
    dp = lax.axis_index("dp")
    x = lax.div(tens, NZ)
    z = lax.rem(tens, NZ)
    core = lax.rem(dp, 2)
    sib = dp + 1 - 2 * core

    def xa(k):
        return lax.rem(x + k, NX)

    def za(k):
        return lax.rem(z + k, NZ)

    def da(k):
        return lax.rem(dp + k, NDP)

    def zdev(k):
        return {"tensor": x * NZ + za(k)}

    def xdev(k):
        return {"tensor": xa(k) * NZ + z}

    def send(src, dst, ssem, rsem, dev):
        return pltpu.make_async_remote_copy(
            src_ref=src, dst_ref=dst, send_sem=ssem, recv_sem=rsem, device_id=dev,
            device_id_type=MESH,
        )

    def each(first, last, body):
        def step(k, carry):
            body(k)
            return carry

        lax.fori_loop(first, last, step, 0)

    class Spread:
        def __init__(self, sems, slots, source, first, peers, entry, entry_in, at):
            (self.e_s, self.e_r, self.n_s, self.y_r, self.r_s, self.s_s, self.s_r) = sems
            self.slots, self.source, self.first, self.peers = slots, source, first, peers
            self.entry, self.entry_in, self.at = entry, entry_in, at

        def enter(self, k):
            return send(self.source, self.entry, self.e_s.at[k], self.e_r.at[k], self.first(k))

        def enter_in(self, k):
            at = self.entry_in(k)
            return send(at, at, self.e_s.at[k], self.e_r.at[k], self.first(k))

        def near(self, k, j):
            at = self.at(dp, k)
            return send(at, at, self.n_s.at[k, j], self.y_r.at[k, j], {"dp": da(2 * j)})

        def near_in(self, k, j):
            at = self.at(da(NDP - 2 * j), k)
            return send(at, at, self.n_s.at[k, j], self.y_r.at[k, j], {"dp": da(2 * j)})

        def way(self, k):
            return 1 + 2 * lax.div(k, self.slots // 2)

        def relay(self, k):
            j = self.way(k)
            at = self.at(da(NDP - 2 * j), k)
            return send(at, at, self.r_s.at[k], self.y_r.at[k, 2], {"dp": da(2 * j)})

        def relay_in(self, k):
            at = self.at(da(4), k)
            return send(at, at, self.r_s.at[k], self.y_r.at[k, 2], {"dp": da(2)})

        def side(self, k, j):
            at = self.at(da(NDP - 2 * j), k)
            return send(at, at, self.s_s.at[k, j], self.s_r.at[k, j], {"dp": sib})

        def side_in(self, k, j):
            at = self.at(lax.rem(sib + NDP - 2 * j, NDP), k)
            return send(at, at, self.s_s.at[k, j], self.s_r.at[k, j], {"dp": sib})

        def start(self):
            each(1, self.peers, lambda k: self.enter(k).start())

        def go_near(self, k):
            self.near(k, 1).start()
            self.near(k, 3).start()
            self.side(k, 0).start()

        def step_near(self, k):
            self.near_in(k, 1).wait_recv()
            self.near_in(k, 3).wait_recv()
            self.relay(k).start()
            self.side(k, 1).start()
            self.side(k, 3).start()

        def step_far(self, k):
            self.relay_in(k).wait_recv()
            self.side(k, 2).start()

        def arrive(self):
            each(0, self.slots, lambda k: each(0, NY, lambda j: self.side_in(k, j).wait_recv()))

        def finish(self):
            each(1, self.peers, lambda k: self.enter(k).wait_send())

            def one(k):
                self.near(k, 1).wait_send()
                self.near(k, 3).wait_send()
                self.relay(k).wait_send()
                each(0, NY, lambda j: self.side(k, j).wait_send())

            each(0, self.slots, one)

    def x_slot(buf):
        return lambda d, k: buf.at[d, xa(NX - k)]

    qkv_w = Spread(
        w4_sems, NX, w4, xdev, NX, w4buf.at[dp, x], lambda k: w4buf.at[dp, xa(NX - k)],
        x_slot(w4buf),
    )
    ffn_w = Spread(
        wm_sems, NX, wbuf.at[dp, x], xdev, NX, wbuf.at[dp, x], lambda k: wbuf.at[dp, xa(NX - k)],
        x_slot(wbuf),
    )
    out_w = Spread(
        wo_sems, 2, wo, zdev, NZ, wobuf.at[dp, z], lambda k: wobuf.at[dp, za(NZ - k)],
        lambda d, k: wobuf.at[d, pl.ds(4 * k, 4)],
    )

    def hz(k):
        return send(hidden, hid.at[z], hz_s.at[k], hz_r.at[k], zdev(k))

    def hz_in(k):
        at = hid.at[za(NZ - k)]
        return send(at, at, hz_s.at[k], hz_r.at[k], zdev(k))

    def columns(at):
        return pl.ds(pl.multiple_of(at * PART, PART), PART)

    def key_rows(at):
        return pl.ds(pl.multiple_of(at * CTX, 128), CTX)

    def kx(k):
        return send(keys.at[:, columns(xa(k))], kraw.at[x], k_s.at[k], k_r.at[k], xdev(k))

    def kx_in(k):
        at = kraw.at[xa(NX - k)]
        return send(at, at, k_s.at[k], k_r.at[k], xdev(k))

    def vx(k):
        return send(
            values.at[:, columns(xa(k))], vall.at[key_rows(x)], v_s.at[k], v_r.at[k], xdev(k)
        )

    def vx_in(k):
        at = vall.at[key_rows(xa(NX - k))]
        return send(at, at, v_s.at[k], v_r.at[k], xdev(k))

    def px(k):
        return send(psend.at[xa(k)], precv.at[x], p_s.at[k], p_r.at[k], xdev(k))

    def px_in(k):
        at = precv.at[xa(NX - k)]
        return send(at, at, p_s.at[k], p_r.at[k], xdev(k))

    def qz(j, k):
        p = xa(NX - j)
        return send(qpk.at[p], qrecv.at[z, p], q_s.at[j, k], q_r.at[j, k], zdev(k))

    def qz_in(j, k):
        at = qrecv.at[za(NZ - k), xa(NX - j)]
        return send(at, at, q_s.at[j, k], q_r.at[j, k], zdev(k))

    def cz(k):
        return send(kvs.at[za(k)], kvrecv.at[z], c_s.at[k], c_r.at[k], zdev(k))

    def cz_in(k):
        at = kvrecv.at[za(NZ - k)]
        return send(at, at, c_s.at[k], c_r.at[k], zdev(k))

    def stx(k):
        return send(stat.at[x], stat.at[x], st_s.at[k], st_r.at[k], xdev(k))

    def stx_in(k):
        at = stat.at[xa(NX - k)]
        return send(at, at, st_s.at[k], st_r.at[k], xdev(k))

    def fx(k):
        return send(kf.at[xa(k)], frecv.at[x], f_s.at[k], f_r.at[k], xdev(k))

    def fx_in(k):
        at = frecv.at[xa(NX - k)]
        return send(at, at, f_s.at[k], f_r.at[k], xdev(k))

    def oex(k):
        return send(obuf.at[za(k)], orecv.at[z], o_s.at[k], o_r.at[k], zdev(k))

    def oex_in(k):
        at = orecv.at[za(NZ - k)]
        return send(at, at, o_s.at[k], o_r.at[k], zdev(k))

    def yx(k):
        return send(ysend.at[xa(k)], yrecv.at[x], y_s.at[k], y_r.at[k], xdev(k))

    def yx_in(k):
        at = yrecv.at[xa(NX - k)]
        return send(at, at, y_s.at[k], y_r.at[k], xdev(k))

    def nz(k):
        return send(hn, hbuf.at[z], n_s.at[k], n_r.at[k], zdev(k))

    def nz_in(k):
        at = hbuf.at[za(NZ - k)]
        return send(at, at, n_s.at[k], n_r.at[k], zdev(k))

    def dz(half, k):
        return send(
            dsend.at[half, za(k)], drecv.at[half, z], d_s.at[half, k], d_r.at[half, k], zdev(k)
        )

    def dz_in(half, k):
        at = drecv.at[half, za(NZ - k)]
        return send(at, at, d_s.at[half, k], d_r.at[half, k], zdev(k))

    own_copies = [
        pltpu.make_async_copy(hidden, hid.at[z], loc.at[0]),
        pltpu.make_async_copy(w4, w4buf.at[dp, x], loc.at[1]),
        pltpu.make_async_copy(wo, wobuf.at[dp, z], loc.at[2]),
        pltpu.make_async_copy(wgu, wbuf.at[dp, x, pl.ds(0, 2)], loc.at[3]),
        pltpu.make_async_copy(keys.at[:, columns(x)], kraw.at[x], loc.at[4]),
        pltpu.make_async_copy(values.at[:, columns(x)], vall.at[key_rows(x)], loc.at[5]),
        pltpu.make_async_copy(wd, wbuf.at[dp, x, 2], loc.at[6]),
    ]
    for copy in own_copies:
        copy.start()

    barrier = pltpu.get_barrier_semaphore()

    def greet(dev):
        pl.semaphore_signal(barrier, inc=1, device_id=dev, device_id_type=MESH)

    each(1, NZ, lambda k: greet(zdev(k)))
    each(1, NX, lambda k: greet(xdev(k)))
    greet({"dp": da(2)})
    greet({"dp": da(6)})
    greet({"dp": sib})
    pl.semaphore_wait(barrier, NZ + NX + 1)

    qkv_w.start()
    own_copies[1].wait()
    qkv_w.go_near(0)
    each(1, NZ, lambda k: hz(k).start())
    own_copies[3].wait()
    own_copies[6].wait()
    ffn_w.enter(1).start()
    ffn_w.enter(3).start()
    each(1, NX, lambda k: kx(k).start())
    out_w.start()

    end_a = lengths[0, 0]
    end_b = end_a + lengths[0, 1]
    span = lax.broadcasted_iota(jnp.int32, (16, HEAD_DIM), 0)
    turns = jnp.zeros((16, HEAD_DIM), jnp.int32)
    shifts, bottoms = [], []
    for slot in range(NCH):
        place = order[0, slot]
        second, third = place >= end_a, place >= end_b
        start = jnp.where(third, end_b, jnp.where(second, end_a, 0))
        moved = jnp.where(third, offsets[0, 2], jnp.where(second, offsets[0, 1], offsets[0, 0]))
        bottom = jnp.where(third, 2 * SPAN, jnp.where(second, SPAN, 0))
        base = moved + (place - start) * CH
        sbase[slot] = base + bottom - slot * CH
        shifts.append(base + bottom - slot * CH)
        bottoms.append(bottom)
        turns = jnp.where(span == slot, base, turns)

    turn_lane = lax.rem(lanes(8), HEAD_DIM // 2)
    rates = jnp.zeros((8, HEAD_DIM), F32)
    for j in range(HEAD_DIM // 2):
        rates = jnp.where(turn_lane == j, RATES[j], rates)

    def circle(position):
        angle = position.astype(F32) * rates[0:1, :]
        laps = jnp.floor(angle * (0.5 / math.pi) + 0.5)
        angle = ((angle - laps * LAP_A) - laps * LAP_B) - laps * LAP_C
        sine = jnp.sin(angle)
        left = lax.broadcasted_iota(jnp.int32, position.shape, 1) < HEAD_DIM // 2
        return jnp.cos(angle), jnp.where(left, -sine, sine)

    scos[...], ssin[...] = circle(turns)

    natural[...] = lax.dot_general(
        jnp.broadcast_to(picked[...].astype(F32), (8, SEL)),
        jnp.full((8, HEAD_DIM), 0.125, F32), (((0,), (0,)), ((), ())),
        precision=HIGH, preferred_element_type=F32,
    )
    for zz in range(NZ):
        for xx in range(NX):
            at = (zz * NX + xx) * OWN
            back = (xx * NZ + zz) * OWN
            rows_of[at : at + OWN] = natural[back : back + OWN].astype(jnp.int32)

    def tokens(i):
        rows = pl.ds(pl.multiple_of(i * 128, 128), 128)
        row = rows_of[rows]
        slot_of = lax.shift_right_logical(row, 10)
        shift = jnp.zeros_like(row)
        bottom = jnp.zeros_like(row)
        for slot in range(NCH):
            mine = slot_of == slot
            shift = jnp.where(mine, shifts[slot], shift)
            bottom = jnp.where(mine, bottoms[slot], bottom)
        codes[rows] = row + shift
        lows[rows] = bottom
        qcos[rows], qsin[rows] = circle(row + shift - bottom)

    each(0, SEL // 128, tokens)

    def qkv_on(k):
        qkv_w.enter_in(k).wait_recv()
        qkv_w.go_near(k)

    each(1, NX, qkv_on)

    each(0, NX, qkv_w.step_near)
    own_copies[2].wait()
    each(1, NZ, lambda k: out_w.enter_in(k).wait_recv())
    each(0, NX, qkv_w.step_far)
    each(0, 2, out_w.go_near)
    ffn_w.go_near(0)

    own_copies[0].wait()
    each(1, NZ, lambda k: hz_in(k).wait_recv())
    qkv_w.arrive()

    low_x = lanes(NZ * OWN) < HEAD_DIM // 2

    def project(k):
        at = xa(k)
        rows = hid[...].reshape(NZ * OWN, D)
        kv = jnp.zeros((NZ * OWN, HEAD_DIM), F32)
        qk = jnp.zeros((NZ * OWN, HEAD_DIM), F32)
        for c in range(NDP):
            left = rows[:, c * 256 : (c + 1) * 256]
            across = (((1,), (1,)), ((), ()))
            kv += lax.dot_general(
                left, w4buf[c, at, 1:].reshape(HEAD_DIM, 256), across, preferred_element_type=F32
            )
            qk += lax.dot_general(
                left, w4buf[c, at, :2].reshape(HEAD_DIM, 256), across, preferred_element_type=F32
            )
        psend[at, :, :HEAD_DIM] = kv.astype(BF16)
        psend[at, :, HEAD_DIM:] = jnp.where(low_x, qk, pltpu.roll(qk, 64, 1)).astype(BF16)
        squares[0] += jnp.where(low_x, qk * qk, 0.0)
        squares[1] += jnp.where(low_x, kv * kv, 0.0)

    low_f = lanes(GRP) < HEAD_DIM // 2

    def take(j, blocks):
        p = xa(NX - j)
        rows = blocks[p]
        q = rows[:, HEAD_DIM:].astype(F32)
        qpk[p] = jnp.where(low_f, q[:GRP], q[GRP:]).astype(BF16)
        at = pl.ds(pl.multiple_of(p * OWN, OWN), OWN)
        kvs[:, at] = rows[:, :HEAD_DIM].reshape(NZ, OWN, HEAD_DIM)
        each(1, NZ, lambda k: qz(j, k).start())

    def project_send(k):
        project(k)
        px(k).start()

    squares[...] = jnp.zeros_like(squares)
    project(0)
    take(0, psend)
    each(1, NX, project_send)
    lane_own = lanes(OWN)
    mine = jnp.zeros((OWN, HEAD_DIM), F32)
    for kind in range(2):
        sums = jnp.sum(squares[kind], axis=1, keepdims=True)
        for g in range(NZ):
            mine = jnp.where(lane_own == 4 * g + 2 * kind, sums[g * OWN : (g + 1) * OWN], mine)
    stat[pl.ds(x, 1)] = mine[None]
    each(1, NX, lambda k: stx(k).start())
    each(1, NX, lambda k: vx(k).start())
    ffn_w.enter(2).start()
    for k in (1, 3):
        ffn_w.enter_in(k).wait_recv()
        ffn_w.go_near(k)

    def taken(j):
        px_in(j).wait_recv()
        take(j, precv)

    each(1, NX, taken)
    each(1, NX, lambda k: stx_in(k).wait_recv())
    both = stat[0]
    for p in range(1, NX):
        both += pltpu.roll(stat[p], 32 * p, 1)
    high = both.astype(BF16).astype(F32)
    kvs[:, GRP:] = jnp.broadcast_to(
        (high + pltpu.roll(both - high, 1, 1)).astype(BF16)[None], (NZ, OWN, HEAD_DIM)
    )
    each(1, NZ, lambda k: cz(k).start())
    qrecv[pl.ds(z, 1)] = qpk[...][None]
    kvrecv[pl.ds(z, 1)] = kvs[pl.ds(z, 1)]
    each(0, 2, out_w.step_near)

    grp_rows = pl.ds(pl.multiple_of(z * GRP, GRP), GRP)
    for block in range(NX):
        first = (block * NZ + z) * CTX
        slot = lax.div(first, CH)
        later = lax.min(slot + 1, NCH - 1)
        row = first + lax.broadcasted_iota(jnp.int32, (1, CTX), 1)
        code = jnp.where(row < (slot + 1) * CH, sbase[slot], sbase[later]) + row
        hit = jnp.max(
            jnp.where(rows_of[:, 0:1] == row, 1, 0), axis=0, keepdims=True
        )
        kcode[:, block * CTX : (block + 1) * CTX] = jnp.where(hit > 0, DEAD, code)
    corner = lax.broadcasted_iota(jnp.int32, (GRP, HEAD_DIM), 0) == lanes(GRP)
    kcode[:, CACHED:KEYS] = jnp.where(
        lanes(1) < GRP,
        jnp.sum(jnp.where(corner, codes[grp_rows], 0), axis=0, keepdims=True),
        DEAD,
    )
    kall[CACHED:KEYS, :] = jnp.zeros((KEYS - CACHED, PART), BF16)
    vall[CACHED:KEYS, :] = jnp.zeros((KEYS - CACHED, PART), BF16)

    own_copies[4].wait()
    each(1, NX, lambda k: kx_in(k).wait_recv())

    def turn(block):
        first = (block * NZ + z) * CTX
        slot = lax.div(first, CH)
        later = lax.min(slot + 1, NCH - 1)
        row = first + lax.broadcasted_iota(jnp.int32, (CTX, HEAD_DIM), 0)
        here = row < (slot + 1) * CH
        cosine = jnp.where(here, scos[pl.ds(slot, 1), :], scos[pl.ds(later, 1), :])
        sine = jnp.where(here, ssin[pl.ds(slot, 1), :], ssin[pl.ds(later, 1), :])
        for h in range(HEADS):
            cols = slice(h * HEAD_DIM, (h + 1) * HEAD_DIM)
            v = kraw[block, :, cols].astype(F32)
            kall[key_rows(block), cols] = (v * cosine + pltpu.roll(v, 64, 1) * sine).astype(BF16)

    each(0, NX, turn)
    def mask(i):
        rows = pl.ds(pl.multiple_of(i * 128, 128), 128)
        code = kcode[...]
        usable = (code <= codes[rows, 0:1]) & (code >= lows[rows, 0:1])
        bias[rows] = jnp.where(usable, 0.0, NEGATIVE)

    each(0, SEL // 128, mask)

    each(0, NX, lambda j: each(1, NZ, lambda k: qz_in(j, k).wait_recv()))
    each(1, NZ, lambda k: cz_in(k).wait_recv())
    low = lanes(SEL // 2) < HEAD_DIM // 2

    def in_order(t):
        return jnp.concatenate(
            [
                t[p * GRP + g * OWN : p * GRP + (g + 1) * OWN]
                for g in range(NZ // 2)
                for p in range(NX)
            ],
            axis=0,
        )

    def q_head(h):
        a = qrecv[2 * h].reshape(SEL // 2, HEAD_DIM).astype(F32)
        b = qrecv[2 * h + 1].reshape(SEL // 2, HEAD_DIM).astype(F32)
        top = jnp.where(low, a, pltpu.roll(b, 64, 1))
        bottom = jnp.where(low, pltpu.roll(a, 64, 1), b)
        return in_order(top), in_order(bottom)

    def f_head(h):
        a = kvrecv[2 * h, :GRP].astype(F32)
        b = kvrecv[2 * h + 1, :GRP].astype(F32)
        return jnp.where(low_f, a, pltpu.roll(b, 64, 1)), jnp.where(low_f, pltpu.roll(a, 64, 1), b)

    each(0, 2, out_w.step_far)
    total = jnp.zeros((OWN, HEAD_DIM), F32)
    for p in range(NZ):
        total += kvrecv[p, GRP:].astype(F32)
    total = total + pltpu.roll(total, HEAD_DIM - 1, 1)
    even = lax.rem(lane_own, 2) == 0
    factor = lax.rsqrt(jnp.where(even, total, 1.0) * (1.0 / D) + EPSILON)
    for g in range(NZ):
        for p in range(NX):
            at = (g * NX + p) * OWN
            col = 32 * p + 4 * g
            sq[0, at : at + OWN] = jnp.broadcast_to(
                factor[:, col : col + 1] * SCORE, (OWN, HEAD_DIM)
            )
            sq[1, at : at + OWN] = jnp.broadcast_to(factor[:, col + 2 : col + 3], (OWN, HEAD_DIM))
    for h in range(HEADS):
        cols = pl.ds(pl.multiple_of(x * PART + h * HEAD_DIM, HEAD_DIM), HEAD_DIM)
        top, bottom = q_head(h)
        gain = gains[0:1, cols]
        for part, rows in ((top, slice(0, SEL // 2)), (bottom, slice(SEL // 2, SEL))):
            v = part * sq[0, rows] * gain
            qh[h, rows] = (v * qcos[rows] + pltpu.roll(v, 64, 1) * qsin[rows]).astype(BF16)
        key, value = f_head(h)
        vall[CACHED : CACHED + GRP, h * HEAD_DIM : (h + 1) * HEAD_DIM] = value.astype(BF16)
        v = key * sq[1, grp_rows] * gains[1:2, cols]
        v = (v * qcos[grp_rows] + pltpu.roll(v, 64, 1) * qsin[grp_rows]).astype(BF16)
        kall[CACHED : CACHED + GRP, h * HEAD_DIM : (h + 1) * HEAD_DIM] = v
        kf[:, :, h * HEAD_DIM : (h + 1) * HEAD_DIM] = v.reshape(NX, OWN, HEAD_DIM)
    each(1, NX, lambda k: fx(k).start())
    frecv[pl.ds(x, 1)] = kf[pl.ds(x, 1)]

    own_copies[5].wait()
    each(1, NX, lambda k: vx_in(k).wait_recv())

    lane = lanes(128)

    def attend(part):
        rows = pl.ds(pl.multiple_of(part * 128, 128), 128)
        two = pl.ds(part * 2, 2)
        marks = jnp.zeros((128, HEAD_DIM), F32)
        for h in range(HEADS):
            cols = slice(h * HEAD_DIM, (h + 1) * HEAD_DIM)
            scores = lax.dot_general(
                qh[h, rows], kall[:, cols], (((1,), (1,)), ((), ())), preferred_element_type=F32
            ) + bias[rows]
            most = jnp.maximum(jnp.max(scores, axis=1, keepdims=True), FLOOR)
            most = most.astype(BF16).astype(F32)
            weight = jnp.exp2(scores - most)
            mass = jnp.sum(weight, axis=1, keepdims=True)
            mixed = jnp.dot(weight.astype(BF16), vall[:, cols], preferred_element_type=F32)
            obuf[two, h * GRP : (h + 1) * GRP, :] = mixed.astype(BF16).reshape(2, GRP, HEAD_DIM)
            high = mass.astype(BF16).astype(F32)
            marks = jnp.where(lane == h, most, marks)
            marks = jnp.where(lane == h + HEADS, high, marks)
            marks = jnp.where(lane == h + 2 * HEADS, mass - high, marks)
        for side in range(2):
            packed = marks[side * GRP : side * GRP + OWN]
            for g in range(1, NX):
                at = side * GRP + g * OWN
                packed += pltpu.roll(marks[at : at + OWN], 32 * g, 1)
            obuf[part * 2 + side, HEADS * GRP :, :] = packed.astype(BF16)

    def attend_far(i):
        part = lax.rem(lax.div(z, 2) + 1 + lax.rem(i + 1, 3), NZ // 2)
        attend(part)
        offset = lax.rem(2 * part + NZ - z, NZ)
        oex(offset).start()
        oex(lax.rem(offset + 1, NZ)).start()

        @pl.when(i > 0)
        def _():
            ffn_w.step_near(2 * i - 1)

    ffn_w.step_near(0)
    each(0, 3, attend_far)
    attend(lax.div(z, 2))
    beside = lax.rem(NZ + 1 - 2 * lax.rem(z, 2), NZ)
    oex(beside).start()
    orecv[pl.ds(z, 1)] = obuf[pl.ds(z, 1)]
    ffn_w.enter_in(2).wait_recv()
    ffn_w.go_near(2)
    out_w.arrive()
    each(1, NZ, lambda k: oex_in(k).wait_recv())

    def marks_of(p):
        return orecv[p, HEADS * GRP :, :].astype(F32)

    peak = marks_of(0)
    for p in range(1, NZ):
        peak = jnp.maximum(peak, marks_of(p))
    mass = jnp.zeros((OWN, HEAD_DIM), F32)
    for p in range(NZ):
        marks = marks_of(p)
        amount = pltpu.roll(marks, HEAD_DIM - HEADS, 1) + pltpu.roll(
            marks, HEAD_DIM - 2 * HEADS, 1
        )
        mass += jnp.exp2(marks - peak) * amount
    valid = lax.rem(lane_own, 32) < HEADS
    inverse = 1.0 / jnp.where(valid, mass, 1.0)
    heads = [jnp.zeros((GRP, HEAD_DIM), F32) for _ in range(HEADS)]
    for p in range(NZ):
        share = jnp.exp2(marks_of(p) - peak) * inverse
        for h in range(HEADS):
            part = orecv[p, h * GRP : (h + 1) * GRP, :].astype(F32)
            weight = jnp.concatenate(
                [
                    jnp.broadcast_to(
                        share[:, 32 * g + h : 32 * g + h + 1], (OWN, HEAD_DIM)
                    )
                    for g in range(NX)
                ],
                axis=0,
            )
            heads[h] += part * weight
    attn = jnp.concatenate(heads, axis=1).astype(BF16)

    def out_block(c):
        got = jnp.dot(attn, wobuf[c].reshape(PART, 256), preferred_element_type=F32)
        cols = pl.ds(pl.multiple_of(c * 256, 256), 256)
        ysend[:, :, cols] = got.astype(BF16).reshape(NX, OWN, 256)

    each(0, NDP, out_block)
    each(1, NX, lambda k: yx(k).start())
    yrecv[pl.ds(x, 1)] = ysend[pl.ds(x, 1)]
    for k in (0, 1, 3):
        ffn_w.step_far(k)
    each(1, NX, lambda k: yx_in(k).wait_recv())
    y = yrecv[0].astype(F32)
    for p in range(1, NX):
        y += yrecv[p].astype(F32)
    y = y * lax.rsqrt(jnp.mean(y * y, axis=1, keepdims=True) + EPSILON) * gains[2:3, :]
    following = (hid[z].astype(F32) + y).astype(BF16)
    hn[...] = following
    each(1, NZ, lambda k: nz(k).start())
    hbuf[pl.ds(z, 1)] = following[None]
    ffn_w.step_near(2)
    ffn_w.step_far(2)

    each(1, NZ, lambda k: nz_in(k).wait_recv())
    ffn_w.arrive()

    def gate(c):
        rows = hbuf[...].reshape(NZ * OWN, D)
        g = jnp.dot(rows, wbuf[:, c, 0].reshape(D, 256), preferred_element_type=F32)
        u = jnp.dot(rows, wbuf[:, c, 1].reshape(D, 256), preferred_element_type=F32)
        cols = pl.ds(pl.multiple_of(c * 256, 256), 256)
        act[:, cols] = (jax.nn.silu(g) * u).astype(BF16)

    each(0, NX, gate)

    def down_half(half):
        def down(c):
            weights = wbuf[half * 4 + c, :, 2].reshape(NX * 256, 256)
            got = jnp.dot(act[...], weights, preferred_element_type=F32)
            cols = pl.ds(pl.multiple_of(c * 256, 256), 256)
            dsend[half, :, :, cols] = got.astype(BF16).reshape(NZ, OWN, 256)

        each(0, 4, down)
        each(1, NZ, lambda k: dz(half, k).start())

    each(0, 2, down_half)
    for half in range(2):
        drecv[half, pl.ds(z, 1)] = dsend[half, pl.ds(z, 1)]

    each(1, NX, lambda k: fx_in(k).wait_recv())
    for p in range(NX):
        both_out[1, :, p * PART : (p + 1) * PART] = frecv[p]

    each(0, NX, lambda j: each(1, NZ, lambda k: qz(j, k).wait_send()))
    for copy in (hz, cz, oex, nz):
        each(1, NZ, lambda k, copy=copy: copy(k).wait_send())
    for copy in (kx, vx, px, stx, fx, yx):
        each(1, NX, lambda k, copy=copy: copy(k).wait_send())
    for weights in (qkv_w, out_w, ffn_w):
        weights.finish()

    each(0, 2, lambda half: each(1, NZ, lambda k: dz_in(half, k).wait_recv()))
    halves = []
    for half in range(2):
        t = drecv[half, 0].astype(F32)
        for p in range(1, NZ):
            t += drecv[half, p].astype(F32)
        halves.append(t)
    t = jnp.concatenate(halves, axis=1)
    t = t * lax.rsqrt(jnp.mean(t * t, axis=1, keepdims=True) + EPSILON) * gains[3:4, :]
    both_out[0] = (hn[...].astype(F32) + t).astype(BF16)
    each(0, 2, lambda half: each(1, NZ, lambda k: dz(half, k).wait_send()))


def layer(
    hidden_sel, picked, order, lengths, offsets, cache_keys, cache_values, w_qkv, w_out,
    w_gate_up, w_down, gains,
):
    w4 = w_qkv.transpose(0, 2, 1)

    vmem = pl.BlockSpec(memory_space=pltpu.VMEM)
    far = pl.BlockSpec(memory_space=pl.ANY)
    smem = pl.BlockSpec(memory_space=pltpu.SMEM)
    dma = pltpu.SemaphoreType.DMA

    def spread(peers, slots):
        return (
            dma((peers,)), dma((peers,)), dma((slots, NY)), dma((slots, NY)), dma((slots,)),
            dma((slots, NY)), dma((slots, NY)),
        )

    both = pl.pallas_call(
        kernel,
        out_shape=jax.ShapeDtypeStruct((2, OWN, D), BF16),
        in_specs=[vmem, far, far, far, far, far, far, vmem, vmem, smem, smem, smem],
        out_specs=vmem,
        scratch_shapes=[
            pltpu.VMEM((NZ, OWN, D), BF16),
            pltpu.VMEM((NDP, NX, 3, 64, 256), BF16),
            pltpu.VMEM((NDP, NZ, 64, 256), BF16),
            pltpu.VMEM((NDP, NX, 3, 256, 256), BF16),
            pltpu.VMEM((NX, CTX, PART), BF16),
            pltpu.VMEM((KEYS, PART), BF16),
            pltpu.VMEM((KEYS, PART), BF16),
            pltpu.VMEM((1, KEYS), jnp.int32),
            pltpu.VMEM((NX, NZ * OWN, 256), BF16),
            pltpu.VMEM((NX, NZ * OWN, 256), BF16),
            pltpu.VMEM((NX, GRP, HEAD_DIM), BF16),
            pltpu.VMEM((NZ, GRP + OWN, HEAD_DIM), BF16),
            pltpu.VMEM((NZ, NX, GRP, HEAD_DIM), BF16),
            pltpu.VMEM((NZ, GRP + OWN, HEAD_DIM), BF16),
            pltpu.VMEM((2, SEL, HEAD_DIM), F32),
            pltpu.VMEM((NX, OWN, HEAD_DIM), F32),
            pltpu.VMEM((HEADS, SEL, HEAD_DIM), BF16),
            pltpu.VMEM((NX, OWN, PART), BF16),
            pltpu.VMEM((NX, OWN, PART), BF16),
            pltpu.VMEM((NZ, HEADS * GRP + OWN, HEAD_DIM), BF16),
            pltpu.VMEM((NZ, HEADS * GRP + OWN, HEAD_DIM), BF16),
            pltpu.VMEM((NX, OWN, D), BF16),
            pltpu.VMEM((NX, OWN, D), BF16),
            pltpu.VMEM((OWN, D), BF16),
            pltpu.VMEM((NZ, OWN, D), BF16),
            pltpu.VMEM((NZ * OWN, NX * 256), BF16),
            pltpu.VMEM((2, NZ, OWN, D // 2), BF16),
            pltpu.VMEM((2, NZ, OWN, D // 2), BF16),
            pltpu.VMEM((SEL, HEAD_DIM), F32),
            pltpu.VMEM((SEL, HEAD_DIM), jnp.int32),
            pltpu.VMEM((SEL, HEAD_DIM), jnp.int32),
            pltpu.VMEM((SEL, HEAD_DIM), jnp.int32),
            pltpu.VMEM((SEL, HEAD_DIM), F32),
            pltpu.VMEM((SEL, HEAD_DIM), F32),
            pltpu.VMEM((16, HEAD_DIM), F32),
            pltpu.VMEM((16, HEAD_DIM), F32),
            pltpu.SMEM((16,), jnp.int32),
            pltpu.VMEM((SEL, KEYS), F32),
            pltpu.VMEM((2, NZ * OWN, HEAD_DIM), F32),
            dma((NZ,)), dma((NZ,)),
            spread(NX, NX),
            spread(NZ, 2),
            spread(NX, NX),
            dma((NX,)), dma((NX,)),
            dma((NX,)), dma((NX,)),
            dma((NX,)), dma((NX,)),
            dma((NX, NZ)), dma((NX, NZ)),
            dma((NZ,)), dma((NZ,)),
            dma((NX,)), dma((NX,)),
            dma((NX,)), dma((NX,)),
            dma((NZ,)), dma((NZ,)),
            dma((NX,)), dma((NX,)),
            dma((NZ,)), dma((NZ,)),
            dma((2, NZ)), dma((2, NZ)),
            dma((7,)),
        ],
        compiler_params=pltpu.CompilerParams(
            collective_id=0, has_side_effects=True, vmem_limit_bytes=56 << 20
        ),
    )(
        hidden_sel[0], cache_keys[0], cache_values[0], w4, w_out, w_gate_up, w_down, gains,
        picked, order, lengths, offsets,
    )
    return (both[:1], both[1:])


def solution(mesh):
    placed = (
        P("dp", "tensor", None),
        P("dp", None),
        P("dp", None),
        P("dp", None),
        P("dp", None),
        P("dp", "tensor", None),
        P("dp", "tensor", None),
        P(None, "dp", "tensor"),
        P("tensor", "dp"),
        P(None, "dp", "tensor"),
        P("tensor", "dp"),
        P(),
    )
    return jax.shard_map(
        layer,
        mesh=mesh,
        in_specs=placed,
        out_specs=(P("dp", "tensor", None), P("dp", "tensor", None)),
        check_vma=False,
    )
```
